32 devices in a mesh: dp: 4 (over z), expert: 8 (over y, x, core).
Axes of the slice: x: 2, y: 2, z: 4, core: 2. Of those that a mesh axis runs over, the one named last changes fastest.
Arguments:
- tokens: bfloat16 [8, 512, 2048], P('expert', 'dp'), may hold values from -12 to 12
- routes: int32 [8, 512, 2], P('expert', 'dp'), may hold values from 0 to 7, all different within a row; in each aligned block of 128 rows (0 to 127, 128 to 255, ..., all dimensions but the last counted through in order) at most 40 rows name the same one
- gate_code: int32 [8, 512, 2], P('expert', 'dp'), may hold values from 0 to 15
- gate_table: float32 [16], replicated, may hold values from 0.1 to 1
- w_gate: bfloat16 [8, 2048, 704], P('expert'), may hold values from -0.125 to 0.125
- w_up: bfloat16 [8, 2048, 704], P('expert'), may hold values from -0.125 to 0.125
- w_down: bfloat16 [8, 704, 2048], P('expert'), may hold values from -0.7 to 0.7
- norm_gain: float32 [2048], replicated, may hold values from 0.25 to 1.75
Outputs:
- relaid_out: bfloat16 [8, 512, 2048], P('expert', None, 'dp')
The draws below stay inside these ranges and needn't reach their ends.
Inputs may be any that keep to these rules, and one draw needn't show every extreme that they name: Within the 128 tokens of one device (aligned blocks of positions) no expert is named by more than 40 routes, a bound that some block reaches; a token's two experts differ.
All inputs are finite; a program needn't handle non-finite values.
Results may differ from the reference program's by a relative error of at most 0.0064.
Values may be sent and summed in bfloat16 or wider, within the bound.
No kernel may reach another device: no remote copies, remote signals or barrier semaphores. Data moves between devices by JAX's collectives and lax.ppermute only.
A program may use at most 64 MiB of HBM per device.

```python
import math
import jax
import jax.numpy as jnp
import numpy as np
from jax import lax

D = 2048
FF = 704
LEVELS = 16
TOK_DEV = 128
EXPERTS = 8
CAP = 40
LENGTH = 512
SEQS = 8
N_DP = 4


def draw_tokens(key, part):
    key_main, key_rows = jax.random.split(key, 2)
    row_scale = 10.0 ** jax.random.uniform(key_rows, (SEQS, LENGTH, 1), jnp.float32, -0.5, 0.5)
    noise_main = jax.random.normal(key_main, (SEQS, LENGTH, D), jnp.float32)
    return jnp.clip(noise_main * row_scale, -12.0, 12.0).astype(jnp.bfloat16)


def draw_w_down(key, part):
    column_scale = 10.0 ** (jnp.arange(D, dtype=jnp.float32) / D - 0.5)
    noise_main = jax.random.normal(key, (EXPERTS, FF, D), jnp.float32)
    values = noise_main * FF ** (-0.5) * column_scale[None, None, :]
    return jnp.clip(values, -0.7, 0.7).astype(jnp.bfloat16)


def touch_ends(values, key, low, top_value):
    longest = values.shape.index(max(values.shape))
    spots = []
    for shift in (0, 1):
        where = [jax.random.randint(jax.random.fold_in(key, axis), (), 0, length) for axis, length in enumerate(values.shape)]
        where[longest] = (where[longest] + shift) % values.shape[longest]
        spots.append(tuple(where))
    return values.at[spots[0]].set(low).at[spots[1]].set(top_value)


def level_of(stream_key, shape, pieces, least, largest):
    factor_of, own = 1.0, jax.random.fold_in(stream_key, 6)
    for axis_at, parts in pieces:
        heights = jnp.exp(jax.random.uniform(jax.random.fold_in(own, axis_at), (parts,), jnp.float32, least / len(pieces), largest / len(pieces)))
        factor_of = factor_of * jnp.repeat(heights, shape[axis_at] // parts).reshape([-1 if axis == axis_at else 1 for axis in range(len(shape))])
    return factor_of


def deal_out(stream_key, own, number, rows, amount, top, bound, lean):
    order = jax.random.permutation(stream_key, amount)
    crowded, usual = shares(amount, rows * top, bound, lean, True), shares(amount, rows * top, bound, lean, False)
    places = jnp.arange(amount)

    def named(lengths, offset_by):
        used = int((lengths > 0).sum())
        fixed = max(1, used // 4)
        moved = fixed + (places - fixed + offset_by * (used - fixed)) % max(1, amount - fixed)
        return jnp.zeros((amount,), jnp.int32).at[order[jnp.where(places < fixed, places, moved)]].set(jnp.asarray(lengths, jnp.int32))

    lengths = jnp.where(number % 4 == 0, named(crowded, number // 4), named(usual, number - number // 4 - 1))
    mixed = jax.random.permutation(jax.random.fold_in(own, 3), amount)
    giver, receiver = mixed[0:amount // 2 * 2:2], mixed[1:amount // 2 * 2:2]
    room = jnp.minimum(lengths[giver] - 1, bound - lengths[receiver]) // 2
    room = jnp.where((giver == order[0]) | (receiver == order[0]) | (lengths[receiver] == 0), 0, jnp.maximum(room, 0))
    moved = jax.random.randint(jax.random.fold_in(own, 4), (amount // 2,), 0, 1 << 20) % (room + 1)
    lengths = lengths.at[giver].add(-moved).at[receiver].add(moved)
    labels = jnp.searchsorted(jnp.cumsum(lengths), jnp.arange(rows * top), side="right").astype(jnp.int32)
    table = labels.reshape(top, rows).T
    table = table[jax.random.permutation(jax.random.fold_in(own, 1), rows)]
    offset_by = jax.random.randint(jax.random.fold_in(own, 2), (rows, 1), 0, top)
    return jnp.take_along_axis(table, (jnp.arange(top)[None, :] + offset_by) % top, axis=1)


def shares(amount, total, bound, skew, full):
    loads = [(1 << 20) // math.isqrt(standing ** skew) + 1 for standing in range(1, amount + 1)]
    largest = bound if full else min(bound, max(-(-total // amount), total * loads[0] // sum(loads)))
    least = 1 if total - largest >= amount - 1 else 0
    given, rest = [largest] + [least] * (amount - 1), total - largest - least * (amount - 1)
    while rest > 0:
        candidates = [i for i in range(1, amount) if given[i] < largest] or [i for i in range(1, amount) if given[i] < bound]
        pool, budget = sum([loads[i] for i in candidates]), rest
        for i in candidates:
            extra = min(bound - given[i], max(1, budget * loads[i] // pool), rest)
            given[i] = given[i] + extra
            rest = rest - extra
    return np.array(given)


def scatter_about(own_key, dims, spread, limit, cuts=(), held_as=jnp.bfloat16):
    factor_of = level_of(own_key, dims, cuts, -0.22, 0.18) if cuts else 1.0
    entries = jax.random.normal(own_key, dims, jnp.float32) * spread * factor_of
    return jnp.minimum(jnp.maximum(entries, -limit), limit).astype(held_as)


def setup_inputs(seed: int = 0) -> dict:
    keys = jax.random.split(jax.random.key(seed), 9)
    tokens = draw_tokens(jax.random.fold_in(keys[8], 71), 0)
    routes_keys = jax.random.split(jax.random.fold_in(keys[1], 1), SEQS * LENGTH // TOK_DEV)
    routes_turns = jax.random.permutation(jax.random.fold_in(keys[1], 3), SEQS * LENGTH // TOK_DEV)
    routes = jax.vmap(lambda own, number: deal_out(jax.random.fold_in(keys[1], 2), own, number, TOK_DEV, EXPERTS, 2, CAP, 2))(routes_keys, routes_turns).reshape((SEQS, LENGTH, 2))
    gate_code = touch_ends(jax.random.randint(keys[2], (SEQS, LENGTH, 2), 0, LEVELS), jax.random.fold_in(keys[2], 1), 0, LEVELS - 1).astype(jnp.int32)
    gate_table = jnp.clip(jnp.exp(jax.random.uniform(keys[3], (LEVELS,), jnp.float32, math.log(0.1), math.log(1.0))), 0.1, 1.0)
    w_gate = scatter_about(keys[4], (EXPERTS, D, FF), D ** -0.5, 0.125, ((0, 8),))
    w_up = scatter_about(keys[5], (EXPERTS, D, FF), D ** -0.5, 0.125, ((0, 8),))
    w_down = draw_w_down(jax.random.fold_in(keys[8], 71), 0)
    norm_gain = jnp.clip(1.0 + 0.15 * jax.random.normal(keys[7], (D,), jnp.float32), 0.25, 1.75)
    return dict(tokens=tokens, routes=routes, gate_code=gate_code, gate_table=gate_table, w_gate=w_gate, w_up=w_up, w_down=w_down, norm_gain=norm_gain)


epsilon = 1e-06

def reference(tokens, routes, gate_code, gate_table, w_gate, w_up, w_down, norm_gain):
    blocks = SEQS * N_DP
    flat_tok = tokens.reshape(-1, D)
    block_routes = routes.reshape(blocks, 2 * TOK_DEV)
    onehot = (block_routes[:, :, None] == jnp.arange(EXPERTS, dtype=jnp.int32)[None, None, :]).astype(jnp.int32)
    slot_pos = lax.optimization_barrier(jnp.sum((jnp.cumsum(onehot, axis=1) - onehot) * onehot, axis=2))
    block_base = (jnp.arange(blocks, dtype=jnp.int32) * CAP)[:, None]
    position = (block_base + slot_pos).reshape(-1, 2).astype(jnp.int32)
    expert_ids = routes.reshape(-1, 2)
    levels = gate_table.shape[0]
    level_match = gate_code.reshape(-1, 2)[:, :, None] == jnp.arange(levels, dtype=jnp.int32)[None, None, :]
    weights = lax.optimization_barrier(jnp.sum(jnp.where(level_match, gate_table[None, None, :], 0.0), axis=2))
    rows_total = blocks * CAP

    def one_expert(summed, inputs):
        expert_index, gate_w, up_w, down_w = inputs
        buffer = jnp.zeros((rows_total, D), jnp.bfloat16)
        for column in range(2):
            chosen = expert_ids[:, column] == expert_index
            target = jnp.where(chosen, position[:, column], rows_total)
            buffer = buffer.at[target].set(flat_tok, mode='drop')
        wide_buffer = buffer.astype(jnp.float32)
        gate_act = jnp.dot(wide_buffer, gate_w.astype(jnp.float32))
        up_act = jnp.dot(wide_buffer, up_w.astype(jnp.float32))
        hidden = (jax.nn.silu(gate_act) * up_act).astype(jnp.bfloat16)
        result = jnp.dot(hidden.astype(jnp.float32), down_w.astype(jnp.float32)).astype(jnp.bfloat16)
        for column in range(2):
            chosen = expert_ids[:, column] == expert_index
            picked = result[jnp.minimum(position[:, column], rows_total - 1)].astype(jnp.float32)
            summed = summed + jnp.where(chosen[:, None], weights[:, column:column + 1] * picked, 0.0)
        return (summed, None)
    start = jnp.zeros((flat_tok.shape[0], D), jnp.float32)
    summed, _ = lax.scan(one_expert, start, (jnp.arange(EXPERTS, dtype=jnp.int32), w_gate, w_up, w_down))
    rounded = lax.optimization_barrier(summed.astype(jnp.bfloat16))
    widened = rounded.astype(jnp.float32)
    inv_rms = lax.rsqrt(lax.optimization_barrier(jnp.mean(widened * widened, axis=1, keepdims=True)) + epsilon)
    return (widened * inv_rms * norm_gain[None, :]).astype(jnp.bfloat16).reshape(SEQS, LENGTH, D)
```

```python
import functools

import jax
import jax.numpy as jnp
from jax import lax
from jax.experimental import pallas as pl
from jax.experimental.pallas import tpu as pltpu
from jax.sharding import PartitionSpec as P

epsilon = 1e-06


F32 = jnp.float32
BF16 = jnp.bfloat16


def expert_ffn(slot_block, w_gate, w_up, w_down):
    shape_in = slot_block.shape
    flat_rows = slot_block.reshape(-1, shape_in[-1])
    gate_act = jnp.dot(flat_rows, w_gate[0], preferred_element_type=F32)
    up_act = jnp.dot(flat_rows, w_up[0], preferred_element_type=F32)
    hidden = (jax.nn.silu(gate_act) * up_act).astype(BF16)
    result = jnp.dot(hidden, w_down[0], preferred_element_type=F32).astype(BF16)
    return result.reshape(shape_in)


def lookup(codes, gate_table):
    levels = gate_table.shape[0]
    match = codes[:, None] == jnp.arange(levels, dtype=jnp.int32)[None, :]
    return jnp.sum(jnp.where(match, gate_table[None, :], 0.0), axis=1)


def combine_pairs(outputs, weights):
    combined = outputs[:, 0] * weights[:, 0:1] + outputs[:, 1] * weights[:, 1:2]
    rounded = lax.optimization_barrier(combined.astype(BF16))
    return rounded.astype(F32)


def local_general(tokens, routes, gate_code, gate_table, w_gate, w_up, w_down, norm_gain):
    own_rows = tokens[0]
    tok_count, feat_width = own_rows.shape
    experts = w_gate.shape[0] * lax.axis_size("expert")
    capacity = 5 * tok_count // (2 * experts)
    route_ids = routes[0].reshape(-1)
    onehot = (route_ids[:, None] == jnp.arange(experts, dtype=jnp.int32)[None, :]).astype(jnp.int32)
    slot_pos = jnp.sum((jnp.cumsum(onehot, axis=0) - onehot) * onehot, axis=1)
    position = route_ids * capacity + slot_pos
    owner_row = (
        jnp.zeros((experts * capacity,), jnp.int32)
        .at[position]
        .set(jnp.arange(2 * tok_count, dtype=jnp.int32) // 2)
    )
    filled = jnp.zeros((experts * capacity,), jnp.bool_).at[position].set(True)
    buffer = jnp.where(filled[:, None], own_rows[owner_row], jnp.zeros((), BF16))
    buffer = buffer.reshape(experts, capacity, feat_width)
    level_ids = gate_code[0].reshape(-1)
    received = lax.all_to_all(buffer, "expert", split_axis=0, concat_axis=0, tiled=True)
    expert_out = expert_ffn(received, w_gate, w_up, w_down)
    returned = lax.all_to_all(expert_out, "expert", split_axis=0, concat_axis=0, tiled=True)
    outputs = (
        returned.reshape(-1, feat_width)[position]
        .astype(F32)
        .reshape(tok_count, 2, feat_width)
    )
    weights = lookup(level_ids, gate_table).reshape(tok_count, 2)
    widened = combine_pairs(outputs, weights)
    inv_rms = lax.rsqrt(jnp.mean(widened * widened, axis=1, keepdims=True) + epsilon)
    normed = (widened * inv_rms * norm_gain[None, :]).astype(BF16)
    relaid = lax.all_to_all(normed, "dp", split_axis=1, concat_axis=0, tiled=True)
    return relaid[None]


def vmem():
    return pl.BlockSpec(memory_space=pltpu.VMEM)


def slot_rows(route_rows, experts, me):
    tok = route_rows.shape[1]
    ids = lax.broadcasted_iota(jnp.int32, (experts, tok), 0) ^ me
    named = (route_rows[0:1, :] == ids) | (route_rows[1:2, :] == ids)
    earlier = lax.broadcasted_iota(jnp.int32, (tok, tok), 0) < lax.broadcasted_iota(
        jnp.int32, (tok, tok), 1
    )
    count = jnp.dot(
        named.astype(F32).astype(BF16), earlier.astype(F32).astype(BF16),
        preferred_element_type=F32,
    )
    return jnp.where(named, count.astype(jnp.int32), -1), ids


def dispatch_body(experts, capacity, route_ref, tok_ref, *out_refs):
    me = lax.axis_index("expert")
    slots, _ = slot_rows(route_ref[...], experts, me)
    tok, width = tok_ref.shape
    lane = lax.broadcasted_iota(jnp.int32, (capacity, tok), 0)
    pick = jnp.concatenate(
        [(lane == slots[j : j + 1, :]).astype(F32) for j in range(experts)], axis=0
    ).astype(BF16)
    tile = 256
    for col in range(0, width, tile):
        rows = jnp.dot(pick, tok_ref[:, col : col + tile], preferred_element_type=F32)
        rows = rows.astype(BF16)
        for j in range(experts):
            out_refs[j][:, col : col + tile] = rows[j * capacity : (j + 1) * capacity, :]


def dispatch(route_rows, own_rows, experts, capacity):
    width = own_rows.shape[1]
    return pl.pallas_call(
        functools.partial(dispatch_body, experts, capacity),
        out_shape=[jax.ShapeDtypeStruct((capacity, width), BF16)] * experts,
        in_specs=[vmem()] * 2,
        out_specs=[vmem()] * experts,
        name="dispatch",
        cost_estimate=pl.CostEstimate(flops=10**8, transcendentals=0, bytes_accessed=2 * 10**6),
        compiler_params=pltpu.CompilerParams(vmem_limit_bytes=16 * 2**20),
    )(route_rows, own_rows)


def selector_body(experts, capacity, route_ref, code_ref, table_ref, sel_ref, weight_ref):
    me = lax.axis_index("expert")
    rows = route_ref[...]
    slots, ids = slot_rows(rows, experts, me)
    tok = rows.shape[1]
    lane = lax.broadcasted_iota(jnp.int32, (capacity, tok), 0)
    for r in range(2):
        mine = jnp.where(rows[r : r + 1, :] == ids, slots, -1)
        pick = jnp.concatenate(
            [(lane == mine[j : j + 1, :]).astype(F32) for j in range(experts)], axis=0
        )
        sel_ref[r * tok : (r + 1) * tok, :] = pick.T.astype(BF16)
        codes = code_ref[r : r + 1, :]
        weights = jnp.zeros((1, tok), F32)
        for level in range(table_ref.shape[0]):
            weights = jnp.where(codes == level, table_ref[level], weights)
        weight_ref[r] = jnp.broadcast_to(weights, (tok, tok)).T


def selector(route_rows, code_rows, gate_table, experts, capacity):
    tok = route_rows.shape[1]
    return pl.pallas_call(
        functools.partial(selector_body, experts, capacity),
        out_shape=[
            jax.ShapeDtypeStruct((2 * tok, experts * capacity), BF16),
            jax.ShapeDtypeStruct((2, tok, tok), F32),
        ],
        in_specs=[vmem(), vmem(), pl.BlockSpec(memory_space=pltpu.SMEM)],
        out_specs=[vmem()] * 2,
        name="selector",
        cost_estimate=pl.CostEstimate(flops=10**7, transcendentals=0, bytes_accessed=10**6),
        compiler_params=pltpu.CompilerParams(vmem_limit_bytes=8 * 2**20),
    )(route_rows, code_rows, gate_table)


def hidden_body(capacity, *refs):
    blocks, (gate_ref, up_ref, hid_ref, x_ref) = refs[:-4], refs[-4:]
    for j, block in enumerate(blocks):
        x_ref[j * capacity : (j + 1) * capacity, :] = block[...]
    hid = gate_ref.shape[0]
    tile = 256
    over = (((1,), (1,)), ((), ()))
    for low in range(0, hid, tile):
        high = min(hid, low + tile)
        gate = lax.dot_general(x_ref[...], gate_ref[low:high, :], over, preferred_element_type=F32)
        up = lax.dot_general(x_ref[...], up_ref[low:high, :], over, preferred_element_type=F32)
        hid_ref[:, low:high] = (gate / (1.0 + jnp.exp(-gate)) * up).astype(BF16)


def hidden_of(blocks, gate_rows, up_rows):
    capacity, width = blocks[0].shape
    rows, hid = capacity * len(blocks), gate_rows.shape[0]
    return pl.pallas_call(
        functools.partial(hidden_body, capacity),
        out_shape=jax.ShapeDtypeStruct((rows, hid), BF16),
        in_specs=[vmem()] * (len(blocks) + 2),
        out_specs=vmem(),
        scratch_shapes=[pltpu.VMEM((rows, width), BF16)],
        name="hidden",
        cost_estimate=pl.CostEstimate(
            flops=4 * rows * hid * width, transcendentals=rows * hid, bytes_accessed=8 * 10**6
        ),
        compiler_params=pltpu.CompilerParams(vmem_limit_bytes=24 * 2**20),
    )(*blocks, gate_rows, up_rows)


def down_body(which, capacity, hid_ref, down_ref, *out_refs):
    ways = lax.axis_size("dp") // 2
    half = lax.axis_index("dp") // ways
    width = out_refs[0].shape[1]
    start = (half if which else 1 - half) * width
    tile = 256
    for col in range(0, width, tile):
        cols = pl.ds(pl.multiple_of(start + col, tile), tile)
        rows = jnp.dot(hid_ref[...], down_ref[:, cols], preferred_element_type=F32).astype(BF16)
        for j, out in enumerate(out_refs):
            out[:, col : col + tile] = rows[j * capacity : (j + 1) * capacity, :]


def down_of(which, hidden, down_rows, experts):
    rows, hid = hidden.shape
    width = down_rows.shape[1] // 2
    capacity = rows // experts
    return pl.pallas_call(
        functools.partial(down_body, which, capacity),
        out_shape=[jax.ShapeDtypeStruct((capacity, width), BF16)] * experts,
        in_specs=[vmem()] * 2,
        out_specs=[vmem()] * experts,
        name=f"down{which}",
        cost_estimate=pl.CostEstimate(
            flops=2 * rows * hid * width, transcendentals=0, bytes_accessed=3 * 10**6
        ),
        compiler_params=pltpu.CompilerParams(vmem_limit_bytes=16 * 2**20),
    )(hidden, down_rows)


def combine_body(has_prior, chunk, *refs):
    if has_prior:
        sel_ref, weight_ref, prior_ref, *rest = refs
    else:
        sel_ref, weight_ref, *rest = refs
        prior_ref = None
    y_ref = rest[-1]
    sum_ref = rest[-2]
    capacity = rest[0].shape[0]
    experts = y_ref.shape[0] // capacity
    blocks, outs = rest[:experts], rest[experts:-2]
    low = lax.axis_index("dp") % len(outs)
    for j, block in enumerate(blocks):
        y_ref[j * capacity : (j + 1) * capacity, :] = block[...]
    tok = weight_ref.shape[1]
    lanes = weight_ref.shape[2]
    tile = 256
    squares = jnp.zeros((tok, lanes), F32)
    for q, out in enumerate(outs):
        start = (low ^ q) * chunk
        for col in range(0, chunk, tile):
            cols = pl.ds(pl.multiple_of(start + col, tile), tile)
            picked = jnp.dot(sel_ref[...], y_ref[:, cols], preferred_element_type=F32)
            for at in range(0, tile, lanes):
                first = picked[:tok, at : at + lanes] * weight_ref[0]
                second = picked[tok:, at : at + lanes] * weight_ref[1]
                rounded = (first + second).astype(BF16)
                out[:, col + at : col + at + lanes] = rounded
                wide = rounded.astype(F32)
                squares = squares + wide * wide
    total = jnp.sum(squares.T, axis=0, keepdims=True)
    total = jnp.broadcast_to(total, sum_ref.shape)
    if prior_ref is not None:
        total = total + prior_ref[...]
    sum_ref[...] = total


def combine_half(select, weights, prior, blocks, chunk):
    capacity, width = blocks[0].shape
    rows = capacity * len(blocks)
    tok = weights.shape[1]
    heads = [select, weights] + ([] if prior is None else [prior])
    return pl.pallas_call(
        functools.partial(combine_body, prior is not None, chunk),
        out_shape=[jax.ShapeDtypeStruct((tok, chunk), BF16)] * (width // chunk)
        + [jax.ShapeDtypeStruct((8, tok), F32)],
        in_specs=[vmem()] * (len(heads) + len(blocks)),
        out_specs=[vmem()] * (width // chunk + 1),
        scratch_shapes=[pltpu.VMEM((rows, width), BF16)],
        name="combine",
        cost_estimate=pl.CostEstimate(
            flops=4 * tok * rows * width, transcendentals=0, bytes_accessed=2 * 10**6
        ),
        compiler_params=pltpu.CompilerParams(vmem_limit_bytes=12 * 2**20),
    )(*heads, *blocks)


def finish_body(feat_width, *refs):
    out_ref = refs[-1]
    gain_ref = refs[-2]
    ways = (len(refs) - 2) // 2
    chunks, sums = refs[:ways], refs[ways : 2 * ways]
    me = lax.axis_index("dp")
    tok, width = chunks[0].shape
    gain = gain_ref[:, pl.ds(pl.multiple_of(me * width, 128), width)]
    for k in range(ways):
        inv = lax.rsqrt(sums[k][0:1, :] * (1.0 / feat_width) + epsilon)
        column = jnp.broadcast_to(inv, (tok, tok)).T[:, 0:1]
        value = chunks[k][...].astype(F32) * column * gain
        out_ref[pl.ds(pl.multiple_of((me ^ k) * tok, tok), tok), :] = value.astype(BF16)


def finish(chunks, sums, gain, feat_width):
    tok, width = chunks[0].shape
    return pl.pallas_call(
        functools.partial(finish_body, feat_width),
        out_shape=jax.ShapeDtypeStruct((tok * len(chunks), width), BF16),
        in_specs=[vmem()] * (2 * len(chunks) + 1),
        out_specs=vmem(),
        name="finish",
        cost_estimate=pl.CostEstimate(flops=10**6, transcendentals=0, bytes_accessed=10**6),
        compiler_params=pltpu.CompilerParams(vmem_limit_bytes=8 * 2**20),
    )(*chunks, *sums, gain)


def swap(value, axis, offset):
    size = lax.axis_size(axis)
    return lax.ppermute(value, axis, [(i, i ^ offset) for i in range(size)])


def far_first(size):
    return sorted(range(1, size), key=lambda k: (-bin(k >> 1).count("1"), k))


def swap_all(blocks, axis):
    moved = {0: blocks[0]}
    for k in far_first(len(blocks)):
        moved[k] = swap(blocks[k], axis, k)
    return [moved[k] for k in range(len(blocks))]


def local_fast(tokens, routes, gate_code, gate_table, w_gate, w_up, w_down, norm_gain):
    own_rows = tokens[0]
    tok, feat_width = own_rows.shape
    experts = lax.axis_size("expert")
    ways = lax.axis_size("dp")
    capacity = 5 * tok // (2 * experts)
    chunk = feat_width // ways
    route_rows = routes[0].T
    blocks = dispatch(route_rows, own_rows, experts, capacity)
    received = swap_all(blocks, "expert")
    select, weights = selector(route_rows, gate_code[0].T, gate_table, experts, capacity)
    hidden = hidden_of(received, w_gate[0].T, w_up[0].T)

    far = swap_all(down_of(0, hidden, w_down[0], experts), "expert")
    near = swap_all(down_of(1, hidden, w_down[0], experts), "expert")

    *far_chunks, part = combine_half(select, weights, None, far, chunk)
    *near_chunks, total = combine_half(select, weights, part, near, chunk)
    mine = swap_all(near_chunks + far_chunks, "dp")
    sums = swap_all([total] * ways, "dp")
    return finish(mine, sums, norm_gain[None, :], feat_width)[None]


def solution(mesh):
    in_specs = (
        P("expert", "dp", None),
        P("expert", "dp", None),
        P("expert", "dp", None),
        P(),
        P("expert", None, None),
        P("expert", None, None),
        P("expert", None, None),
        P(),
    )
    out_specs = P("expert", None, "dp")

    def whole(tokens, routes, gate_code, gate_table, w_gate, w_up, w_down, norm_gain):
        args = (tokens, routes, gate_code, gate_table, w_gate, w_up, w_down, norm_gain)
        experts, ways = mesh.shape["expert"], mesh.shape["dp"]
        tok, feat = tokens.shape[1] // ways, tokens.shape[2]
        power = experts & (experts - 1) == 0 and ways & (ways - 1) == 0
        fits = power and 2 <= experts <= 8 and 2 <= ways <= 4
        fits = fits and tok % 128 == 0 and w_gate.shape[0] == experts
        fits = fits and 5 * tok % (16 * experts) == 0 and feat % (256 * ways) == 0
        body = local_fast if fits else local_general
        f = jax.shard_map(body, mesh=mesh, in_specs=in_specs, out_specs=out_specs, check_vma=False)
        return f(*args)

    return whole
```

```python
import functools

import jax
import jax.numpy as jnp
from jax import lax
from jax.experimental import pallas as pl
from jax.experimental.pallas import tpu as pltpu
from jax.sharding import PartitionSpec as P


epsilon = 1e-06


F32 = jnp.float32
BF16 = jnp.bfloat16


def expert_ffn(slot_block, w_gate, w_up, w_down):
    shape_in = slot_block.shape
    flat_rows = slot_block.reshape(-1, shape_in[-1])
    gate_act = jnp.dot(flat_rows, w_gate[0], preferred_element_type=F32)
    up_act = jnp.dot(flat_rows, w_up[0], preferred_element_type=F32)
    hidden = (jax.nn.silu(gate_act) * up_act).astype(BF16)
    result = jnp.dot(hidden, w_down[0], preferred_element_type=F32).astype(BF16)
    return result.reshape(shape_in)


def lookup(codes, gate_table):
    levels = gate_table.shape[0]
    match = codes[:, None] == jnp.arange(levels, dtype=jnp.int32)[None, :]
    return jnp.sum(jnp.where(match, gate_table[None, :], 0.0), axis=1)


def combine_pairs(outputs, weights):
    combined = outputs[:, 0] * weights[:, 0:1] + outputs[:, 1] * weights[:, 1:2]
    rounded = lax.optimization_barrier(combined.astype(BF16))
    return rounded.astype(F32)


def local_general(tokens, routes, gate_code, gate_table, w_gate, w_up, w_down, norm_gain):
    own_rows = tokens[0]
    tok_count, feat_width = own_rows.shape
    experts = w_gate.shape[0] * lax.axis_size("expert")
    capacity = 5 * tok_count // (2 * experts)
    route_ids = routes[0].reshape(-1)
    onehot = (route_ids[:, None] == jnp.arange(experts, dtype=jnp.int32)[None, :]).astype(jnp.int32)
    slot_pos = jnp.sum((jnp.cumsum(onehot, axis=0) - onehot) * onehot, axis=1)
    position = route_ids * capacity + slot_pos
    owner_row = (
        jnp.zeros((experts * capacity,), jnp.int32)
        .at[position]
        .set(jnp.arange(2 * tok_count, dtype=jnp.int32) // 2)
    )
    filled = jnp.zeros((experts * capacity,), jnp.bool_).at[position].set(True)
    buffer = jnp.where(filled[:, None], own_rows[owner_row], jnp.zeros((), BF16))
    buffer = buffer.reshape(experts, capacity, feat_width)
    level_ids = gate_code[0].reshape(-1)
    received = lax.all_to_all(buffer, "expert", split_axis=0, concat_axis=0, tiled=True)
    expert_out = expert_ffn(received, w_gate, w_up, w_down)
    returned = lax.all_to_all(expert_out, "expert", split_axis=0, concat_axis=0, tiled=True)
    outputs = (
        returned.reshape(-1, feat_width)[position]
        .astype(F32)
        .reshape(tok_count, 2, feat_width)
    )
    weights = lookup(level_ids, gate_table).reshape(tok_count, 2)
    widened = combine_pairs(outputs, weights)
    inv_rms = lax.rsqrt(jnp.mean(widened * widened, axis=1, keepdims=True) + epsilon)
    normed = (widened * inv_rms * norm_gain[None, :]).astype(BF16)
    relaid = lax.all_to_all(normed, "dp", split_axis=1, concat_axis=0, tiled=True)
    return relaid[None]


def vmem():
    return pl.BlockSpec(memory_space=pltpu.VMEM)


def slot_rows(route_rows, experts, me):
    tok = route_rows.shape[1]
    ids = lax.broadcasted_iota(jnp.int32, (experts, tok), 0) ^ me
    named = (route_rows[0:1, :] == ids) | (route_rows[1:2, :] == ids)
    earlier = lax.broadcasted_iota(jnp.int32, (tok, tok), 0) < lax.broadcasted_iota(
        jnp.int32, (tok, tok), 1
    )
    count = jnp.dot(
        named.astype(F32).astype(BF16), earlier.astype(F32).astype(BF16),
        preferred_element_type=F32,
    )
    return jnp.where(named, count.astype(jnp.int32), -1), ids


def dispatch_body(experts, capacity, route_hbm, tok_hbm, *refs):
    *out_refs, route_ref, tok_ref, sems = refs
    copies = [
        pltpu.make_async_copy(route_hbm, route_ref, sems.at[0]),
        pltpu.make_async_copy(tok_hbm, tok_ref, sems.at[1]),
    ]
    for copy in copies:
        copy.start()
    me = lax.axis_index("expert")
    tok, width = tok_ref.shape
    lane = lax.broadcasted_iota(jnp.int32, (capacity, tok), 0)
    copies[0].wait()
    slots, _ = slot_rows(route_ref[...], experts, me)
    pick = jnp.concatenate(
        [(lane == slots[j : j + 1, :]).astype(F32) for j in range(experts)], axis=0
    ).astype(BF16)
    copies[1].wait()
    tile = 256
    for col in range(0, width, tile):
        rows = jnp.dot(pick, tok_ref[:, col : col + tile], preferred_element_type=F32)
        rows = rows.astype(BF16)
        for j in range(experts):
            out_refs[j][:, col : col + tile] = rows[j * capacity : (j + 1) * capacity, :]


def dispatch(route_rows, own_rows, experts, capacity):
    width = own_rows.shape[1]
    return pl.pallas_call(
        functools.partial(dispatch_body, experts, capacity),
        out_shape=[jax.ShapeDtypeStruct((capacity, width), BF16)] * experts,
        in_specs=[pl.BlockSpec(memory_space=pltpu.HBM)] * 2,
        out_specs=[vmem()] * experts,
        scratch_shapes=[
            pltpu.VMEM(route_rows.shape, jnp.int32),
            pltpu.VMEM(own_rows.shape, BF16),
            pltpu.SemaphoreType.DMA((2,)),
        ],
        name="dispatch",
        cost_estimate=pl.CostEstimate(flops=10**8, transcendentals=0, bytes_accessed=2 * 10**6),
        compiler_params=pltpu.CompilerParams(vmem_limit_bytes=16 * 2**20),
    )(route_rows, own_rows)


def selector_body(experts, capacity, route_ref, code_ref, table_ref, *refs):
    sources, (sel_ref, weight_ref), copied, sems = refs[:3], refs[3:5], refs[5:8], refs[8]
    copies = [
        pltpu.make_async_copy(src, dst, sems.at[i])
        for i, (src, dst) in enumerate(zip(sources, copied))
    ]
    for copy in copies:
        copy.start()
    me = lax.axis_index("expert")
    rows = route_ref[...]
    slots, ids = slot_rows(rows, experts, me)
    tok = rows.shape[1]
    lane = lax.broadcasted_iota(jnp.int32, (capacity, tok), 0)
    for r in range(2):
        mine = jnp.where(rows[r : r + 1, :] == ids, slots, -1)
        pick = jnp.concatenate(
            [(lane == mine[j : j + 1, :]).astype(F32) for j in range(experts)], axis=0
        )
        sel_ref[r * tok : (r + 1) * tok, :] = pick.T.astype(BF16)
        codes = code_ref[r : r + 1, :]
        weights = jnp.zeros((1, tok), F32)
        for level in range(table_ref.shape[0]):
            weights = jnp.where(codes == level, table_ref[level], weights)
        weight_ref[r] = jnp.broadcast_to(weights, (tok, tok)).T
    for copy in copies:
        copy.wait()


def selector(route_rows, code_rows, gate_table, matrices, experts, capacity):
    tok = route_rows.shape[1]
    return pl.pallas_call(
        functools.partial(selector_body, experts, capacity),
        out_shape=[
            jax.ShapeDtypeStruct((2 * tok, experts * capacity), BF16),
            jax.ShapeDtypeStruct((2, tok, tok), F32),
        ]
        + [jax.ShapeDtypeStruct(m.shape, m.dtype) for m in matrices],
        in_specs=[vmem(), vmem(), pl.BlockSpec(memory_space=pltpu.SMEM)]
        + [pl.BlockSpec(memory_space=pltpu.HBM)] * 3,
        out_specs=[vmem()] * 5,
        scratch_shapes=[pltpu.SemaphoreType.DMA((3,))],
        name="selector",
        cost_estimate=pl.CostEstimate(flops=10**7, transcendentals=0, bytes_accessed=10**7),
        compiler_params=pltpu.CompilerParams(vmem_limit_bytes=24 * 2**20),
    )(route_rows, code_rows, gate_table, *matrices)


def half_start(which, width):
    own = lax.axis_index("dp") // (lax.axis_size("dp") // 2)
    return (own if which else 1 - own) * width


def write_down(hid_ref, down_ref, start, out_refs):
    capacity, width = out_refs[0].shape
    tile = 256
    for col in range(0, width, tile):
        cols = pl.ds(pl.multiple_of(start + col, tile), tile)
        rows = jnp.dot(hid_ref[...], down_ref[:, cols], preferred_element_type=F32).astype(BF16)
        for j, out in enumerate(out_refs):
            out[:, col : col + tile] = rows[j * capacity : (j + 1) * capacity, :]


def expert_body(count, *refs):
    blocks, (gate_ref, up_ref, down_ref) = refs[:count], refs[count : count + 3]
    hid_ref, x_ref, outs = refs[count + 3], refs[-1], refs[count + 4 : -1]
    capacity = blocks[0].shape[0]
    for j, block in enumerate(blocks):
        x_ref[j * capacity : (j + 1) * capacity, :] = block[...]
    hid = gate_ref.shape[0]
    tile = 256
    over = (((1,), (1,)), ((), ()))
    for low in range(0, hid, tile):
        high = min(hid, low + tile)
        gate = lax.dot_general(x_ref[...], gate_ref[low:high, :], over, preferred_element_type=F32)
        up = lax.dot_general(x_ref[...], up_ref[low:high, :], over, preferred_element_type=F32)
        hid_ref[:, low:high] = (gate / (1.0 + jnp.exp(-gate)) * up).astype(BF16)
    write_down(hid_ref, down_ref, half_start(0, outs[0].shape[1]), outs)


def expert_far(blocks, gate_rows, up_rows, down_rows):
    count = len(blocks)
    capacity, width = blocks[0].shape
    rows, hid = capacity * count, gate_rows.shape[0]
    out_width = down_rows.shape[1] // 2
    hidden, *outs = pl.pallas_call(
        functools.partial(expert_body, count),
        out_shape=[jax.ShapeDtypeStruct((rows, hid), BF16)]
        + [jax.ShapeDtypeStruct((capacity, out_width), BF16)] * count,
        in_specs=[vmem()] * (count + 3),
        out_specs=[vmem()] * (count + 1),
        scratch_shapes=[pltpu.VMEM((rows, width), BF16)],
        cost_estimate=pl.CostEstimate(
            flops=5 * rows * hid * width, transcendentals=rows * hid, bytes_accessed=8 * 10**6
        ),
        compiler_params=pltpu.CompilerParams(vmem_limit_bytes=24 * 2**20),
    )(*blocks, gate_rows, up_rows, down_rows)
    return hidden, outs


def near_body(hid_ref, down_ref, *out_refs):
    write_down(hid_ref, down_ref, half_start(1, out_refs[0].shape[1]), out_refs)


def expert_near(hidden, down_rows, count):
    rows, hid = hidden.shape
    width = down_rows.shape[1] // 2
    return pl.pallas_call(
        near_body,
        out_shape=[jax.ShapeDtypeStruct((rows // count, width), BF16)] * count,
        in_specs=[vmem()] * 2,
        out_specs=[vmem()] * count,
        cost_estimate=pl.CostEstimate(
            flops=2 * rows * hid * width, transcendentals=0, bytes_accessed=3 * 10**6
        ),
        compiler_params=pltpu.CompilerParams(vmem_limit_bytes=16 * 2**20),
    )(hidden, down_rows)


def combine_body(has_prior, chunk, *refs):
    if has_prior:
        sel_ref, weight_ref, prior_ref, *rest = refs
    else:
        sel_ref, weight_ref, *rest = refs
        prior_ref = None
    y_ref = rest[-1]
    sum_ref = rest[-2]
    capacity = rest[0].shape[0]
    experts = y_ref.shape[0] // capacity
    blocks, outs = rest[:experts], rest[experts:-2]
    low = lax.axis_index("dp") % len(outs)
    for j, block in enumerate(blocks):
        y_ref[j * capacity : (j + 1) * capacity, :] = block[...]
    tok = weight_ref.shape[1]
    lanes = weight_ref.shape[2]
    tile = 256
    squares = jnp.zeros((tok, lanes), F32)
    for q, out in enumerate(outs):
        start = (low ^ q) * chunk
        for col in range(0, chunk, tile):
            cols = pl.ds(pl.multiple_of(start + col, tile), tile)
            picked = jnp.dot(sel_ref[...], y_ref[:, cols], preferred_element_type=F32)
            for at in range(0, tile, lanes):
                first = picked[:tok, at : at + lanes] * weight_ref[0]
                second = picked[tok:, at : at + lanes] * weight_ref[1]
                rounded = (first + second).astype(BF16)
                out[:, col + at : col + at + lanes] = rounded
                wide = rounded.astype(F32)
                squares = squares + wide * wide
    total = jnp.sum(squares.T, axis=0, keepdims=True)
    total = jnp.broadcast_to(total, sum_ref.shape)
    if prior_ref is not None:
        total = total + prior_ref[...]
    sum_ref[...] = total


def combine_half(select, weights, prior, blocks, chunk):
    capacity, width = blocks[0].shape
    rows = capacity * len(blocks)
    tok = weights.shape[1]
    heads = [select, weights] + ([] if prior is None else [prior])
    return pl.pallas_call(
        functools.partial(combine_body, prior is not None, chunk),
        out_shape=[jax.ShapeDtypeStruct((tok, chunk), BF16)] * (width // chunk)
        + [jax.ShapeDtypeStruct((8, tok), F32)],
        in_specs=[vmem()] * (len(heads) + len(blocks)),
        out_specs=[vmem()] * (width // chunk + 1),
        scratch_shapes=[pltpu.VMEM((rows, width), BF16)],
        cost_estimate=pl.CostEstimate(
            flops=4 * tok * rows * width, transcendentals=0, bytes_accessed=2 * 10**6
        ),
        compiler_params=pltpu.CompilerParams(vmem_limit_bytes=12 * 2**20),
    )(*heads, *blocks)


def gain_body(gain_ref, out_ref):
    width = out_ref.shape[1]
    start = pl.multiple_of(lax.axis_index("dp") * width, 128)
    out_ref[...] = jnp.broadcast_to(gain_ref[:, pl.ds(start, width)], out_ref.shape)


def own_gain(norm_gain, chunk):
    return pl.pallas_call(
        gain_body,
        out_shape=jax.ShapeDtypeStruct((8, chunk), F32),
        in_specs=[vmem()],
        out_specs=vmem(),
        name="gain",
        cost_estimate=pl.CostEstimate(flops=10**4, transcendentals=0, bytes_accessed=10**4),
        compiler_params=pltpu.CompilerParams(vmem_limit_bytes=2**20),
    )(norm_gain[None, :])


def finish_body(feat_width, *refs):
    out_ref = refs[-1]
    gain_ref = refs[-2]
    ways = (len(refs) - 2) // 2
    chunks, sums = refs[:ways], refs[ways : 2 * ways]
    me = lax.axis_index("dp")
    tok = chunks[0].shape[0]
    gain = gain_ref[0:1, :]
    for k in range(ways):
        inv = lax.rsqrt(sums[k][0:1, :] * (1.0 / feat_width) + epsilon)
        column = jnp.broadcast_to(inv, (tok, tok)).T[:, 0:1]
        value = chunks[k][...].astype(F32) * column * gain
        out_ref[pl.ds(pl.multiple_of((me ^ k) * tok, tok), tok), :] = value.astype(BF16)


def finish(chunks, sums, gain, feat_width):
    tok, width = chunks[0].shape
    return pl.pallas_call(
        functools.partial(finish_body, feat_width),
        out_shape=jax.ShapeDtypeStruct((tok * len(chunks), width), BF16),
        in_specs=[vmem()] * (2 * len(chunks) + 1),
        out_specs=vmem(),
        name="finish",
        cost_estimate=pl.CostEstimate(flops=10**6, transcendentals=0, bytes_accessed=10**6),
        compiler_params=pltpu.CompilerParams(vmem_limit_bytes=8 * 2**20),
    )(*chunks, *sums, gain)


def swap(value, axis, offset):
    size = lax.axis_size(axis)
    return lax.ppermute(value, axis, [(i, i ^ offset) for i in range(size)])


def swap_each(values, axis):
    moved = {}
    for k, value in values.items():
        moved[k] = swap(value, axis, k) if k else value
    return moved


def local_fast(tokens, routes, gate_code, gate_table, w_gate, w_up, w_down, norm_gain):
    return fast_steps(tokens, routes, gate_code, gate_table, w_gate, w_up, w_down, norm_gain)


def fast_steps(tokens, routes, gate_code, gate_table, w_gate, w_up, w_down, norm_gain):
    own_rows = tokens[0]
    tok, feat_width = own_rows.shape
    experts = lax.axis_size("expert")
    ways = lax.axis_size("dp")
    half = ways // 2
    capacity = 5 * tok // (2 * experts)
    chunk = feat_width // ways
    links = [bin(k >> 1).count("1") for k in range(experts)]
    first = [k for k in range(experts - 1, -1, -1) if links[k] != 1]
    second = [k for k in range(experts) if links[k] == 1]

    route_rows = routes[0].T
    blocks = dispatch(route_rows, own_rows, experts, capacity)
    got_a = swap_each({k: blocks[k] for k in first}, "expert")
    got_b = swap_each({k: blocks[k] for k in second}, "expert")
    select, weights, gate_rows, up_rows, down_rows = selector(
        route_rows, gate_code[0].T, gate_table,
        (w_gate[0].T, w_up[0].T, w_down[0]), experts, capacity,
    )

    hid_a, far_a = expert_far([got_a[k] for k in first], gate_rows, up_rows, down_rows)
    far = swap_each(dict(zip(first, far_a)), "expert")
    near_a = expert_near(hid_a, down_rows, len(first))
    hid_b, far_b = expert_far([got_b[k] for k in second], gate_rows, up_rows, down_rows)
    far |= swap_each(dict(zip(second, far_b)), "expert")
    near_b = expert_near(hid_b, down_rows, len(second))
    near = swap_each(dict(zip(first, near_a)), "expert")
    near |= swap_each(dict(zip(second, near_b)), "expert")

    order = range(experts)
    *far_chunks, part = combine_half(select, weights, None, [far[k] for k in order], chunk)
    chunks = swap_each({half + q: c for q, c in enumerate(far_chunks)}, "dp")
    gain = own_gain(norm_gain, chunk)
    *near_chunks, total = combine_half(select, weights, part, [near[k] for k in order], chunk)
    sums = swap_each({k: total for k in range(ways - 1, -1, -1)}, "dp")
    chunks |= swap_each({q: c for q, c in enumerate(near_chunks)}, "dp")
    mine = range(ways)
    return finish([chunks[k] for k in mine], [sums[k] for k in mine], gain, feat_width)[None]


def solution(mesh):
    in_specs = (
        P("expert", "dp", None),
        P("expert", "dp", None),
        P("expert", "dp", None),
        P(),
        P("expert", None, None),
        P("expert", None, None),
        P("expert", None, None),
        P(),
    )
    out_specs = P("expert", None, "dp")

    def whole(tokens, routes, gate_code, gate_table, w_gate, w_up, w_down, norm_gain):
        args = (tokens, routes, gate_code, gate_table, w_gate, w_up, w_down, norm_gain)
        experts, ways = mesh.shape["expert"], mesh.shape["dp"]
        tok, feat = tokens.shape[1] // ways, tokens.shape[2]
        power = experts & (experts - 1) == 0 and ways & (ways - 1) == 0
        fits = power and 4 <= experts <= 8 and 2 <= ways <= 4
        fits = fits and tok % 128 == 0 and w_gate.shape[0] == experts
        fits = fits and 5 * tok % (16 * experts) == 0 and feat % (256 * ways) == 0
        body = local_fast if fits else local_general
        f = jax.shard_map(body, mesh=mesh, in_specs=in_specs, out_specs=out_specs, check_vma=False)
        return f(*args)

    return whole
```

```python
import functools

import jax
import jax.numpy as jnp
from jax import lax
from jax.experimental import pallas as pl
from jax.experimental.pallas import tpu as pltpu
from jax.sharding import PartitionSpec as P


epsilon = 1e-06


F32 = jnp.float32
BF16 = jnp.bfloat16


def expert_ffn(slot_block, w_gate, w_up, w_down):
    shape_in = slot_block.shape
    flat_rows = slot_block.reshape(-1, shape_in[-1])
    gate_act = jnp.dot(flat_rows, w_gate[0], preferred_element_type=F32)
    up_act = jnp.dot(flat_rows, w_up[0], preferred_element_type=F32)
    hidden = (jax.nn.silu(gate_act) * up_act).astype(BF16)
    result = jnp.dot(hidden, w_down[0], preferred_element_type=F32).astype(BF16)
    return result.reshape(shape_in)


def lookup(codes, gate_table):
    levels = gate_table.shape[0]
    match = codes[:, None] == jnp.arange(levels, dtype=jnp.int32)[None, :]
    return jnp.sum(jnp.where(match, gate_table[None, :], 0.0), axis=1)


def combine_pairs(outputs, weights):
    combined = outputs[:, 0] * weights[:, 0:1] + outputs[:, 1] * weights[:, 1:2]
    rounded = lax.optimization_barrier(combined.astype(BF16))
    return rounded.astype(F32)


def local_general(tokens, routes, gate_code, gate_table, w_gate, w_up, w_down, norm_gain):
    own_rows = tokens[0]
    tok_count, feat_width = own_rows.shape
    experts = w_gate.shape[0] * lax.axis_size("expert")
    capacity = 5 * tok_count // (2 * experts)
    route_ids = routes[0].reshape(-1)
    onehot = (route_ids[:, None] == jnp.arange(experts, dtype=jnp.int32)[None, :]).astype(jnp.int32)
    slot_pos = jnp.sum((jnp.cumsum(onehot, axis=0) - onehot) * onehot, axis=1)
    position = route_ids * capacity + slot_pos
    owner_row = (
        jnp.zeros((experts * capacity,), jnp.int32)
        .at[position]
        .set(jnp.arange(2 * tok_count, dtype=jnp.int32) // 2)
    )
    filled = jnp.zeros((experts * capacity,), jnp.bool_).at[position].set(True)
    buffer = jnp.where(filled[:, None], own_rows[owner_row], jnp.zeros((), BF16))
    buffer = buffer.reshape(experts, capacity, feat_width)
    level_ids = gate_code[0].reshape(-1)
    received = lax.all_to_all(buffer, "expert", split_axis=0, concat_axis=0, tiled=True)
    expert_out = expert_ffn(received, w_gate, w_up, w_down)
    returned = lax.all_to_all(expert_out, "expert", split_axis=0, concat_axis=0, tiled=True)
    outputs = (
        returned.reshape(-1, feat_width)[position]
        .astype(F32)
        .reshape(tok_count, 2, feat_width)
    )
    weights = lookup(level_ids, gate_table).reshape(tok_count, 2)
    widened = combine_pairs(outputs, weights)
    inv_rms = lax.rsqrt(jnp.mean(widened * widened, axis=1, keepdims=True) + epsilon)
    normed = (widened * inv_rms * norm_gain[None, :]).astype(BF16)
    relaid = lax.all_to_all(normed, "dp", split_axis=1, concat_axis=0, tiled=True)
    return relaid[None]


def vmem():
    return pl.BlockSpec(memory_space=pltpu.VMEM)


def slot_rows(route_rows, experts, me):
    tok = route_rows.shape[1]
    ids = lax.broadcasted_iota(jnp.int32, (experts, tok), 0) ^ me
    named = (route_rows[0:1, :] == ids) | (route_rows[1:2, :] == ids)
    earlier = lax.broadcasted_iota(jnp.int32, (tok, tok), 0) < lax.broadcasted_iota(
        jnp.int32, (tok, tok), 1
    )
    count = jnp.dot(
        named.astype(F32).astype(BF16), earlier.astype(F32).astype(BF16),
        preferred_element_type=F32,
    )
    return jnp.where(named, count.astype(jnp.int32), -1), ids


def dispatch_body(experts, capacity, route_hbm, tok_hbm, *refs):
    *out_refs, route_ref, tok_ref, sems = refs
    copies = [
        pltpu.make_async_copy(route_hbm, route_ref, sems.at[0]),
        pltpu.make_async_copy(tok_hbm, tok_ref, sems.at[1]),
    ]
    for copy in copies:
        copy.start()
    me = lax.axis_index("expert")
    tok, width = tok_ref.shape
    lane = lax.broadcasted_iota(jnp.int32, (capacity, tok), 0)
    copies[0].wait()
    slots, _ = slot_rows(route_ref[...], experts, me)
    pick = jnp.concatenate(
        [(lane == slots[j : j + 1, :]).astype(F32) for j in range(experts)], axis=0
    ).astype(BF16)
    copies[1].wait()
    tile = 256
    for col in range(0, width, tile):
        rows = jnp.dot(pick, tok_ref[:, col : col + tile], preferred_element_type=F32)
        rows = rows.astype(BF16)
        for j in range(experts):
            out_refs[j][:, col : col + tile] = rows[j * capacity : (j + 1) * capacity, :]


def dispatch(route_rows, own_rows, experts, capacity):
    width = own_rows.shape[1]
    return pl.pallas_call(
        functools.partial(dispatch_body, experts, capacity),
        out_shape=[jax.ShapeDtypeStruct((capacity, width), BF16)] * experts,
        in_specs=[pl.BlockSpec(memory_space=pltpu.HBM)] * 2,
        out_specs=[vmem()] * experts,
        scratch_shapes=[
            pltpu.VMEM(route_rows.shape, jnp.int32),
            pltpu.VMEM(own_rows.shape, BF16),
            pltpu.SemaphoreType.DMA((2,)),
        ],
        name="dispatch",
        cost_estimate=pl.CostEstimate(flops=10**8, transcendentals=0, bytes_accessed=2 * 10**6),
        compiler_params=pltpu.CompilerParams(vmem_limit_bytes=16 * 2**20),
    )(route_rows, own_rows)


def selector_body(experts, capacity, route_ref, code_ref, table_ref, sel_ref, weight_ref):
    me = lax.axis_index("expert")
    rows = route_ref[...]
    slots, ids = slot_rows(rows, experts, me)
    tok = rows.shape[1]
    lane = lax.broadcasted_iota(jnp.int32, (capacity, tok), 0)
    for r in range(2):
        mine = jnp.where(rows[r : r + 1, :] == ids, slots, -1)
        pick = jnp.concatenate(
            [(lane == mine[j : j + 1, :]).astype(F32) for j in range(experts)], axis=0
        )
        sel_ref[r * tok : (r + 1) * tok, :] = pick.T.astype(BF16)
        codes = code_ref[r : r + 1, :]
        weights = jnp.zeros((1, tok), F32)
        for level in range(table_ref.shape[0]):
            weights = jnp.where(codes == level, table_ref[level], weights)
        weight_ref[r] = jnp.broadcast_to(weights, (tok, tok)).T


def selector(route_rows, code_rows, gate_table, experts, capacity):
    tok = route_rows.shape[1]
    return pl.pallas_call(
        functools.partial(selector_body, experts, capacity),
        out_shape=[
            jax.ShapeDtypeStruct((2 * tok, experts * capacity), BF16),
            jax.ShapeDtypeStruct((2, tok, tok), F32),
        ],
        in_specs=[vmem(), vmem(), pl.BlockSpec(memory_space=pltpu.SMEM)],
        out_specs=[vmem()] * 2,
        name="selector",
        cost_estimate=pl.CostEstimate(flops=2 * 10**10, transcendentals=0, bytes_accessed=10**8),
        compiler_params=pltpu.CompilerParams(vmem_limit_bytes=8 * 2**20),
    )(route_rows, code_rows, gate_table)


def chunk_columns(down_ref, offsets, chunk):
    me, tile = lax.axis_index("dp"), 256
    for q, offset in enumerate(offsets):
        for col in range(0, chunk, tile):
            start = pl.multiple_of((me ^ offset) * chunk + col, tile)
            at = q * chunk + col
            yield slice(at, at + tile), down_ref[:, pl.ds(start, tile)]


def write_down(hid_ref, down_ref, offsets, out_refs):
    capacity, width = out_refs[0].shape
    for cols, weight in chunk_columns(down_ref, offsets, width // len(offsets)):
        rows = jnp.dot(hid_ref[...], weight, preferred_element_type=F32).astype(BF16)
        for j, out in enumerate(out_refs):
            out[:, cols] = rows[j * capacity : (j + 1) * capacity, :]


def expert_body(count, pieces, *refs):
    blocks, (gate_ref, up_ref, down_ref) = refs[:count], refs[count : count + 3]
    hid_ref, x_ref, outs = refs[count + 3], refs[-1], refs[count + 4 : -1]
    capacity = blocks[0].shape[0]
    for j, block in enumerate(blocks):
        x_ref[j * capacity : (j + 1) * capacity, :] = block[...]
    hid = gate_ref.shape[0]
    tile = 256
    over = (((1,), (1,)), ((), ()))
    for low in range(0, hid, tile):
        high = min(hid, low + tile)
        gate = lax.dot_general(x_ref[...], gate_ref[low:high, :], over, preferred_element_type=F32)
        up = lax.dot_general(x_ref[...], up_ref[low:high, :], over, preferred_element_type=F32)
        hid_ref[:, low:high] = (gate / (1.0 + jnp.exp(-gate)) * up).astype(BF16)
    for p, offsets in enumerate(pieces):
        write_down(hid_ref, down_ref, offsets, outs[p * count : (p + 1) * count])


def expert_call(blocks, gate_rows, up_rows, down_rows, pieces, ways):
    count = len(blocks)
    capacity, width = blocks[0].shape
    rows, hid = capacity * count, gate_rows.shape[0]
    chunk = down_rows.shape[1] // ways
    shapes = [
        jax.ShapeDtypeStruct((capacity, chunk * len(offsets)), BF16)
        for offsets in pieces
        for _ in range(count)
    ]
    hidden, *outs = pl.pallas_call(
        functools.partial(expert_body, count, pieces),
        out_shape=[jax.ShapeDtypeStruct((rows, hid), BF16)] + shapes,
        in_specs=[vmem()] * (count + 3),
        out_specs=[vmem()] * (1 + len(shapes)),
        scratch_shapes=[pltpu.VMEM((rows, width), BF16)],
        cost_estimate=pl.CostEstimate(
            flops=5 * rows * hid * width, transcendentals=rows * hid, bytes_accessed=8 * 10**6
        ),
        compiler_params=pltpu.CompilerParams(vmem_limit_bytes=24 * 2**20),
    )(*blocks, gate_rows, up_rows, down_rows)
    return hidden, [outs[p * count : (p + 1) * count] for p in range(len(pieces))]


def down_body(offsets, hid_ref, down_ref, *out_refs):
    write_down(hid_ref, down_ref, offsets, out_refs)


def down_call(hidden, down_rows, count, offsets, ways):
    rows, hid = hidden.shape
    width = down_rows.shape[1] // ways * len(offsets)
    return pl.pallas_call(
        functools.partial(down_body, offsets),
        out_shape=[jax.ShapeDtypeStruct((rows // count, width), BF16)] * count,
        in_specs=[vmem()] * 2,
        out_specs=[vmem()] * count,
        cost_estimate=pl.CostEstimate(
            flops=2 * rows * hid * width, transcendentals=0, bytes_accessed=3 * 10**6
        ),
        compiler_params=pltpu.CompilerParams(vmem_limit_bytes=16 * 2**20),
    )(hidden, down_rows)


def gather_blocks(blocks, y_ref, low):
    capacity, width = blocks[0].shape[0], y_ref.shape[1]
    for j, block in enumerate(blocks):
        start = low if block.shape[1] > width else 0
        y_ref[j * capacity : (j + 1) * capacity, :] = block[:, start : start + width]


def combine_chunk(sel_ref, weight_ref, y_ref, low, out_ref, squares):
    tok, lanes = squares.shape
    chunk, tile = out_ref.shape[1], 256
    for col in range(0, chunk, tile):
        picked = jnp.dot(
            sel_ref[...], y_ref[:, low + col : low + col + tile], preferred_element_type=F32
        )
        for at in range(0, tile, lanes):
            first = picked[:tok, at : at + lanes] * weight_ref[0]
            second = picked[tok:, at : at + lanes] * weight_ref[1]
            rounded = (first + second).astype(BF16)
            out_ref[:, col + at : col + at + lanes] = rounded
            wide = rounded.astype(F32)
            squares = squares + wide * wide
    return squares


def early_body(count, sel_ref, weight_ref, *refs):
    blocks, (out_ref, sum_ref, y_ref) = refs[:count], refs[count:]
    gather_blocks(blocks, y_ref, 0)
    squares = jnp.zeros(sum_ref.shape, F32)
    sum_ref[...] = combine_chunk(sel_ref, weight_ref, y_ref, 0, out_ref, squares)


def combine_early(select, weights, blocks, width):
    rows, tok = blocks[0].shape[0] * len(blocks), weights.shape[1]
    return pl.pallas_call(
        functools.partial(early_body, len(blocks)),
        out_shape=[
            jax.ShapeDtypeStruct((tok, width), BF16),
            jax.ShapeDtypeStruct((tok, weights.shape[2]), F32),
        ],
        in_specs=[vmem()] * (2 + len(blocks)),
        out_specs=[vmem()] * 2,
        scratch_shapes=[pltpu.VMEM((rows, width), BF16)],
        name="combine_early",
        cost_estimate=pl.CostEstimate(
            flops=4 * tok * rows * width, transcendentals=0, bytes_accessed=10**6
        ),
        compiler_params=pltpu.CompilerParams(vmem_limit_bytes=12 * 2**20),
    )(select, weights, *blocks)


def late_body(count, feat_width, sel_ref, weight_ref, part_ref, gain_ref, *refs):
    blocks, y_ref, outs, sum_ref = refs[:count], refs[-1], refs[count:-2], refs[-2]
    chunk = outs[0].shape[1]
    gather_blocks(blocks, y_ref, feat_width - chunk * len(outs))
    squares = part_ref[...]
    for q, out in enumerate(outs):
        squares = combine_chunk(sel_ref, weight_ref, y_ref, q * chunk, out, squares)
    total = jnp.sum(squares, axis=1, keepdims=True)
    tok = total.shape[0]
    sum_ref[...] = jnp.broadcast_to(total, (tok, tok)).T[0:8, :]
    inv = lax.rsqrt(total * (1.0 / feat_width) + epsilon)
    for q, out in enumerate(outs):
        gain = gain_ref[0:1, q * chunk : (q + 1) * chunk]
        out[...] = (out[...].astype(F32) * inv * gain).astype(BF16)


def combine_late(select, weights, part, gain, blocks, chunk, feat_width):
    width = gain.shape[1]
    rows, tok = blocks[0].shape[0] * len(blocks), weights.shape[1]
    return pl.pallas_call(
        functools.partial(late_body, len(blocks), feat_width),
        out_shape=[jax.ShapeDtypeStruct((tok, chunk), BF16)] * (width // chunk)
        + [jax.ShapeDtypeStruct((8, tok), F32)],
        in_specs=[vmem()] * (4 + len(blocks)),
        out_specs=[vmem()] * (width // chunk + 1),
        scratch_shapes=[pltpu.VMEM((rows, width), BF16)],
        name="combine_late",
        cost_estimate=pl.CostEstimate(
            flops=4 * tok * rows * width, transcendentals=0, bytes_accessed=2 * 10**6
        ),
        compiler_params=pltpu.CompilerParams(vmem_limit_bytes=12 * 2**20),
    )(select, weights, part, gain, *blocks)


def gain_body(offsets, gain_ref, out_ref):
    chunk = out_ref.shape[1] // len(offsets)
    me = lax.axis_index("dp")
    for q, offset in enumerate(offsets):
        start = pl.multiple_of((me ^ offset) * chunk, 128)
        row = gain_ref[:, pl.ds(start, chunk)]
        out_ref[:, q * chunk : (q + 1) * chunk] = jnp.broadcast_to(row, (8, chunk))


def gain_of(norm_gain, offsets, chunk):
    return pl.pallas_call(
        functools.partial(gain_body, offsets),
        out_shape=jax.ShapeDtypeStruct((8, chunk * len(offsets)), F32),
        in_specs=[vmem()],
        out_specs=vmem(),
        cost_estimate=pl.CostEstimate(flops=10**4, transcendentals=0, bytes_accessed=10**4),
        compiler_params=pltpu.CompilerParams(vmem_limit_bytes=2**20),
    )(norm_gain[None, :])


def finish_body(feat_width, ready, raw, *refs):
    ways = len(ready) + len(raw)
    chunks, sums = refs[:ways], refs[ways : ways + len(raw)]
    gain_ref, out_ref, scratch, sems = refs[ways + len(raw) :]
    me = lax.axis_index("dp")
    tok = chunks[0].shape[0]

    def put(source, k):
        rows = pl.ds(pl.multiple_of((me ^ k) * tok, tok), tok)
        copy = pltpu.make_async_copy(source, out_ref.at[rows, :], sems.at[k])
        copy.start()
        return copy

    copies = [put(chunks[i], k) for i, k in enumerate(ready)]
    for i, k in enumerate(raw):
        inv = lax.rsqrt(sums[i][0:1, :] * (1.0 / feat_width) + epsilon)
        column = jnp.broadcast_to(inv, (tok, tok)).T[:, 0:1]
        value = chunks[len(ready) + i][...].astype(F32) * column * gain_ref[0:1, :]
        scratch[i] = value.astype(BF16)
        copies.append(put(scratch.at[i], k))
    for copy in copies:
        copy.wait()


def finish(ready, raw, sums, gain, feat_width):
    first = next(iter(ready.values()))
    tok, width = first.shape
    ways = len(ready) + len(raw)
    return pl.pallas_call(
        functools.partial(finish_body, feat_width, tuple(ready), tuple(raw)),
        out_shape=jax.ShapeDtypeStruct((tok * ways, width), BF16),
        in_specs=[vmem()] * (ways + len(raw) + 1),
        out_specs=pl.BlockSpec(memory_space=pltpu.HBM),
        scratch_shapes=[
            pltpu.VMEM((len(raw), tok, width), BF16),
            pltpu.SemaphoreType.DMA((ways,)),
        ],
        name="finish",
        cost_estimate=pl.CostEstimate(flops=10**6, transcendentals=0, bytes_accessed=10**6),
        compiler_params=pltpu.CompilerParams(vmem_limit_bytes=8 * 2**20),
    )(*ready.values(), *raw.values(), *[sums[k] for k in raw], gain)


def swap(value, axis, offset):
    size = lax.axis_size(axis)
    return lax.ppermute(value, axis, [(i, i ^ offset) for i in range(size)])


def swap_each(values, axis):
    moved = {}
    for k, value in values.items():
        moved[k] = swap(value, axis, k) if k else value
    return moved


def local_fast(tokens, routes, gate_code, gate_table, w_gate, w_up, w_down, norm_gain):
    return fast_steps(tokens, routes, gate_code, gate_table, w_gate, w_up, w_down, norm_gain)


def fast_steps(tokens, routes, gate_code, gate_table, w_gate, w_up, w_down, norm_gain):
    own_rows = tokens[0]
    tok, feat_width = own_rows.shape
    experts = lax.axis_size("expert")
    ways = lax.axis_size("dp")
    capacity = 5 * tok // (2 * experts)
    chunk = feat_width // ways
    links = [bin(k >> 1).count("1") for k in range(experts)]
    close = [k for k in range(2, experts) if links[k] == 1] + [1, 0]
    away = [k for k in range(experts) if links[k] == 2]
    early = (ways // 2,)
    late = tuple(k for k in range(ways - 1, -1, -1) if k not in early)

    route_rows = routes[0].T
    blocks = dispatch(
        pltpu.with_memory_space_constraint(route_rows, pltpu.HBM),
        pltpu.with_memory_space_constraint(own_rows, pltpu.HBM),
        experts, capacity,
    )
    near = swap_each({k: blocks[k] for k in close}, "expert")
    far = swap_each({k: blocks[k] for k in away}, "expert")
    select, weights = selector(route_rows, gate_code[0].T, gate_table, experts, capacity)
    matrices = w_gate[0].T, w_up[0].T, w_down[0]

    _, (outputs,) = expert_call([near[k] for k in close], *matrices, (early + late,), ways)
    back = swap_each(dict(zip(close, outputs)), "expert")
    gain_own = gain_of(norm_gain, (0,), chunk)
    hidden, (away_early,) = expert_call([far[k] for k in away], *matrices, (early,), ways)
    got_early = back | swap_each(dict(zip(away, away_early)), "expert")
    away_late = down_call(hidden, matrices[2], len(away), late, ways)
    got_late = back | swap_each(dict(zip(away, away_late)), "expert")

    order = range(experts)
    first, part = combine_early(
        select, weights, [got_early[k] for k in order], chunk
    )
    raw = swap_each({early[0]: first}, "dp")
    gain_late = gain_of(norm_gain, late, chunk)
    *rest, total = combine_late(
        select, weights, part, gain_late, [got_late[k] for k in order], chunk, feat_width
    )
    ready = swap_each(dict(zip(late, rest)), "dp")
    sums = swap_each({k: total for k in early}, "dp")
    return finish(ready, raw, sums, gain_own, feat_width)[None]


def solution(mesh):
    in_specs = (
        P("expert", "dp", None),
        P("expert", "dp", None),
        P("expert", "dp", None),
        P(),
        P("expert", None, None),
        P("expert", None, None),
        P("expert", None, None),
        P(),
    )
    out_specs = P("expert", None, "dp")

    def whole(tokens, routes, gate_code, gate_table, w_gate, w_up, w_down, norm_gain):
        args = (tokens, routes, gate_code, gate_table, w_gate, w_up, w_down, norm_gain)
        experts, ways = mesh.shape["expert"], mesh.shape["dp"]
        tok, feat = tokens.shape[1] // ways, tokens.shape[2]
        power = experts & (experts - 1) == 0 and ways & (ways - 1) == 0
        fits = power and experts == 8 and 2 <= ways <= 4
        fits = fits and tok % 128 == 0 and w_gate.shape[0] == experts
        fits = fits and 5 * tok % (16 * experts) == 0 and feat % (256 * ways) == 0
        body = local_fast if fits else local_general
        f = jax.shard_map(body, mesh=mesh, in_specs=in_specs, out_specs=out_specs, check_vma=False)
        return f(*args)

    return whole
```

```python
import functools

import jax
import jax.numpy as jnp
from jax import lax
from jax.experimental import pallas as pl
from jax.experimental.pallas import tpu as pltpu
from jax.sharding import PartitionSpec as P


epsilon = 1e-06


F32 = jnp.float32
BF16 = jnp.bfloat16


def expert_ffn(slot_block, w_gate, w_up, w_down):
    shape_in = slot_block.shape
    flat_rows = slot_block.reshape(-1, shape_in[-1])
    gate_act = jnp.dot(flat_rows, w_gate[0], preferred_element_type=F32)
    up_act = jnp.dot(flat_rows, w_up[0], preferred_element_type=F32)
    hidden = (jax.nn.silu(gate_act) * up_act).astype(BF16)
    result = jnp.dot(hidden, w_down[0], preferred_element_type=F32).astype(BF16)
    return result.reshape(shape_in)


def lookup(codes, gate_table):
    levels = gate_table.shape[0]
    match = codes[:, None] == jnp.arange(levels, dtype=jnp.int32)[None, :]
    return jnp.sum(jnp.where(match, gate_table[None, :], 0.0), axis=1)


def combine_pairs(outputs, weights):
    combined = outputs[:, 0] * weights[:, 0:1] + outputs[:, 1] * weights[:, 1:2]
    rounded = lax.optimization_barrier(combined.astype(BF16))
    return rounded.astype(F32)


def local_general(tokens, routes, gate_code, gate_table, w_gate, w_up, w_down, norm_gain):
    own_rows = tokens[0]
    tok_count, feat_width = own_rows.shape
    experts = w_gate.shape[0] * lax.axis_size("expert")
    capacity = 5 * tok_count // (2 * experts)
    route_ids = routes[0].reshape(-1)
    onehot = (route_ids[:, None] == jnp.arange(experts, dtype=jnp.int32)[None, :]).astype(jnp.int32)
    slot_pos = jnp.sum((jnp.cumsum(onehot, axis=0) - onehot) * onehot, axis=1)
    position = route_ids * capacity + slot_pos
    owner_row = (
        jnp.zeros((experts * capacity,), jnp.int32)
        .at[position]
        .set(jnp.arange(2 * tok_count, dtype=jnp.int32) // 2)
    )
    filled = jnp.zeros((experts * capacity,), jnp.bool_).at[position].set(True)
    buffer = jnp.where(filled[:, None], own_rows[owner_row], jnp.zeros((), BF16))
    buffer = buffer.reshape(experts, capacity, feat_width)
    level_ids = gate_code[0].reshape(-1)
    received = lax.all_to_all(buffer, "expert", split_axis=0, concat_axis=0, tiled=True)
    expert_out = expert_ffn(received, w_gate, w_up, w_down)
    returned = lax.all_to_all(expert_out, "expert", split_axis=0, concat_axis=0, tiled=True)
    outputs = (
        returned.reshape(-1, feat_width)[position]
        .astype(F32)
        .reshape(tok_count, 2, feat_width)
    )
    weights = lookup(level_ids, gate_table).reshape(tok_count, 2)
    widened = combine_pairs(outputs, weights)
    inv_rms = lax.rsqrt(jnp.mean(widened * widened, axis=1, keepdims=True) + epsilon)
    normed = (widened * inv_rms * norm_gain[None, :]).astype(BF16)
    relaid = lax.all_to_all(normed, "dp", split_axis=1, concat_axis=0, tiled=True)
    return relaid[None]


def vmem():
    return pl.BlockSpec(memory_space=pltpu.VMEM)


def slot_rows(route_rows, experts, me):
    tok = route_rows.shape[1]
    ids = lax.broadcasted_iota(jnp.int32, (experts, tok), 0) ^ me
    named = (route_rows[0:1, :] == ids) | (route_rows[1:2, :] == ids)
    earlier = lax.broadcasted_iota(jnp.int32, (tok, tok), 0) < lax.broadcasted_iota(
        jnp.int32, (tok, tok), 1
    )
    count = jnp.dot(
        named.astype(F32).astype(BF16), earlier.astype(F32).astype(BF16),
        preferred_element_type=F32,
    )
    return jnp.where(named, count.astype(jnp.int32), -1), ids


def dispatch_body(experts, capacity, route_hbm, tok_hbm, *refs):
    *out_refs, route_ref, tok_ref, sems = refs
    copies = [
        pltpu.make_async_copy(route_hbm, route_ref, sems.at[0]),
        pltpu.make_async_copy(tok_hbm, tok_ref, sems.at[1]),
    ]
    for copy in copies:
        copy.start()
    me = lax.axis_index("expert")
    tok, width = tok_ref.shape
    lane = lax.broadcasted_iota(jnp.int32, (capacity, tok), 0)
    copies[0].wait()
    slots, _ = slot_rows(route_ref[...], experts, me)
    pick = jnp.concatenate(
        [(lane == slots[j : j + 1, :]).astype(F32) for j in range(experts)], axis=0
    ).astype(BF16)
    copies[1].wait()
    tile = 256
    for col in range(0, width, tile):
        rows = jnp.dot(pick, tok_ref[:, col : col + tile], preferred_element_type=F32)
        rows = rows.astype(BF16)
        for j in range(experts):
            out_refs[j][:, col : col + tile] = rows[j * capacity : (j + 1) * capacity, :]


def dispatch(route_rows, own_rows, experts, capacity):
    width = own_rows.shape[1]
    return pl.pallas_call(
        functools.partial(dispatch_body, experts, capacity),
        out_shape=[jax.ShapeDtypeStruct((capacity, width), BF16)] * experts,
        in_specs=[pl.BlockSpec(memory_space=pltpu.HBM)] * 2,
        out_specs=[vmem()] * experts,
        scratch_shapes=[
            pltpu.VMEM(route_rows.shape, jnp.int32),
            pltpu.VMEM(own_rows.shape, BF16),
            pltpu.SemaphoreType.DMA((2,)),
        ],
        name="dispatch",
        cost_estimate=pl.CostEstimate(flops=10**8, transcendentals=0, bytes_accessed=2 * 10**6),
        compiler_params=pltpu.CompilerParams(vmem_limit_bytes=16 * 2**20),
    )(route_rows, own_rows)


def selector_body(experts, capacity, route_ref, code_ref, table_ref, sel_ref, weight_ref):
    me = lax.axis_index("expert")
    rows = route_ref[...]
    slots, ids = slot_rows(rows, experts, me)
    tok = rows.shape[1]
    lane = lax.broadcasted_iota(jnp.int32, (capacity, tok), 0)
    for r in range(2):
        mine = jnp.where(rows[r : r + 1, :] == ids, slots, -1)
        pick = jnp.concatenate(
            [(lane == mine[j : j + 1, :]).astype(F32) for j in range(experts)], axis=0
        )
        sel_ref[r * tok : (r + 1) * tok, :] = pick.T.astype(BF16)
        codes = code_ref[r : r + 1, :]
        weights = jnp.zeros((1, tok), F32)
        for level in range(table_ref.shape[0]):
            weights = jnp.where(codes == level, table_ref[level], weights)
        weight_ref[r] = jnp.broadcast_to(weights, (tok, tok)).T


def selector(route_rows, code_rows, gate_table, experts, capacity):
    tok = route_rows.shape[1]
    return pl.pallas_call(
        functools.partial(selector_body, experts, capacity),
        out_shape=[
            jax.ShapeDtypeStruct((2 * tok, experts * capacity), BF16),
            jax.ShapeDtypeStruct((2, tok, tok), F32),
        ],
        in_specs=[vmem(), vmem(), pl.BlockSpec(memory_space=pltpu.SMEM)],
        out_specs=[vmem()] * 2,
        name="selector",
        cost_estimate=pl.CostEstimate(flops=2 * 10**10, transcendentals=0, bytes_accessed=10**8),
        compiler_params=pltpu.CompilerParams(vmem_limit_bytes=8 * 2**20),
    )(route_rows, code_rows, gate_table)


def chunk_columns(down_ref, offsets, chunk):
    me, tile = lax.axis_index("dp"), 256
    for q, offset in enumerate(offsets):
        for col in range(0, chunk, tile):
            start = pl.multiple_of((me ^ offset) * chunk + col, tile)
            at = q * chunk + col
            yield slice(at, at + tile), down_ref[:, pl.ds(start, tile)]


def write_down(hid_ref, down_ref, offsets, out_refs):
    capacity, width = out_refs[0].shape
    for cols, weight in chunk_columns(down_ref, offsets, width // len(offsets)):
        rows = jnp.dot(hid_ref[...], weight, preferred_element_type=F32).astype(BF16)
        for j, out in enumerate(out_refs):
            out[:, cols] = rows[j * capacity : (j + 1) * capacity, :]


def expert_body(count, pieces, *refs):
    blocks, (gate_ref, up_ref, down_ref) = refs[:count], refs[count : count + 3]
    hid_ref, x_ref, outs = refs[count + 3], refs[-1], refs[count + 4 : -1]
    capacity = blocks[0].shape[0]
    for j, block in enumerate(blocks):
        x_ref[j * capacity : (j + 1) * capacity, :] = block[...]
    hid = gate_ref.shape[0]
    tile = 256
    over = (((1,), (1,)), ((), ()))
    for low in range(0, hid, tile):
        high = min(hid, low + tile)
        gate = lax.dot_general(x_ref[...], gate_ref[low:high, :], over, preferred_element_type=F32)
        up = lax.dot_general(x_ref[...], up_ref[low:high, :], over, preferred_element_type=F32)
        hid_ref[:, low:high] = (gate / (1.0 + jnp.exp(-gate)) * up).astype(BF16)
    for p, offsets in enumerate(pieces):
        write_down(hid_ref, down_ref, offsets, outs[p * count : (p + 1) * count])


def expert_call(blocks, gate_rows, up_rows, down_rows, pieces, ways):
    count = len(blocks)
    capacity, width = blocks[0].shape
    rows, hid = capacity * count, gate_rows.shape[0]
    chunk = down_rows.shape[1] // ways
    shapes = [
        jax.ShapeDtypeStruct((capacity, chunk * len(offsets)), BF16)
        for offsets in pieces
        for _ in range(count)
    ]
    hidden, *outs = pl.pallas_call(
        functools.partial(expert_body, count, pieces),
        out_shape=[jax.ShapeDtypeStruct((rows, hid), BF16)] + shapes,
        in_specs=[vmem()] * (count + 3),
        out_specs=[vmem()] * (1 + len(shapes)),
        scratch_shapes=[pltpu.VMEM((rows, width), BF16)],
        cost_estimate=pl.CostEstimate(
            flops=5 * rows * hid * width, transcendentals=rows * hid, bytes_accessed=8 * 10**6
        ),
        compiler_params=pltpu.CompilerParams(vmem_limit_bytes=24 * 2**20),
    )(*blocks, gate_rows, up_rows, down_rows)
    return hidden, [outs[p * count : (p + 1) * count] for p in range(len(pieces))]


def down_body(offsets, hid_ref, down_ref, *out_refs):
    write_down(hid_ref, down_ref, offsets, out_refs)


def down_call(hidden, down_rows, count, offsets, ways):
    rows, hid = hidden.shape
    width = down_rows.shape[1] // ways * len(offsets)
    return pl.pallas_call(
        functools.partial(down_body, offsets),
        out_shape=[jax.ShapeDtypeStruct((rows // count, width), BF16)] * count,
        in_specs=[vmem()] * 2,
        out_specs=[vmem()] * count,
        cost_estimate=pl.CostEstimate(
            flops=2 * rows * hid * width, transcendentals=0, bytes_accessed=3 * 10**6
        ),
        compiler_params=pltpu.CompilerParams(vmem_limit_bytes=16 * 2**20),
    )(hidden, down_rows)


def gather_blocks(blocks, y_ref, low):
    capacity, width = blocks[0].shape[0], y_ref.shape[1]
    for j, block in enumerate(blocks):
        start = low if block.shape[1] > width else 0
        y_ref[j * capacity : (j + 1) * capacity, :] = block[:, start : start + width]


def combine_chunk(sel_ref, weight_ref, y_ref, low, out_ref, squares):
    tok, lanes = squares.shape
    chunk, tile = out_ref.shape[1], 256
    for col in range(0, chunk, tile):
        picked = jnp.dot(
            sel_ref[...], y_ref[:, low + col : low + col + tile], preferred_element_type=F32
        )
        for at in range(0, tile, lanes):
            first = picked[:tok, at : at + lanes] * weight_ref[0]
            second = picked[tok:, at : at + lanes] * weight_ref[1]
            rounded = (first + second).astype(BF16)
            out_ref[:, col + at : col + at + lanes] = rounded
            wide = rounded.astype(F32)
            squares = squares + wide * wide
    return squares


def early_body(count, sel_ref, weight_ref, *refs):
    blocks, (out_ref, sum_ref, y_ref) = refs[:count], refs[count:]
    gather_blocks(blocks, y_ref, 0)
    squares = jnp.zeros(sum_ref.shape, F32)
    sum_ref[...] = combine_chunk(sel_ref, weight_ref, y_ref, 0, out_ref, squares)


def combine_early(select, weights, blocks, width):
    rows, tok = blocks[0].shape[0] * len(blocks), weights.shape[1]
    return pl.pallas_call(
        functools.partial(early_body, len(blocks)),
        out_shape=[
            jax.ShapeDtypeStruct((tok, width), BF16),
            jax.ShapeDtypeStruct((tok, weights.shape[2]), F32),
        ],
        in_specs=[vmem()] * (2 + len(blocks)),
        out_specs=[vmem()] * 2,
        scratch_shapes=[pltpu.VMEM((rows, width), BF16)],
        name="combine_early",
        cost_estimate=pl.CostEstimate(
            flops=4 * tok * rows * width, transcendentals=0, bytes_accessed=10**6
        ),
        compiler_params=pltpu.CompilerParams(vmem_limit_bytes=12 * 2**20),
    )(select, weights, *blocks)


def late_body(count, feat_width, sel_ref, weight_ref, part_ref, gain_ref, *refs):
    blocks, y_ref, outs, sum_ref = refs[:count], refs[-1], refs[count:-2], refs[-2]
    chunk = outs[0].shape[1]
    gather_blocks(blocks, y_ref, feat_width - chunk * len(outs))
    squares = part_ref[...]
    for q, out in enumerate(outs):
        squares = combine_chunk(sel_ref, weight_ref, y_ref, q * chunk, out, squares)
    total = jnp.sum(squares, axis=1, keepdims=True)
    tok = total.shape[0]
    sum_ref[...] = jnp.broadcast_to(total, (tok, tok)).T[0:8, :]
    inv = lax.rsqrt(total * (1.0 / feat_width) + epsilon)
    for q, out in enumerate(outs):
        gain = gain_ref[0:1, q * chunk : (q + 1) * chunk]
        out[...] = (out[...].astype(F32) * inv * gain).astype(BF16)


def combine_late(select, weights, part, gain, blocks, chunk, feat_width):
    width = gain.shape[1]
    rows, tok = blocks[0].shape[0] * len(blocks), weights.shape[1]
    return pl.pallas_call(
        functools.partial(late_body, len(blocks), feat_width),
        out_shape=[jax.ShapeDtypeStruct((tok, chunk), BF16)] * (width // chunk)
        + [jax.ShapeDtypeStruct((8, tok), F32)],
        in_specs=[vmem()] * (4 + len(blocks)),
        out_specs=[vmem()] * (width // chunk + 1),
        scratch_shapes=[pltpu.VMEM((rows, width), BF16)],
        name="combine_late",
        cost_estimate=pl.CostEstimate(
            flops=4 * tok * rows * width, transcendentals=0, bytes_accessed=2 * 10**6
        ),
        compiler_params=pltpu.CompilerParams(vmem_limit_bytes=12 * 2**20),
    )(select, weights, part, gain, *blocks)


def gain_body(offsets, gain_ref, out_ref):
    chunk = out_ref.shape[1] // len(offsets)
    me = lax.axis_index("dp")
    for q, offset in enumerate(offsets):
        start = pl.multiple_of((me ^ offset) * chunk, 128)
        row = gain_ref[:, pl.ds(start, chunk)]
        out_ref[:, q * chunk : (q + 1) * chunk] = jnp.broadcast_to(row, (8, chunk))


def gain_of(norm_gain, offsets, chunk):
    return pl.pallas_call(
        functools.partial(gain_body, offsets),
        out_shape=jax.ShapeDtypeStruct((8, chunk * len(offsets)), F32),
        in_specs=[vmem()],
        out_specs=vmem(),
        cost_estimate=pl.CostEstimate(flops=10**4, transcendentals=0, bytes_accessed=10**4),
        compiler_params=pltpu.CompilerParams(vmem_limit_bytes=2**20),
    )(norm_gain[None, :])


def finish_body(feat_width, ready, raw, *refs):
    ways = len(ready) + len(raw)
    chunks, sums = refs[:ways], refs[ways : ways + len(raw)]
    gain_ref, out_ref, scratch, sems = refs[ways + len(raw) :]
    me = lax.axis_index("dp")
    tok = chunks[0].shape[0]

    def put(source, k):
        rows = pl.ds(pl.multiple_of((me ^ k) * tok, tok), tok)
        copy = pltpu.make_async_copy(source, out_ref.at[rows, :], sems.at[k])
        copy.start()
        return copy

    copies = [put(chunks[i], k) for i, k in enumerate(ready)]
    for i, k in enumerate(raw):
        inv = lax.rsqrt(sums[i][0:1, :] * (1.0 / feat_width) + epsilon)
        column = jnp.broadcast_to(inv, (tok, tok)).T[:, 0:1]
        value = chunks[len(ready) + i][...].astype(F32) * column * gain_ref[0:1, :]
        scratch[i] = value.astype(BF16)
        copies.append(put(scratch.at[i], k))
    for copy in copies:
        copy.wait()


def finish(ready, raw, sums, gain, feat_width):
    first = next(iter(ready.values()))
    tok, width = first.shape
    ways = len(ready) + len(raw)
    return pl.pallas_call(
        functools.partial(finish_body, feat_width, tuple(ready), tuple(raw)),
        out_shape=jax.ShapeDtypeStruct((tok * ways, width), BF16),
        in_specs=[vmem()] * (ways + len(raw) + 1),
        out_specs=pl.BlockSpec(memory_space=pltpu.HBM),
        scratch_shapes=[
            pltpu.VMEM((len(raw), tok, width), BF16),
            pltpu.SemaphoreType.DMA((ways,)),
        ],
        name="finish",
        cost_estimate=pl.CostEstimate(flops=10**6, transcendentals=0, bytes_accessed=10**6),
        compiler_params=pltpu.CompilerParams(vmem_limit_bytes=8 * 2**20),
    )(*ready.values(), *raw.values(), *[sums[k] for k in raw], gain)


def swap(value, axis, offset):
    size = lax.axis_size(axis)
    return lax.ppermute(value, axis, [(i, i ^ offset) for i in range(size)])


def swap_each(values, axis):
    moved = {}
    for k, value in values.items():
        moved[k] = swap(value, axis, k) if k else value
    return moved


def local_fast(tokens, routes, gate_code, gate_table, w_gate, w_up, w_down, norm_gain):
    return fast_steps(tokens, routes, gate_code, gate_table, w_gate, w_up, w_down, norm_gain)


def fast_steps(tokens, routes, gate_code, gate_table, w_gate, w_up, w_down, norm_gain):
    own_rows = tokens[0]
    tok, feat_width = own_rows.shape
    experts = lax.axis_size("expert")
    ways = lax.axis_size("dp")
    capacity = 5 * tok // (2 * experts)
    chunk = feat_width // ways
    close = [4, 5, 2, 3, 1, 0]
    away = [6, 7]
    early = (ways // 2,)
    late = tuple(k for k in range(ways - 1, -1, -1) if k not in early)

    route_rows = routes[0].T
    blocks = dispatch(
        pltpu.with_memory_space_constraint(route_rows, pltpu.HBM),
        pltpu.with_memory_space_constraint(own_rows, pltpu.HBM),
        experts, capacity,
    )
    near = swap_each({k: blocks[k] for k in close}, "expert")
    far = swap_each({k: blocks[k] for k in away}, "expert")
    select, weights = selector(route_rows, gate_code[0].T, gate_table, experts, capacity)
    matrices = w_gate[0].T, w_up[0].T, w_down[0]

    _, (outputs,) = expert_call([near[k] for k in close], *matrices, (early + late,), ways)
    back = swap_each(dict(zip(close, outputs)), "expert")
    gain_own = gain_of(norm_gain, (0,), chunk)
    hidden, (away_early,) = expert_call([far[k] for k in away], *matrices, (early,), ways)
    got_early = back | swap_each(dict(zip(away, away_early)), "expert")
    away_late = down_call(hidden, matrices[2], len(away), late, ways)
    got_late = back | swap_each(dict(zip(away, away_late)), "expert")

    order = range(experts)
    first, part = combine_early(
        select, weights, [got_early[k] for k in order], chunk
    )
    raw = swap_each({early[0]: first}, "dp")
    gain_late = gain_of(norm_gain, late, chunk)
    *rest, total = combine_late(
        select, weights, part, gain_late, [got_late[k] for k in order], chunk, feat_width
    )
    ready = swap_each(dict(zip(late, rest)), "dp")
    sums = swap_each({k: total for k in early}, "dp")
    return finish(ready, raw, sums, gain_own, feat_width)[None]


def solution(mesh):
    in_specs = (
        P("expert", "dp", None),
        P("expert", "dp", None),
        P("expert", "dp", None),
        P(),
        P("expert", None, None),
        P("expert", None, None),
        P("expert", None, None),
        P(),
    )
    out_specs = P("expert", None, "dp")

    def whole(tokens, routes, gate_code, gate_table, w_gate, w_up, w_down, norm_gain):
        args = (tokens, routes, gate_code, gate_table, w_gate, w_up, w_down, norm_gain)
        experts, ways = mesh.shape["expert"], mesh.shape["dp"]
        tok, feat = tokens.shape[1] // ways, tokens.shape[2]
        power = experts & (experts - 1) == 0 and ways & (ways - 1) == 0
        fits = power and experts == 8 and 2 <= ways <= 4
        fits = fits and tok % 128 == 0 and w_gate.shape[0] == experts
        fits = fits and 5 * tok % (16 * experts) == 0 and feat % (256 * ways) == 0
        body = local_fast if fits else local_general
        f = jax.shard_map(body, mesh=mesh, in_specs=in_specs, out_specs=out_specs, check_vma=False)
        return f(*args)

    return whole
```

```python
import functools

import jax
import jax.numpy as jnp
from jax import lax
from jax.experimental import pallas as pl
from jax.experimental.pallas import tpu as pltpu
from jax.sharding import PartitionSpec as P


epsilon = 1e-06


F32 = jnp.float32
BF16 = jnp.bfloat16


def expert_ffn(slot_block, w_gate, w_up, w_down):
    shape_in = slot_block.shape
    flat_rows = slot_block.reshape(-1, shape_in[-1])
    gate_act = jnp.dot(flat_rows, w_gate[0], preferred_element_type=F32)
    up_act = jnp.dot(flat_rows, w_up[0], preferred_element_type=F32)
    hidden = (jax.nn.silu(gate_act) * up_act).astype(BF16)
    result = jnp.dot(hidden, w_down[0], preferred_element_type=F32).astype(BF16)
    return result.reshape(shape_in)


def lookup(codes, gate_table):
    levels = gate_table.shape[0]
    match = codes[:, None] == jnp.arange(levels, dtype=jnp.int32)[None, :]
    return jnp.sum(jnp.where(match, gate_table[None, :], 0.0), axis=1)


def combine_pairs(outputs, weights):
    combined = outputs[:, 0] * weights[:, 0:1] + outputs[:, 1] * weights[:, 1:2]
    rounded = lax.optimization_barrier(combined.astype(BF16))
    return rounded.astype(F32)


def local_general(tokens, routes, gate_code, gate_table, w_gate, w_up, w_down, norm_gain):
    own_rows = tokens[0]
    tok_count, feat_width = own_rows.shape
    experts = w_gate.shape[0] * lax.axis_size("expert")
    capacity = 5 * tok_count // (2 * experts)
    route_ids = routes[0].reshape(-1)
    onehot = (route_ids[:, None] == jnp.arange(experts, dtype=jnp.int32)[None, :]).astype(jnp.int32)
    slot_pos = jnp.sum((jnp.cumsum(onehot, axis=0) - onehot) * onehot, axis=1)
    position = route_ids * capacity + slot_pos
    owner_row = (
        jnp.zeros((experts * capacity,), jnp.int32)
        .at[position]
        .set(jnp.arange(2 * tok_count, dtype=jnp.int32) // 2)
    )
    filled = jnp.zeros((experts * capacity,), jnp.bool_).at[position].set(True)
    buffer = jnp.where(filled[:, None], own_rows[owner_row], jnp.zeros((), BF16))
    buffer = buffer.reshape(experts, capacity, feat_width)
    level_ids = gate_code[0].reshape(-1)
    received = lax.all_to_all(buffer, "expert", split_axis=0, concat_axis=0, tiled=True)
    expert_out = expert_ffn(received, w_gate, w_up, w_down)
    returned = lax.all_to_all(expert_out, "expert", split_axis=0, concat_axis=0, tiled=True)
    outputs = (
        returned.reshape(-1, feat_width)[position]
        .astype(F32)
        .reshape(tok_count, 2, feat_width)
    )
    weights = lookup(level_ids, gate_table).reshape(tok_count, 2)
    widened = combine_pairs(outputs, weights)
    inv_rms = lax.rsqrt(jnp.mean(widened * widened, axis=1, keepdims=True) + epsilon)
    normed = (widened * inv_rms * norm_gain[None, :]).astype(BF16)
    relaid = lax.all_to_all(normed, "dp", split_axis=1, concat_axis=0, tiled=True)
    return relaid[None]


def vmem():
    return pl.BlockSpec(memory_space=pltpu.VMEM)


def slot_rows(route_rows, experts, me):
    tok = route_rows.shape[1]
    ids = lax.broadcasted_iota(jnp.int32, (experts, tok), 0) ^ me
    named = (route_rows[0:1, :] == ids) | (route_rows[1:2, :] == ids)
    earlier = lax.broadcasted_iota(jnp.int32, (tok, tok), 0) < lax.broadcasted_iota(
        jnp.int32, (tok, tok), 1
    )
    count = jnp.dot(
        named.astype(F32).astype(BF16), earlier.astype(F32).astype(BF16),
        preferred_element_type=F32,
    )
    return jnp.where(named, count.astype(jnp.int32), -1), ids


def dispatch_body(experts, capacity, route_hbm, tok_hbm, *refs):
    *out_refs, route_ref, tok_ref, sems = refs
    copies = [
        pltpu.make_async_copy(route_hbm, route_ref, sems.at[0]),
        pltpu.make_async_copy(tok_hbm, tok_ref, sems.at[1]),
    ]
    for copy in copies:
        copy.start()
    me = lax.axis_index("expert")
    tok, width = tok_ref.shape
    lane = lax.broadcasted_iota(jnp.int32, (capacity, tok), 0)
    copies[0].wait()
    slots, _ = slot_rows(route_ref[...], experts, me)
    pick = jnp.concatenate(
        [(lane == slots[j : j + 1, :]).astype(F32) for j in range(experts)], axis=0
    ).astype(BF16)
    copies[1].wait()
    tile = 256
    for col in range(0, width, tile):
        rows = jnp.dot(pick, tok_ref[:, col : col + tile], preferred_element_type=F32)
        rows = rows.astype(BF16)
        for j in range(experts):
            out_refs[j][:, col : col + tile] = rows[j * capacity : (j + 1) * capacity, :]


def dispatch(route_rows, own_rows, experts, capacity):
    width = own_rows.shape[1]
    return pl.pallas_call(
        functools.partial(dispatch_body, experts, capacity),
        out_shape=[jax.ShapeDtypeStruct((capacity, width), BF16)] * experts,
        in_specs=[pl.BlockSpec(memory_space=pltpu.HBM)] * 2,
        out_specs=[vmem()] * experts,
        scratch_shapes=[
            pltpu.VMEM(route_rows.shape, jnp.int32),
            pltpu.VMEM(own_rows.shape, BF16),
            pltpu.SemaphoreType.DMA((2,)),
        ],
        name="dispatch",
        cost_estimate=pl.CostEstimate(flops=10**8, transcendentals=0, bytes_accessed=2 * 10**6),
        compiler_params=pltpu.CompilerParams(vmem_limit_bytes=16 * 2**20),
    )(route_rows, own_rows)


def selector_body(experts, capacity, route_ref, code_ref, table_ref, sel_ref, weight_ref):
    me = lax.axis_index("expert")
    rows = route_ref[...]
    slots, ids = slot_rows(rows, experts, me)
    tok = rows.shape[1]
    lane = lax.broadcasted_iota(jnp.int32, (capacity, tok), 0)
    for r in range(2):
        mine = jnp.where(rows[r : r + 1, :] == ids, slots, -1)
        pick = jnp.concatenate(
            [(lane == mine[j : j + 1, :]).astype(F32) for j in range(experts)], axis=0
        )
        sel_ref[r * tok : (r + 1) * tok, :] = pick.T.astype(BF16)
        codes = code_ref[r : r + 1, :]
        weights = jnp.zeros((1, tok), F32)
        for level in range(table_ref.shape[0]):
            weights = jnp.where(codes == level, table_ref[level], weights)
        weight_ref[r] = jnp.broadcast_to(weights, (tok, tok)).T


def selector(route_rows, code_rows, gate_table, experts, capacity):
    tok = route_rows.shape[1]
    return pl.pallas_call(
        functools.partial(selector_body, experts, capacity),
        out_shape=[
            jax.ShapeDtypeStruct((2 * tok, experts * capacity), BF16),
            jax.ShapeDtypeStruct((2, tok, tok), F32),
        ],
        in_specs=[vmem(), vmem(), pl.BlockSpec(memory_space=pltpu.SMEM)],
        out_specs=[vmem()] * 2,
        name="selector",
        cost_estimate=pl.CostEstimate(flops=2 * 10**10, transcendentals=0, bytes_accessed=10**8),
        compiler_params=pltpu.CompilerParams(vmem_limit_bytes=8 * 2**20),
    )(route_rows, code_rows, gate_table)


def chunk_columns(down_ref, offset, chunk):
    me, tile = lax.axis_index("dp"), 256
    for col in range(0, chunk, tile):
        start = pl.multiple_of((me ^ offset) * chunk + col, tile)
        yield col, tile, down_ref[:, pl.ds(start, tile)]


def write_down(hid_ref, down_ref, chunk, plan, out_refs):
    for offset in dict.fromkeys(k for _, offsets in plan for k in offsets):
        for col, tile, weight in chunk_columns(down_ref, offset, chunk):
            rows = jnp.dot(hid_ref[...], weight, preferred_element_type=F32).astype(BF16)
            for (j, offsets), out in zip(plan, out_refs):
                if offset in offsets:
                    capacity = out.shape[0]
                    at = offsets.index(offset) * chunk + col
                    out[:, at : at + tile] = rows[j * capacity : (j + 1) * capacity, :]


def expert_body(count, chunk, plan, *refs):
    blocks, (gate_ref, up_ref, down_ref) = refs[:count], refs[count : count + 3]
    hid_ref, x_ref, outs = refs[count + 3], refs[-1], refs[count + 4 : -1]
    capacity = blocks[0].shape[0]
    for j, block in enumerate(blocks):
        x_ref[j * capacity : (j + 1) * capacity, :] = block[...]
    hid = gate_ref.shape[0]
    tile = 256
    over = (((1,), (1,)), ((), ()))
    for low in range(0, hid, tile):
        high = min(hid, low + tile)
        gate = lax.dot_general(x_ref[...], gate_ref[low:high, :], over, preferred_element_type=F32)
        up = lax.dot_general(x_ref[...], up_ref[low:high, :], over, preferred_element_type=F32)
        hid_ref[:, low:high] = (gate / (1.0 + jnp.exp(-gate)) * up).astype(BF16)
    write_down(hid_ref, down_ref, chunk, plan, outs)


def expert_call(blocks, gate_rows, up_rows, down_rows, plan, chunk):
    count = len(blocks)
    capacity, width = blocks[0].shape
    rows, hid = capacity * count, gate_rows.shape[0]
    shapes = [jax.ShapeDtypeStruct((capacity, chunk * len(offsets)), BF16) for _, offsets in plan]
    return pl.pallas_call(
        functools.partial(expert_body, count, chunk, plan),
        out_shape=[jax.ShapeDtypeStruct((rows, hid), BF16)] + shapes,
        in_specs=[vmem()] * (count + 3),
        out_specs=[vmem()] * (1 + len(shapes)),
        scratch_shapes=[pltpu.VMEM((rows, width), BF16)],
        cost_estimate=pl.CostEstimate(
            flops=5 * rows * hid * width, transcendentals=rows * hid, bytes_accessed=8 * 10**6
        ),
        compiler_params=pltpu.CompilerParams(vmem_limit_bytes=24 * 2**20),
    )(*blocks, gate_rows, up_rows, down_rows)


def down_body(chunk, plan, hid_ref, down_ref, *out_refs):
    write_down(hid_ref, down_ref, chunk, plan, out_refs)


def down_call(hidden, down_rows, count, plan, chunk):
    rows, hid = hidden.shape
    return pl.pallas_call(
        functools.partial(down_body, chunk, plan),
        out_shape=[
            jax.ShapeDtypeStruct((rows // count, chunk * len(offsets)), BF16) for _, offsets in plan
        ],
        in_specs=[vmem()] * 2,
        out_specs=[vmem()] * len(plan),
        cost_estimate=pl.CostEstimate(
            flops=2 * rows * hid * chunk, transcendentals=0, bytes_accessed=3 * 10**6
        ),
        compiler_params=pltpu.CompilerParams(vmem_limit_bytes=16 * 2**20),
    )(hidden, down_rows)


def gather_blocks(blocks, y_ref, low):
    capacity, width = blocks[0].shape[0], y_ref.shape[1]
    for j, block in enumerate(blocks):
        start = low if block.shape[1] > width else 0
        y_ref[j * capacity : (j + 1) * capacity, :] = block[:, start : start + width]


def combine_chunk(sel_ref, weight_ref, y_ref, low, out_ref, squares):
    tok, lanes = squares.shape
    chunk, tile = out_ref.shape[1], 256
    for col in range(0, chunk, tile):
        picked = jnp.dot(
            sel_ref[...], y_ref[:, low + col : low + col + tile], preferred_element_type=F32
        )
        for at in range(0, tile, lanes):
            first = picked[:tok, at : at + lanes] * weight_ref[0]
            second = picked[tok:, at : at + lanes] * weight_ref[1]
            rounded = (first + second).astype(BF16)
            out_ref[:, col + at : col + at + lanes] = rounded
            wide = rounded.astype(F32)
            squares = squares + wide * wide
    return squares


def early_body(count, sel_ref, weight_ref, *refs):
    blocks, (out_ref, sum_ref, y_ref) = refs[:count], refs[count:]
    gather_blocks(blocks, y_ref, 0)
    squares = jnp.zeros(sum_ref.shape, F32)
    sum_ref[...] = combine_chunk(sel_ref, weight_ref, y_ref, 0, out_ref, squares)


def combine_early(select, weights, blocks, width):
    rows, tok = blocks[0].shape[0] * len(blocks), weights.shape[1]
    return pl.pallas_call(
        functools.partial(early_body, len(blocks)),
        out_shape=[
            jax.ShapeDtypeStruct((tok, width), BF16),
            jax.ShapeDtypeStruct((tok, weights.shape[2]), F32),
        ],
        in_specs=[vmem()] * (2 + len(blocks)),
        out_specs=[vmem()] * 2,
        scratch_shapes=[pltpu.VMEM((rows, width), BF16)],
        name="combine_early",
        cost_estimate=pl.CostEstimate(
            flops=4 * tok * rows * width, transcendentals=0, bytes_accessed=10**6
        ),
        compiler_params=pltpu.CompilerParams(vmem_limit_bytes=12 * 2**20),
    )(select, weights, *blocks)


def late_body(count, feat_width, sel_ref, weight_ref, part_ref, gain_ref, *refs):
    blocks, y_ref, outs, sum_ref = refs[:count], refs[-1], refs[count:-2], refs[-2]
    chunk = outs[0].shape[1]
    gather_blocks(blocks, y_ref, feat_width - chunk * len(outs))
    squares = part_ref[...]
    for q, out in enumerate(outs):
        squares = combine_chunk(sel_ref, weight_ref, y_ref, q * chunk, out, squares)
    total = jnp.sum(squares, axis=1, keepdims=True)
    tok = total.shape[0]
    sum_ref[...] = jnp.broadcast_to(total, (tok, tok)).T[0:8, :]
    inv = lax.rsqrt(total * (1.0 / feat_width) + epsilon)
    for q, out in enumerate(outs):
        gain = gain_ref[0:1, q * chunk : (q + 1) * chunk]
        out[...] = (out[...].astype(F32) * inv * gain).astype(BF16)


def combine_late(select, weights, part, gain, blocks, chunk, feat_width):
    width = gain.shape[1]
    rows, tok = blocks[0].shape[0] * len(blocks), weights.shape[1]
    return pl.pallas_call(
        functools.partial(late_body, len(blocks), feat_width),
        out_shape=[jax.ShapeDtypeStruct((tok, chunk), BF16)] * (width // chunk)
        + [jax.ShapeDtypeStruct((8, tok), F32)],
        in_specs=[vmem()] * (4 + len(blocks)),
        out_specs=[vmem()] * (width // chunk + 1),
        scratch_shapes=[pltpu.VMEM((rows, width), BF16)],
        name="combine_late",
        cost_estimate=pl.CostEstimate(
            flops=4 * tok * rows * width, transcendentals=0, bytes_accessed=2 * 10**6
        ),
        compiler_params=pltpu.CompilerParams(vmem_limit_bytes=12 * 2**20),
    )(select, weights, part, gain, *blocks)


def gain_body(offsets, gain_ref, out_ref):
    chunk = out_ref.shape[1] // len(offsets)
    me = lax.axis_index("dp")
    for q, offset in enumerate(offsets):
        start = pl.multiple_of((me ^ offset) * chunk, 128)
        row = gain_ref[:, pl.ds(start, chunk)]
        out_ref[:, q * chunk : (q + 1) * chunk] = jnp.broadcast_to(row, (8, chunk))


def gain_of(norm_gain, offsets, chunk):
    return pl.pallas_call(
        functools.partial(gain_body, offsets),
        out_shape=jax.ShapeDtypeStruct((8, chunk * len(offsets)), F32),
        in_specs=[vmem()],
        out_specs=vmem(),
        cost_estimate=pl.CostEstimate(flops=10**4, transcendentals=0, bytes_accessed=10**4),
        compiler_params=pltpu.CompilerParams(vmem_limit_bytes=2**20),
    )(norm_gain[None, :])


def finish_body(feat_width, ready, raw, *refs):
    ways = len(ready) + len(raw)
    chunks, sums = refs[:ways], refs[ways : ways + len(raw)]
    gain_ref, out_ref, scratch, sems = refs[ways + len(raw) :]
    me = lax.axis_index("dp")
    tok = chunks[0].shape[0]

    def put(source, k):
        rows = pl.ds(pl.multiple_of((me ^ k) * tok, tok), tok)
        copy = pltpu.make_async_copy(source, out_ref.at[rows, :], sems.at[k])
        copy.start()
        return copy

    copies = [put(chunks[i], k) for i, k in enumerate(ready)]
    for i, k in enumerate(raw):
        inv = lax.rsqrt(sums[i][0:1, :] * (1.0 / feat_width) + epsilon)
        column = jnp.broadcast_to(inv, (tok, tok)).T[:, 0:1]
        value = chunks[len(ready) + i][...].astype(F32) * column * gain_ref[0:1, :]
        scratch[i] = value.astype(BF16)
        copies.append(put(scratch.at[i], k))
    for copy in copies:
        copy.wait()


def finish(ready, raw, sums, gain, feat_width):
    first = next(iter(ready.values()))
    tok, width = first.shape
    ways = len(ready) + len(raw)
    return pl.pallas_call(
        functools.partial(finish_body, feat_width, tuple(ready), tuple(raw)),
        out_shape=jax.ShapeDtypeStruct((tok * ways, width), BF16),
        in_specs=[vmem()] * (ways + len(raw) + 1),
        out_specs=pl.BlockSpec(memory_space=pltpu.HBM),
        scratch_shapes=[
            pltpu.VMEM((len(raw), tok, width), BF16),
            pltpu.SemaphoreType.DMA((ways,)),
        ],
        name="finish",
        cost_estimate=pl.CostEstimate(flops=10**6, transcendentals=0, bytes_accessed=10**6),
        compiler_params=pltpu.CompilerParams(vmem_limit_bytes=8 * 2**20),
    )(*ready.values(), *raw.values(), *[sums[k] for k in raw], gain)


def swap(value, axis, offset):
    size = lax.axis_size(axis)
    return lax.ppermute(value, axis, [(i, i ^ offset) for i in range(size)])


def swap_each(values, axis):
    moved = {}
    for k, value in values.items():
        moved[k] = swap(value, axis, k) if k else value
    return moved


def local_fast(tokens, routes, gate_code, gate_table, w_gate, w_up, w_down, norm_gain):
    return fast_steps(tokens, routes, gate_code, gate_table, w_gate, w_up, w_down, norm_gain)


def fast_steps(tokens, routes, gate_code, gate_table, w_gate, w_up, w_down, norm_gain):
    own_rows = tokens[0]
    tok, feat_width = own_rows.shape
    experts = lax.axis_size("expert")
    ways = lax.axis_size("dp")
    capacity = 5 * tok // (2 * experts)
    chunk = feat_width // ways
    along_y, along_x, own, away = [4, 5], [2, 3], [1, 0], [6, 7]
    close = along_y + along_x + own
    early = (ways - 1,)
    late = tuple(range(ways - 2, -1, -1))

    route_rows = routes[0].T
    blocks = dispatch(
        pltpu.with_memory_space_constraint(route_rows, pltpu.HBM),
        pltpu.with_memory_space_constraint(own_rows, pltpu.HBM),
        experts, capacity,
    )
    near = swap_each({k: blocks[k] for k in close}, "expert")
    far = swap_each({k: blocks[k] for k in away}, "expert")
    select, weights = selector(route_rows, gate_code[0].T, gate_table, experts, capacity)
    matrices = w_gate[0].T, w_up[0].T, w_down[0]

    plan = [(close.index(k), early) for k in along_y]
    plan += [(close.index(k), early + late) for k in along_x + own]
    plan += [(close.index(k), late) for k in along_y]
    _, *outputs = expert_call([near[k] for k in close], *matrices, plan, chunk)
    y_early, x_whole, own_whole, y_late = outputs[:2], outputs[2:4], outputs[4:6], outputs[6:]
    got_early = swap_each(dict(zip(along_y, y_early)), "expert")
    whole = swap_each(dict(zip(along_x, x_whole)), "expert")
    whole |= swap_each(dict(zip(own, own_whole)), "expert")
    got_late = swap_each(dict(zip(along_y, y_late)), "expert")
    gain_own = gain_of(norm_gain, (0,), chunk)
    plan = [(j, early) for j in range(len(away))]
    hidden, *away_early = expert_call([far[k] for k in away], *matrices, plan, chunk)
    got_early |= whole | swap_each(dict(zip(away, away_early)), "expert")
    plan = [(j, late) for j in range(len(away))]
    away_late = down_call(hidden, matrices[2], len(away), plan, chunk)
    got_late |= whole | swap_each(dict(zip(away, away_late)), "expert")

    order = range(experts)
    first, part = combine_early(
        select, weights, [got_early[k] for k in order], chunk
    )
    raw = swap_each({early[0]: first}, "dp")
    gain_late = gain_of(norm_gain, late, chunk)
    *rest, total = combine_late(
        select, weights, part, gain_late, [got_late[k] for k in order], chunk, feat_width
    )
    ready = swap_each(dict(zip(late, rest)), "dp")
    sums = swap_each({k: total for k in early}, "dp")
    return finish(ready, raw, sums, gain_own, feat_width)[None]


def solution(mesh):
    in_specs = (
        P("expert", "dp", None),
        P("expert", "dp", None),
        P("expert", "dp", None),
        P(),
        P("expert", None, None),
        P("expert", None, None),
        P("expert", None, None),
        P(),
    )
    out_specs = P("expert", None, "dp")

    def whole(tokens, routes, gate_code, gate_table, w_gate, w_up, w_down, norm_gain):
        args = (tokens, routes, gate_code, gate_table, w_gate, w_up, w_down, norm_gain)
        experts, ways = mesh.shape["expert"], mesh.shape["dp"]
        tok, feat = tokens.shape[1] // ways, tokens.shape[2]
        power = experts & (experts - 1) == 0 and ways & (ways - 1) == 0
        fits = power and experts == 8 and 2 <= ways <= 4
        fits = fits and tok % 128 == 0 and w_gate.shape[0] == experts
        fits = fits and 5 * tok % (16 * experts) == 0 and feat % (256 * ways) == 0
        body = local_fast if fits else local_general
        f = jax.shard_map(body, mesh=mesh, in_specs=in_specs, out_specs=out_specs, check_vma=False)
        return f(*args)

    return whole
```

```python
import functools

import jax
import jax.numpy as jnp
from jax import lax
from jax.experimental import pallas as pl
from jax.experimental.pallas import tpu as pltpu
from jax.sharding import PartitionSpec as P


epsilon = 1e-06


F32 = jnp.float32
BF16 = jnp.bfloat16


def expert_ffn(slot_block, w_gate, w_up, w_down):
    shape_in = slot_block.shape
    flat_rows = slot_block.reshape(-1, shape_in[-1])
    gate_act = jnp.dot(flat_rows, w_gate[0], preferred_element_type=F32)
    up_act = jnp.dot(flat_rows, w_up[0], preferred_element_type=F32)
    hidden = (jax.nn.silu(gate_act) * up_act).astype(BF16)
    result = jnp.dot(hidden, w_down[0], preferred_element_type=F32).astype(BF16)
    return result.reshape(shape_in)


def lookup(codes, gate_table):
    levels = gate_table.shape[0]
    match = codes[:, None] == jnp.arange(levels, dtype=jnp.int32)[None, :]
    return jnp.sum(jnp.where(match, gate_table[None, :], 0.0), axis=1)


def combine_pairs(outputs, weights):
    combined = outputs[:, 0] * weights[:, 0:1] + outputs[:, 1] * weights[:, 1:2]
    rounded = lax.optimization_barrier(combined.astype(BF16))
    return rounded.astype(F32)


def local_general(tokens, routes, gate_code, gate_table, w_gate, w_up, w_down, norm_gain):
    own_rows = tokens[0]
    tok_count, feat_width = own_rows.shape
    experts = w_gate.shape[0] * lax.axis_size("expert")
    capacity = 5 * tok_count // (2 * experts)
    route_ids = routes[0].reshape(-1)
    onehot = (route_ids[:, None] == jnp.arange(experts, dtype=jnp.int32)[None, :]).astype(jnp.int32)
    slot_pos = jnp.sum((jnp.cumsum(onehot, axis=0) - onehot) * onehot, axis=1)
    position = route_ids * capacity + slot_pos
    owner_row = (
        jnp.zeros((experts * capacity,), jnp.int32)
        .at[position]
        .set(jnp.arange(2 * tok_count, dtype=jnp.int32) // 2)
    )
    filled = jnp.zeros((experts * capacity,), jnp.bool_).at[position].set(True)
    buffer = jnp.where(filled[:, None], own_rows[owner_row], jnp.zeros((), BF16))
    buffer = buffer.reshape(experts, capacity, feat_width)
    level_ids = gate_code[0].reshape(-1)
    received = lax.all_to_all(buffer, "expert", split_axis=0, concat_axis=0, tiled=True)
    expert_out = expert_ffn(received, w_gate, w_up, w_down)
    returned = lax.all_to_all(expert_out, "expert", split_axis=0, concat_axis=0, tiled=True)
    outputs = (
        returned.reshape(-1, feat_width)[position]
        .astype(F32)
        .reshape(tok_count, 2, feat_width)
    )
    weights = lookup(level_ids, gate_table).reshape(tok_count, 2)
    widened = combine_pairs(outputs, weights)
    inv_rms = lax.rsqrt(jnp.mean(widened * widened, axis=1, keepdims=True) + epsilon)
    normed = (widened * inv_rms * norm_gain[None, :]).astype(BF16)
    relaid = lax.all_to_all(normed, "dp", split_axis=1, concat_axis=0, tiled=True)
    return relaid[None]


CLOSE, AWAY = [4, 2, 5, 3, 1], [6, 7]


def vmem():
    return pl.BlockSpec(memory_space=pltpu.VMEM)


def slot_rows(route_rows, experts, me):
    tok = route_rows.shape[1]
    ids = lax.broadcasted_iota(jnp.int32, (experts, tok), 0) ^ me
    named = (route_rows[0:1, :] == ids) | (route_rows[1:2, :] == ids)
    earlier = lax.broadcasted_iota(jnp.int32, (tok, tok), 0) < lax.broadcasted_iota(
        jnp.int32, (tok, tok), 1
    )
    count = jnp.dot(
        named.astype(F32).astype(BF16), earlier.astype(F32).astype(BF16),
        preferred_element_type=F32,
    )
    return jnp.where(named, count.astype(jnp.int32), -1), ids


def dispatch_body(experts, capacity, route_hbm, tok_hbm, *refs):
    *out_refs, route_ref, tok_ref, sems = refs
    copies = [
        pltpu.make_async_copy(route_hbm, route_ref, sems.at[0]),
        pltpu.make_async_copy(tok_hbm, tok_ref, sems.at[1]),
    ]
    for copy in copies:
        copy.start()
    me = lax.axis_index("expert")
    tok, width = tok_ref.shape
    lane = lax.broadcasted_iota(jnp.int32, (capacity, tok), 0)
    copies[0].wait()
    slots, _ = slot_rows(route_ref[...], experts, me)
    pick = jnp.concatenate(
        [(lane == slots[j : j + 1, :]).astype(F32) for j in range(experts)], axis=0
    ).astype(BF16)
    copies[1].wait()
    tile = 256
    for col in range(0, width, tile):
        rows = jnp.dot(pick, tok_ref[:, col : col + tile], preferred_element_type=F32)
        rows = rows.astype(BF16)
        for j in range(experts):
            out_refs[j][:, col : col + tile] = rows[j * capacity : (j + 1) * capacity, :]


def dispatch(route_rows, own_rows, experts, capacity):
    width = own_rows.shape[1]
    return pl.pallas_call(
        functools.partial(dispatch_body, experts, capacity),
        out_shape=[jax.ShapeDtypeStruct((capacity, width), BF16)] * experts,
        in_specs=[pl.BlockSpec(memory_space=pltpu.HBM)] * 2,
        out_specs=[vmem()] * experts,
        scratch_shapes=[
            pltpu.VMEM(route_rows.shape, jnp.int32),
            pltpu.VMEM(own_rows.shape, BF16),
            pltpu.SemaphoreType.DMA((2,)),
        ],
        name="dispatch",
        cost_estimate=pl.CostEstimate(flops=10**8, transcendentals=0, bytes_accessed=2 * 10**6),
        compiler_params=pltpu.CompilerParams(vmem_limit_bytes=16 * 2**20),
    )(route_rows, own_rows)


def selector_body(experts, capacity, route_ref, code_ref, table_ref, sel_ref, weight_ref):
    me = lax.axis_index("expert")
    rows = route_ref[...]
    slots, ids = slot_rows(rows, experts, me)
    tok = rows.shape[1]
    lane = lax.broadcasted_iota(jnp.int32, (capacity, tok), 0)
    for r in range(2):
        mine = jnp.where(rows[r : r + 1, :] == ids, slots, -1)
        pick = jnp.concatenate(
            [(lane == mine[j : j + 1, :]).astype(F32) for j in range(experts)], axis=0
        )
        sel_ref[r * tok : (r + 1) * tok, :] = pick.T.astype(BF16)
        codes = code_ref[r : r + 1, :]
        weights = jnp.zeros((1, tok), F32)
        for level in range(table_ref.shape[0]):
            weights = jnp.where(codes == level, table_ref[level], weights)
        weight_ref[r] = jnp.broadcast_to(weights, (tok, tok)).T


def selector(route_rows, code_rows, gate_table, experts, capacity):
    tok = route_rows.shape[1]
    return pl.pallas_call(
        functools.partial(selector_body, experts, capacity),
        out_shape=[
            jax.ShapeDtypeStruct((2 * tok, experts * capacity), BF16),
            jax.ShapeDtypeStruct((2, tok, tok), F32),
        ],
        in_specs=[vmem(), vmem(), pl.BlockSpec(memory_space=pltpu.SMEM)],
        out_specs=[vmem()] * 2,
        name="selector",
        cost_estimate=pl.CostEstimate(flops=2 * 10**10, transcendentals=0, bytes_accessed=10**8),
        compiler_params=pltpu.CompilerParams(vmem_limit_bytes=8 * 2**20),
    )(route_rows, code_rows, gate_table)


def chunk_columns(down_ref, offset, chunk):
    me, tile = lax.axis_index("dp"), 256
    for col in range(0, chunk, tile):
        start = pl.multiple_of((me ^ offset) * chunk + col, tile)
        yield col, tile, down_ref[:, pl.ds(start, tile)]


def write_down(hid_ref, down_ref, chunk, plan, out_refs):
    for offset in dict.fromkeys(k for _, offsets in plan for k in offsets):
        for col, tile, weight in chunk_columns(down_ref, offset, chunk):
            rows = jnp.dot(hid_ref[...], weight, preferred_element_type=F32).astype(BF16)
            for (j, offsets), out in zip(plan, out_refs):
                if offset in offsets:
                    capacity = out.shape[0]
                    at = offsets.index(offset) * chunk + col
                    out[:, at : at + tile] = rows[j * capacity : (j + 1) * capacity, :]


def expert_body(count, chunk, plan, *refs):
    blocks, (gate_ref, up_ref, down_ref) = refs[:count], refs[count : count + 3]
    hid_ref, x_ref, outs = refs[count + 3], refs[-1], refs[count + 4 : -1]
    capacity = blocks[0].shape[0]
    for j, block in enumerate(blocks):
        x_ref[j * capacity : (j + 1) * capacity, :] = block[...]
    hid = gate_ref.shape[0]
    tile = 256
    over = (((1,), (1,)), ((), ()))
    for low in range(0, hid, tile):
        high = min(hid, low + tile)
        gate = lax.dot_general(x_ref[...], gate_ref[low:high, :], over, preferred_element_type=F32)
        up = lax.dot_general(x_ref[...], up_ref[low:high, :], over, preferred_element_type=F32)
        hid_ref[:, low:high] = (gate / (1.0 + jnp.exp(-gate)) * up).astype(BF16)
    write_down(hid_ref, down_ref, chunk, plan, outs)


def expert_call(blocks, gate_rows, up_rows, down_rows, plan, chunk):
    count = len(blocks)
    capacity, width = blocks[0].shape
    rows, hid = capacity * count, gate_rows.shape[0]
    shapes = [jax.ShapeDtypeStruct((capacity, chunk * len(offsets)), BF16) for _, offsets in plan]
    return pl.pallas_call(
        functools.partial(expert_body, count, chunk, plan),
        out_shape=[jax.ShapeDtypeStruct((rows, hid), BF16)] + shapes,
        in_specs=[vmem()] * (count + 3),
        out_specs=[vmem()] * (1 + len(shapes)),
        scratch_shapes=[pltpu.VMEM((rows, width), BF16)],
        cost_estimate=pl.CostEstimate(
            flops=5 * rows * hid * width, transcendentals=rows * hid, bytes_accessed=8 * 10**6
        ),
        compiler_params=pltpu.CompilerParams(vmem_limit_bytes=24 * 2**20),
    )(*blocks, gate_rows, up_rows, down_rows)


def down_body(chunk, plan, hid_ref, down_ref, *out_refs):
    write_down(hid_ref, down_ref, chunk, plan, out_refs)


def down_call(hidden, down_rows, count, plan, chunk):
    rows, hid = hidden.shape
    return pl.pallas_call(
        functools.partial(down_body, chunk, plan),
        out_shape=[
            jax.ShapeDtypeStruct((rows // count, chunk * len(offsets)), BF16) for _, offsets in plan
        ],
        in_specs=[vmem()] * 2,
        out_specs=[vmem()] * len(plan),
        cost_estimate=pl.CostEstimate(
            flops=2 * rows * hid * chunk, transcendentals=0, bytes_accessed=3 * 10**6
        ),
        compiler_params=pltpu.CompilerParams(vmem_limit_bytes=16 * 2**20),
    )(hidden, down_rows)


def gather_blocks(blocks, y_ref, low):
    capacity, width = blocks[0].shape[0], y_ref.shape[1]
    for j, block in enumerate(blocks):
        start = low if block.shape[1] > width else 0
        y_ref[j * capacity : (j + 1) * capacity, :] = block[:, start : start + width]


def combine_chunk(sel_ref, weight_ref, y_ref, low, out_ref, squares):
    tok, lanes = squares.shape
    chunk, tile = out_ref.shape[1], 256
    for col in range(0, chunk, tile):
        picked = jnp.dot(
            sel_ref[...], y_ref[:, low + col : low + col + tile], preferred_element_type=F32
        )
        for at in range(0, tile, lanes):
            first = picked[:tok, at : at + lanes] * weight_ref[0]
            second = picked[tok:, at : at + lanes] * weight_ref[1]
            rounded = (first + second).astype(BF16)
            out_ref[:, col + at : col + at + lanes] = rounded
            wide = rounded.astype(F32)
            squares = squares + wide * wide
    return squares


def early_body(count, sel_ref, weight_ref, *refs):
    blocks, (out_ref, sum_ref, y_ref) = refs[:count], refs[count:]
    gather_blocks(blocks, y_ref, 0)
    squares = jnp.zeros(sum_ref.shape, F32)
    sum_ref[...] = combine_chunk(sel_ref, weight_ref, y_ref, 0, out_ref, squares)


def combine_early(select, weights, blocks, width):
    rows, tok = blocks[0].shape[0] * len(blocks), weights.shape[1]
    return pl.pallas_call(
        functools.partial(early_body, len(blocks)),
        out_shape=[
            jax.ShapeDtypeStruct((tok, width), BF16),
            jax.ShapeDtypeStruct((tok, weights.shape[2]), F32),
        ],
        in_specs=[vmem()] * (2 + len(blocks)),
        out_specs=[vmem()] * 2,
        scratch_shapes=[pltpu.VMEM((rows, width), BF16)],
        name="combine_early",
        cost_estimate=pl.CostEstimate(
            flops=4 * tok * rows * width, transcendentals=0, bytes_accessed=10**6
        ),
        compiler_params=pltpu.CompilerParams(vmem_limit_bytes=12 * 2**20),
    )(select, weights, *blocks)


def late_body(count, feat_width, sel_ref, weight_ref, part_ref, gain_ref, *refs):
    blocks, y_ref, outs, sum_ref = refs[:count], refs[-1], refs[count:-2], refs[-2]
    chunk = outs[0].shape[1]
    gather_blocks(blocks, y_ref, feat_width - chunk * len(outs))
    squares = part_ref[...]
    for q, out in enumerate(outs):
        squares = combine_chunk(sel_ref, weight_ref, y_ref, q * chunk, out, squares)
    total = jnp.sum(squares, axis=1, keepdims=True)
    tok = total.shape[0]
    sum_ref[...] = jnp.broadcast_to(total, (tok, tok)).T[0:8, :]
    inv = lax.rsqrt(total * (1.0 / feat_width) + epsilon)
    for q, out in enumerate(outs):
        gain = gain_ref[0:1, q * chunk : (q + 1) * chunk]
        out[...] = (out[...].astype(F32) * inv * gain).astype(BF16)


def combine_late(select, weights, part, gain, blocks, chunk, feat_width):
    width = gain.shape[1]
    rows, tok = blocks[0].shape[0] * len(blocks), weights.shape[1]
    return pl.pallas_call(
        functools.partial(late_body, len(blocks), feat_width),
        out_shape=[jax.ShapeDtypeStruct((tok, chunk), BF16)] * (width // chunk)
        + [jax.ShapeDtypeStruct((8, tok), F32)],
        in_specs=[vmem()] * (4 + len(blocks)),
        out_specs=[vmem()] * (width // chunk + 1),
        scratch_shapes=[pltpu.VMEM((rows, width), BF16)],
        name="combine_late",
        cost_estimate=pl.CostEstimate(
            flops=4 * tok * rows * width, transcendentals=0, bytes_accessed=2 * 10**6
        ),
        compiler_params=pltpu.CompilerParams(vmem_limit_bytes=12 * 2**20),
    )(select, weights, part, gain, *blocks)


def gain_body(offsets, gain_ref, out_ref):
    chunk = out_ref.shape[1] // len(offsets)
    me = lax.axis_index("dp")
    for q, offset in enumerate(offsets):
        start = pl.multiple_of((me ^ offset) * chunk, 128)
        row = gain_ref[:, pl.ds(start, chunk)]
        out_ref[:, q * chunk : (q + 1) * chunk] = jnp.broadcast_to(row, (8, chunk))


def gain_of(norm_gain, offsets, chunk):
    return pl.pallas_call(
        functools.partial(gain_body, offsets),
        out_shape=jax.ShapeDtypeStruct((8, chunk * len(offsets)), F32),
        in_specs=[vmem()],
        out_specs=vmem(),
        cost_estimate=pl.CostEstimate(flops=10**4, transcendentals=0, bytes_accessed=10**4),
        compiler_params=pltpu.CompilerParams(vmem_limit_bytes=2**20),
    )(norm_gain[None, :])


def finish_body(feat_width, ready, raw, *refs):
    ways = len(ready) + len(raw)
    chunks, sums = refs[:ways], refs[ways : ways + len(raw)]
    gain_ref, out_ref, scratch, sems = refs[ways + len(raw) :]
    me = lax.axis_index("dp")
    tok = chunks[0].shape[0]

    def put(source, k):
        rows = pl.ds(pl.multiple_of((me ^ k) * tok, tok), tok)
        copy = pltpu.make_async_copy(source, out_ref.at[rows, :], sems.at[k])
        copy.start()
        return copy

    copies = [put(chunks[i], k) for i, k in enumerate(ready)]
    for i, k in enumerate(raw):
        inv = lax.rsqrt(sums[i][0:1, :] * (1.0 / feat_width) + epsilon)
        column = jnp.broadcast_to(inv, (tok, tok)).T[:, 0:1]
        value = chunks[len(ready) + i][...].astype(F32) * column * gain_ref[0:1, :]
        scratch[i] = value.astype(BF16)
        copies.append(put(scratch.at[i], k))
    for copy in copies:
        copy.wait()


def finish(ready, raw, sums, gain, feat_width):
    first = next(iter(ready.values()))
    tok, width = first.shape
    ways = len(ready) + len(raw)
    return pl.pallas_call(
        functools.partial(finish_body, feat_width, tuple(ready), tuple(raw)),
        out_shape=jax.ShapeDtypeStruct((tok * ways, width), BF16),
        in_specs=[vmem()] * (ways + len(raw) + 1),
        out_specs=pl.BlockSpec(memory_space=pltpu.HBM),
        scratch_shapes=[
            pltpu.VMEM((len(raw), tok, width), BF16),
            pltpu.SemaphoreType.DMA((ways,)),
        ],
        name="finish",
        cost_estimate=pl.CostEstimate(flops=10**6, transcendentals=0, bytes_accessed=10**6),
        compiler_params=pltpu.CompilerParams(vmem_limit_bytes=8 * 2**20),
    )(*ready.values(), *raw.values(), *[sums[k] for k in raw], gain)


def swap(value, axis, offset):
    size = lax.axis_size(axis)
    return lax.ppermute(value, axis, [(i, i ^ offset) for i in range(size)])


def swap_each(values, axis):
    moved = {}
    for k, value in values.items():
        moved[k] = swap(value, axis, k) if k else value
    return moved


def local_fast(tokens, routes, gate_code, gate_table, w_gate, w_up, w_down, norm_gain):
    return fast_steps(tokens, routes, gate_code, gate_table, w_gate, w_up, w_down, norm_gain)


def fast_steps(tokens, routes, gate_code, gate_table, w_gate, w_up, w_down, norm_gain):
    own_rows = tokens[0]
    tok, feat_width = own_rows.shape
    experts = lax.axis_size("expert")
    ways = lax.axis_size("dp")
    capacity = 5 * tok // (2 * experts)
    chunk = feat_width // ways
    close, away = CLOSE + [0], AWAY
    early = (ways // 2,)
    late = tuple(k for k in range(ways - 1, -1, -1) if k not in early)

    route_rows = routes[0].T
    blocks = dispatch(
        pltpu.with_memory_space_constraint(route_rows, pltpu.HBM),
        pltpu.with_memory_space_constraint(own_rows, pltpu.HBM),
        experts, capacity,
    )
    near = swap_each({k: blocks[k] for k in close}, "expert")
    far = swap_each({k: blocks[k] for k in away}, "expert")
    select, weights = selector(route_rows, gate_code[0].T, gate_table, experts, capacity)
    matrices = w_gate[0].T, w_up[0].T, w_down[0]

    plan = [(j, early + late) for j in range(len(close))]
    _, *outputs = expert_call([near[k] for k in close], *matrices, plan, chunk)
    back = swap_each(dict(zip(close, outputs)), "expert")
    gain_own = gain_of(norm_gain, (0,), chunk)
    plan = [(j, early) for j in range(len(away))]
    hidden, *away_early = expert_call([far[k] for k in away], *matrices, plan, chunk)
    got_early = back | swap_each(dict(zip(away, away_early)), "expert")
    plan = [(j, late) for j in range(len(away))]
    away_late = down_call(hidden, matrices[2], len(away), plan, chunk)
    got_late = back | swap_each(dict(zip(away, away_late)), "expert")

    order = range(experts)
    first, part = combine_early(
        select, weights, [got_early[k] for k in order], chunk
    )
    raw = swap_each({early[0]: first}, "dp")
    gain_late = gain_of(norm_gain, late, chunk)
    *rest, total = combine_late(
        select, weights, part, gain_late, [got_late[k] for k in order], chunk, feat_width
    )
    ready = swap_each(dict(zip(late, rest)), "dp")
    sums = swap_each({k: total for k in early}, "dp")
    return finish(ready, raw, sums, gain_own, feat_width)[None]


def solution(mesh):
    in_specs = (
        P("expert", "dp", None),
        P("expert", "dp", None),
        P("expert", "dp", None),
        P(),
        P("expert", None, None),
        P("expert", None, None),
        P("expert", None, None),
        P(),
    )
    out_specs = P("expert", None, "dp")

    def whole(tokens, routes, gate_code, gate_table, w_gate, w_up, w_down, norm_gain):
        args = (tokens, routes, gate_code, gate_table, w_gate, w_up, w_down, norm_gain)
        experts, ways = mesh.shape["expert"], mesh.shape["dp"]
        tok, feat = tokens.shape[1] // ways, tokens.shape[2]
        power = experts & (experts - 1) == 0 and ways & (ways - 1) == 0
        fits = power and experts == 8 and 2 <= ways <= 4
        fits = fits and tok % 128 == 0 and w_gate.shape[0] == experts
        fits = fits and 5 * tok % (16 * experts) == 0 and feat % (256 * ways) == 0
        body = local_fast if fits else local_general
        f = jax.shard_map(body, mesh=mesh, in_specs=in_specs, out_specs=out_specs, check_vma=False)
        return f(*args)

    return whole
```

```python
import functools

import jax
import jax.numpy as jnp
from jax import lax
from jax.experimental import pallas as pl
from jax.experimental.pallas import tpu as pltpu
from jax.sharding import PartitionSpec as P


epsilon = 1e-06


F32 = jnp.float32
BF16 = jnp.bfloat16


def expert_ffn(slot_block, w_gate, w_up, w_down):
    shape_in = slot_block.shape
    flat_rows = slot_block.reshape(-1, shape_in[-1])
    gate_act = jnp.dot(flat_rows, w_gate[0], preferred_element_type=F32)
    up_act = jnp.dot(flat_rows, w_up[0], preferred_element_type=F32)
    hidden = (jax.nn.silu(gate_act) * up_act).astype(BF16)
    result = jnp.dot(hidden, w_down[0], preferred_element_type=F32).astype(BF16)
    return result.reshape(shape_in)


def lookup(codes, gate_table):
    levels = gate_table.shape[0]
    match = codes[:, None] == jnp.arange(levels, dtype=jnp.int32)[None, :]
    return jnp.sum(jnp.where(match, gate_table[None, :], 0.0), axis=1)


def combine_pairs(outputs, weights):
    combined = outputs[:, 0] * weights[:, 0:1] + outputs[:, 1] * weights[:, 1:2]
    rounded = lax.optimization_barrier(combined.astype(BF16))
    return rounded.astype(F32)


def local_general(tokens, routes, gate_code, gate_table, w_gate, w_up, w_down, norm_gain):
    own_rows = tokens[0]
    tok_count, feat_width = own_rows.shape
    experts = w_gate.shape[0] * lax.axis_size("expert")
    capacity = 5 * tok_count // (2 * experts)
    route_ids = routes[0].reshape(-1)
    onehot = (route_ids[:, None] == jnp.arange(experts, dtype=jnp.int32)[None, :]).astype(jnp.int32)
    slot_pos = jnp.sum((jnp.cumsum(onehot, axis=0) - onehot) * onehot, axis=1)
    position = route_ids * capacity + slot_pos
    owner_row = (
        jnp.zeros((experts * capacity,), jnp.int32)
        .at[position]
        .set(jnp.arange(2 * tok_count, dtype=jnp.int32) // 2)
    )
    filled = jnp.zeros((experts * capacity,), jnp.bool_).at[position].set(True)
    buffer = jnp.where(filled[:, None], own_rows[owner_row], jnp.zeros((), BF16))
    buffer = buffer.reshape(experts, capacity, feat_width)
    level_ids = gate_code[0].reshape(-1)
    received = lax.all_to_all(buffer, "expert", split_axis=0, concat_axis=0, tiled=True)
    expert_out = expert_ffn(received, w_gate, w_up, w_down)
    returned = lax.all_to_all(expert_out, "expert", split_axis=0, concat_axis=0, tiled=True)
    outputs = (
        returned.reshape(-1, feat_width)[position]
        .astype(F32)
        .reshape(tok_count, 2, feat_width)
    )
    weights = lookup(level_ids, gate_table).reshape(tok_count, 2)
    widened = combine_pairs(outputs, weights)
    inv_rms = lax.rsqrt(jnp.mean(widened * widened, axis=1, keepdims=True) + epsilon)
    normed = (widened * inv_rms * norm_gain[None, :]).astype(BF16)
    relaid = lax.all_to_all(normed, "dp", split_axis=1, concat_axis=0, tiled=True)
    return relaid[None]


CLOSE, AWAY = [4, 2, 5, 3, 1], [6, 7]


def vmem():
    return pl.BlockSpec(memory_space=pltpu.VMEM)


def slot_rows(route_rows, experts, me):
    tok = route_rows.shape[1]
    ids = lax.broadcasted_iota(jnp.int32, (experts, tok), 0) ^ me
    named = (route_rows[0:1, :] == ids) | (route_rows[1:2, :] == ids)
    earlier = lax.broadcasted_iota(jnp.int32, (tok, tok), 0) < lax.broadcasted_iota(
        jnp.int32, (tok, tok), 1
    )
    count = jnp.dot(
        named.astype(F32).astype(BF16), earlier.astype(F32).astype(BF16),
        preferred_element_type=F32,
    )
    return jnp.where(named, count.astype(jnp.int32), -1), ids


def dispatch_body(experts, capacity, route_hbm, tok_hbm, *refs):
    *out_refs, route_ref, tok_ref, sems = refs
    copies = [
        pltpu.make_async_copy(route_hbm, route_ref, sems.at[0]),
        pltpu.make_async_copy(tok_hbm, tok_ref, sems.at[1]),
    ]
    for copy in copies:
        copy.start()
    me = lax.axis_index("expert")
    tok, width = tok_ref.shape
    lane = lax.broadcasted_iota(jnp.int32, (capacity, tok), 0)
    copies[0].wait()
    slots, _ = slot_rows(route_ref[...], experts, me)
    pick = jnp.concatenate(
        [(lane == slots[j : j + 1, :]).astype(F32) for j in range(experts)], axis=0
    ).astype(BF16)
    copies[1].wait()
    tile = 256
    for col in range(0, width, tile):
        rows = jnp.dot(pick, tok_ref[:, col : col + tile], preferred_element_type=F32)
        rows = rows.astype(BF16)
        for j in range(experts):
            out_refs[j][:, col : col + tile] = rows[j * capacity : (j + 1) * capacity, :]


def dispatch(route_rows, own_rows, experts, capacity):
    width = own_rows.shape[1]
    return pl.pallas_call(
        functools.partial(dispatch_body, experts, capacity),
        out_shape=[jax.ShapeDtypeStruct((capacity, width), BF16)] * experts,
        in_specs=[pl.BlockSpec(memory_space=pltpu.HBM)] * 2,
        out_specs=[vmem()] * experts,
        scratch_shapes=[
            pltpu.VMEM(route_rows.shape, jnp.int32),
            pltpu.VMEM(own_rows.shape, BF16),
            pltpu.SemaphoreType.DMA((2,)),
        ],
        name="dispatch",
        cost_estimate=pl.CostEstimate(flops=10**8, transcendentals=0, bytes_accessed=2 * 10**6),
        compiler_params=pltpu.CompilerParams(vmem_limit_bytes=16 * 2**20),
    )(route_rows, own_rows)


def selector_body(experts, capacity, route_ref, code_ref, table_ref, sel_ref, weight_ref):
    me = lax.axis_index("expert")
    rows = route_ref[...]
    slots, ids = slot_rows(rows, experts, me)
    tok = rows.shape[1]
    lane = lax.broadcasted_iota(jnp.int32, (capacity, tok), 0)
    for r in range(2):
        mine = jnp.where(rows[r : r + 1, :] == ids, slots, -1)
        pick = jnp.concatenate(
            [(lane == mine[j : j + 1, :]).astype(F32) for j in range(experts)], axis=0
        )
        sel_ref[r * tok : (r + 1) * tok, :] = pick.T.astype(BF16)
        codes = code_ref[r : r + 1, :]
        weights = jnp.zeros((1, tok), F32)
        for level in range(table_ref.shape[0]):
            weights = jnp.where(codes == level, table_ref[level], weights)
        weight_ref[r] = jnp.broadcast_to(weights, (tok, tok)).T


def selector(route_rows, code_rows, gate_table, experts, capacity):
    tok = route_rows.shape[1]
    return pl.pallas_call(
        functools.partial(selector_body, experts, capacity),
        out_shape=[
            jax.ShapeDtypeStruct((2 * tok, experts * capacity), BF16),
            jax.ShapeDtypeStruct((2, tok, tok), F32),
        ],
        in_specs=[vmem(), vmem(), pl.BlockSpec(memory_space=pltpu.SMEM)],
        out_specs=[vmem()] * 2,
        name="selector",
        cost_estimate=pl.CostEstimate(flops=2 * 10**10, transcendentals=0, bytes_accessed=10**8),
        compiler_params=pltpu.CompilerParams(vmem_limit_bytes=8 * 2**20),
    )(route_rows, code_rows, gate_table)


def chunk_columns(down_ref, offset, chunk):
    me, tile = lax.axis_index("dp"), 256
    for col in range(0, chunk, tile):
        start = pl.multiple_of((me ^ offset) * chunk + col, tile)
        yield col, tile, down_ref[:, pl.ds(start, tile)]


def write_down(hid_ref, down_ref, chunk, plan, out_refs):
    for offset in dict.fromkeys(k for _, offsets in plan for k in offsets):
        for col, tile, weight in chunk_columns(down_ref, offset, chunk):
            rows = jnp.dot(hid_ref[...], weight, preferred_element_type=F32).astype(BF16)
            for (j, offsets), out in zip(plan, out_refs):
                if offset in offsets:
                    capacity = out.shape[0]
                    at = offsets.index(offset) * chunk + col
                    out[:, at : at + tile] = rows[j * capacity : (j + 1) * capacity, :]


def expert_body(count, chunk, plan, *refs):
    blocks, (gate_ref, up_ref, down_ref) = refs[:count], refs[count : count + 3]
    hid_ref, x_ref, outs = refs[count + 3], refs[-1], refs[count + 4 : -1]
    capacity = blocks[0].shape[0]
    for j, block in enumerate(blocks):
        x_ref[j * capacity : (j + 1) * capacity, :] = block[...]
    hid = gate_ref.shape[0]
    tile = 256
    over = (((1,), (1,)), ((), ()))
    for low in range(0, hid, tile):
        high = min(hid, low + tile)
        gate = lax.dot_general(x_ref[...], gate_ref[low:high, :], over, preferred_element_type=F32)
        up = lax.dot_general(x_ref[...], up_ref[low:high, :], over, preferred_element_type=F32)
        hid_ref[:, low:high] = (gate / (1.0 + jnp.exp(-gate)) * up).astype(BF16)
    write_down(hid_ref, down_ref, chunk, plan, outs)


def expert_call(blocks, gate_rows, up_rows, down_rows, plan, chunk):
    count = len(blocks)
    capacity, width = blocks[0].shape
    rows, hid = capacity * count, gate_rows.shape[0]
    shapes = [jax.ShapeDtypeStruct((capacity, chunk * len(offsets)), BF16) for _, offsets in plan]
    return pl.pallas_call(
        functools.partial(expert_body, count, chunk, plan),
        out_shape=[jax.ShapeDtypeStruct((rows, hid), BF16)] + shapes,
        in_specs=[vmem()] * (count + 3),
        out_specs=[vmem()] * (1 + len(shapes)),
        scratch_shapes=[pltpu.VMEM((rows, width), BF16)],
        cost_estimate=pl.CostEstimate(
            flops=5 * rows * hid * width, transcendentals=rows * hid, bytes_accessed=8 * 10**6
        ),
        compiler_params=pltpu.CompilerParams(vmem_limit_bytes=24 * 2**20),
    )(*blocks, gate_rows, up_rows, down_rows)


def down_body(chunk, plan, hid_ref, down_ref, *out_refs):
    write_down(hid_ref, down_ref, chunk, plan, out_refs)


def down_call(hidden, down_rows, count, plan, chunk):
    rows, hid = hidden.shape
    return pl.pallas_call(
        functools.partial(down_body, chunk, plan),
        out_shape=[
            jax.ShapeDtypeStruct((rows // count, chunk * len(offsets)), BF16) for _, offsets in plan
        ],
        in_specs=[vmem()] * 2,
        out_specs=[vmem()] * len(plan),
        cost_estimate=pl.CostEstimate(
            flops=2 * rows * hid * chunk, transcendentals=0, bytes_accessed=3 * 10**6
        ),
        compiler_params=pltpu.CompilerParams(vmem_limit_bytes=16 * 2**20),
    )(hidden, down_rows)


def gather_blocks(blocks, y_ref, low):
    capacity, width = blocks[0].shape[0], y_ref.shape[1]
    for j, block in enumerate(blocks):
        start = low if block.shape[1] > width else 0
        y_ref[j * capacity : (j + 1) * capacity, :] = block[:, start : start + width]


def combine_chunk(sel_ref, weight_ref, y_ref, low, out_ref, squares):
    tok, lanes = squares.shape
    chunk, tile = out_ref.shape[1], 256
    for col in range(0, chunk, tile):
        picked = jnp.dot(
            sel_ref[...], y_ref[:, low + col : low + col + tile], preferred_element_type=F32
        )
        for at in range(0, tile, lanes):
            first = picked[:tok, at : at + lanes] * weight_ref[0]
            second = picked[tok:, at : at + lanes] * weight_ref[1]
            rounded = (first + second).astype(BF16)
            out_ref[:, col + at : col + at + lanes] = rounded
            wide = rounded.astype(F32)
            squares = squares + wide * wide
    return squares


def early_body(count, sel_ref, weight_ref, *refs):
    blocks, (out_ref, sum_ref, y_ref) = refs[:count], refs[count:]
    gather_blocks(blocks, y_ref, 0)
    squares = jnp.zeros(sum_ref.shape, F32)
    sum_ref[...] = combine_chunk(sel_ref, weight_ref, y_ref, 0, out_ref, squares)


def combine_early(select, weights, blocks, width):
    rows, tok = blocks[0].shape[0] * len(blocks), weights.shape[1]
    return pl.pallas_call(
        functools.partial(early_body, len(blocks)),
        out_shape=[
            jax.ShapeDtypeStruct((tok, width), BF16),
            jax.ShapeDtypeStruct((tok, weights.shape[2]), F32),
        ],
        in_specs=[vmem()] * (2 + len(blocks)),
        out_specs=[vmem()] * 2,
        scratch_shapes=[pltpu.VMEM((rows, width), BF16)],
        name="combine_early",
        cost_estimate=pl.CostEstimate(
            flops=4 * tok * rows * width, transcendentals=0, bytes_accessed=10**6
        ),
        compiler_params=pltpu.CompilerParams(vmem_limit_bytes=12 * 2**20),
    )(select, weights, *blocks)


def late_body(count, feat_width, sel_ref, weight_ref, part_ref, gain_ref, *refs):
    blocks, y_ref, outs, sum_ref = refs[:count], refs[-1], refs[count:-2], refs[-2]
    chunk = outs[0].shape[1]
    gather_blocks(blocks, y_ref, feat_width - chunk * len(outs))
    squares = part_ref[...]
    for q, out in enumerate(outs):
        squares = combine_chunk(sel_ref, weight_ref, y_ref, q * chunk, out, squares)
    total = jnp.sum(squares, axis=1, keepdims=True)
    tok = total.shape[0]
    sum_ref[...] = jnp.broadcast_to(total, (tok, tok)).T[0:8, :]
    inv = lax.rsqrt(total * (1.0 / feat_width) + epsilon)
    for q, out in enumerate(outs):
        gain = gain_ref[0:1, q * chunk : (q + 1) * chunk]
        out[...] = (out[...].astype(F32) * inv * gain).astype(BF16)


def combine_late(select, weights, part, gain, blocks, chunk, feat_width):
    width = gain.shape[1]
    rows, tok = blocks[0].shape[0] * len(blocks), weights.shape[1]
    return pl.pallas_call(
        functools.partial(late_body, len(blocks), feat_width),
        out_shape=[jax.ShapeDtypeStruct((tok, chunk), BF16)] * (width // chunk)
        + [jax.ShapeDtypeStruct((8, tok), F32)],
        in_specs=[vmem()] * (4 + len(blocks)),
        out_specs=[vmem()] * (width // chunk + 1),
        scratch_shapes=[pltpu.VMEM((rows, width), BF16)],
        name="combine_late",
        cost_estimate=pl.CostEstimate(
            flops=4 * tok * rows * width, transcendentals=0, bytes_accessed=2 * 10**6
        ),
        compiler_params=pltpu.CompilerParams(vmem_limit_bytes=12 * 2**20),
    )(select, weights, part, gain, *blocks)


def gain_body(offsets, gain_ref, out_ref):
    chunk = out_ref.shape[1] // len(offsets)
    me = lax.axis_index("dp")
    for q, offset in enumerate(offsets):
        start = pl.multiple_of((me ^ offset) * chunk, 128)
        row = gain_ref[:, pl.ds(start, chunk)]
        out_ref[:, q * chunk : (q + 1) * chunk] = jnp.broadcast_to(row, (8, chunk))


def gain_of(norm_gain, offsets, chunk):
    return pl.pallas_call(
        functools.partial(gain_body, offsets),
        out_shape=jax.ShapeDtypeStruct((8, chunk * len(offsets)), F32),
        in_specs=[vmem()],
        out_specs=vmem(),
        cost_estimate=pl.CostEstimate(flops=10**4, transcendentals=0, bytes_accessed=10**4),
        compiler_params=pltpu.CompilerParams(vmem_limit_bytes=2**20),
    )(norm_gain[None, :])


def finish_body(feat_width, ready, raw, *refs):
    ways = len(ready) + len(raw)
    chunks, sums = refs[:ways], refs[ways : ways + len(raw)]
    gain_ref, out_ref, scratch, sems = refs[ways + len(raw) :]
    me = lax.axis_index("dp")
    tok = chunks[0].shape[0]

    def put(source, k):
        rows = pl.ds(pl.multiple_of((me ^ k) * tok, tok), tok)
        copy = pltpu.make_async_copy(source, out_ref.at[rows, :], sems.at[k])
        copy.start()
        return copy

    copies = [put(chunks[i], k) for i, k in enumerate(ready)]
    for i, k in enumerate(raw):
        inv = lax.rsqrt(sums[i][0:1, :] * (1.0 / feat_width) + epsilon)
        column = jnp.broadcast_to(inv, (tok, tok)).T[:, 0:1]
        value = chunks[len(ready) + i][...].astype(F32) * column * gain_ref[0:1, :]
        scratch[i] = value.astype(BF16)
        copies.append(put(scratch.at[i], k))
    for copy in copies:
        copy.wait()


def finish(ready, raw, sums, gain, feat_width):
    first = next(iter(ready.values()))
    tok, width = first.shape
    ways = len(ready) + len(raw)
    return pl.pallas_call(
        functools.partial(finish_body, feat_width, tuple(ready), tuple(raw)),
        out_shape=jax.ShapeDtypeStruct((tok * ways, width), BF16),
        in_specs=[vmem()] * (ways + len(raw) + 1),
        out_specs=pl.BlockSpec(memory_space=pltpu.HBM),
        scratch_shapes=[
            pltpu.VMEM((len(raw), tok, width), BF16),
            pltpu.SemaphoreType.DMA((ways,)),
        ],
        name="finish",
        cost_estimate=pl.CostEstimate(flops=10**6, transcendentals=0, bytes_accessed=10**6),
        compiler_params=pltpu.CompilerParams(vmem_limit_bytes=8 * 2**20),
    )(*ready.values(), *raw.values(), *[sums[k] for k in raw], gain)


def swap(value, axis, offset):
    size = lax.axis_size(axis)
    return lax.ppermute(value, axis, [(i, i ^ offset) for i in range(size)])


def swap_each(values, axis):
    moved = {}
    for k, value in values.items():
        moved[k] = swap(value, axis, k) if k else value
    return moved


def local_fast(tokens, routes, gate_code, gate_table, w_gate, w_up, w_down, norm_gain):
    return fast_steps(tokens, routes, gate_code, gate_table, w_gate, w_up, w_down, norm_gain)


def fast_steps(tokens, routes, gate_code, gate_table, w_gate, w_up, w_down, norm_gain):
    own_rows = tokens[0]
    tok, feat_width = own_rows.shape
    experts = lax.axis_size("expert")
    ways = lax.axis_size("dp")
    capacity = 5 * tok // (2 * experts)
    chunk = feat_width // ways
    close, away = CLOSE + [0], AWAY
    early = (ways - 1,)
    late = tuple(range(ways - 2, -1, -1))

    route_rows = routes[0].T
    blocks = dispatch(
        pltpu.with_memory_space_constraint(route_rows, pltpu.HBM),
        pltpu.with_memory_space_constraint(own_rows, pltpu.HBM),
        experts, capacity,
    )
    near = swap_each({k: blocks[k] for k in close}, "expert")
    far = swap_each({k: blocks[k] for k in away}, "expert")
    select, weights = selector(route_rows, gate_code[0].T, gate_table, experts, capacity)
    matrices = w_gate[0].T, w_up[0].T, w_down[0]

    plan = [(j, early + late) for j in range(len(close))]
    _, *outputs = expert_call([near[k] for k in close], *matrices, plan, chunk)
    back = swap_each(dict(zip(close, outputs)), "expert")
    gain_own = gain_of(norm_gain, (0,), chunk)
    plan = [(j, early) for j in range(len(away))]
    hidden, *away_early = expert_call([far[k] for k in away], *matrices, plan, chunk)
    got_early = back | swap_each(dict(zip(away, away_early)), "expert")
    plan = [(j, late) for j in range(len(away))]
    away_late = down_call(hidden, matrices[2], len(away), plan, chunk)
    got_late = back | swap_each(dict(zip(away, away_late)), "expert")

    order = range(experts)
    first, part = combine_early(
        select, weights, [got_early[k] for k in order], chunk
    )
    raw = swap_each({early[0]: first}, "dp")
    gain_late = gain_of(norm_gain, late, chunk)
    *rest, total = combine_late(
        select, weights, part, gain_late, [got_late[k] for k in order], chunk, feat_width
    )
    ready = swap_each(dict(zip(late, rest)), "dp")
    sums = swap_each({k: total for k in early}, "dp")
    return finish(ready, raw, sums, gain_own, feat_width)[None]


def solution(mesh):
    in_specs = (
        P("expert", "dp", None),
        P("expert", "dp", None),
        P("expert", "dp", None),
        P(),
        P("expert", None, None),
        P("expert", None, None),
        P("expert", None, None),
        P(),
    )
    out_specs = P("expert", None, "dp")

    def whole(tokens, routes, gate_code, gate_table, w_gate, w_up, w_down, norm_gain):
        args = (tokens, routes, gate_code, gate_table, w_gate, w_up, w_down, norm_gain)
        experts, ways = mesh.shape["expert"], mesh.shape["dp"]
        tok, feat = tokens.shape[1] // ways, tokens.shape[2]
        power = experts & (experts - 1) == 0 and ways & (ways - 1) == 0
        fits = power and experts == 8 and ways == 4
        fits = fits and tok % 128 == 0 and w_gate.shape[0] == experts
        fits = fits and 5 * tok % (16 * experts) == 0 and feat % (256 * ways) == 0
        body = local_fast if fits else local_general
        f = jax.shard_map(body, mesh=mesh, in_specs=in_specs, out_specs=out_specs, check_vma=False)
        return f(*args)

    return whole
```

```python
import functools

import jax
import jax.numpy as jnp
from jax import lax
from jax.experimental import pallas as pl
from jax.experimental.pallas import tpu as pltpu
from jax.sharding import PartitionSpec as P


epsilon = 1e-06


F32 = jnp.float32
BF16 = jnp.bfloat16


def expert_ffn(slot_block, w_gate, w_up, w_down):
    shape_in = slot_block.shape
    flat_rows = slot_block.reshape(-1, shape_in[-1])
    gate_act = jnp.dot(flat_rows, w_gate[0], preferred_element_type=F32)
    up_act = jnp.dot(flat_rows, w_up[0], preferred_element_type=F32)
    hidden = (jax.nn.silu(gate_act) * up_act).astype(BF16)
    result = jnp.dot(hidden, w_down[0], preferred_element_type=F32).astype(BF16)
    return result.reshape(shape_in)


def lookup(codes, gate_table):
    levels = gate_table.shape[0]
    match = codes[:, None] == jnp.arange(levels, dtype=jnp.int32)[None, :]
    return jnp.sum(jnp.where(match, gate_table[None, :], 0.0), axis=1)


def combine_pairs(outputs, weights):
    combined = outputs[:, 0] * weights[:, 0:1] + outputs[:, 1] * weights[:, 1:2]
    rounded = lax.optimization_barrier(combined.astype(BF16))
    return rounded.astype(F32)


def local_general(tokens, routes, gate_code, gate_table, w_gate, w_up, w_down, norm_gain):
    own_rows = tokens[0]
    tok_count, feat_width = own_rows.shape
    experts = w_gate.shape[0] * lax.axis_size("expert")
    capacity = 5 * tok_count // (2 * experts)
    route_ids = routes[0].reshape(-1)
    onehot = (route_ids[:, None] == jnp.arange(experts, dtype=jnp.int32)[None, :]).astype(jnp.int32)
    slot_pos = jnp.sum((jnp.cumsum(onehot, axis=0) - onehot) * onehot, axis=1)
    position = route_ids * capacity + slot_pos
    owner_row = (
        jnp.zeros((experts * capacity,), jnp.int32)
        .at[position]
        .set(jnp.arange(2 * tok_count, dtype=jnp.int32) // 2)
    )
    filled = jnp.zeros((experts * capacity,), jnp.bool_).at[position].set(True)
    buffer = jnp.where(filled[:, None], own_rows[owner_row], jnp.zeros((), BF16))
    buffer = buffer.reshape(experts, capacity, feat_width)
    level_ids = gate_code[0].reshape(-1)
    received = lax.all_to_all(buffer, "expert", split_axis=0, concat_axis=0, tiled=True)
    expert_out = expert_ffn(received, w_gate, w_up, w_down)
    returned = lax.all_to_all(expert_out, "expert", split_axis=0, concat_axis=0, tiled=True)
    outputs = (
        returned.reshape(-1, feat_width)[position]
        .astype(F32)
        .reshape(tok_count, 2, feat_width)
    )
    weights = lookup(level_ids, gate_table).reshape(tok_count, 2)
    widened = combine_pairs(outputs, weights)
    inv_rms = lax.rsqrt(jnp.mean(widened * widened, axis=1, keepdims=True) + epsilon)
    normed = (widened * inv_rms * norm_gain[None, :]).astype(BF16)
    relaid = lax.all_to_all(normed, "dp", split_axis=1, concat_axis=0, tiled=True)
    return relaid[None]


OUT, BACK, AWAY = [2, 4, 3, 5, 1], [4, 2, 5, 3, 1], [6, 7]


def vmem():
    return pl.BlockSpec(memory_space=pltpu.VMEM)


def slot_rows(route_rows, experts, me):
    tok = route_rows.shape[1]
    ids = lax.broadcasted_iota(jnp.int32, (experts, tok), 0) ^ me
    named = (route_rows[0:1, :] == ids) | (route_rows[1:2, :] == ids)
    earlier = lax.broadcasted_iota(jnp.int32, (tok, tok), 0) < lax.broadcasted_iota(
        jnp.int32, (tok, tok), 1
    )
    count = jnp.dot(
        named.astype(F32).astype(BF16), earlier.astype(F32).astype(BF16),
        preferred_element_type=F32,
    )
    return jnp.where(named, count.astype(jnp.int32), -1), ids


def dispatch_body(experts, capacity, route_hbm, tok_hbm, *refs):
    *out_refs, route_ref, tok_ref, sems = refs
    copies = [
        pltpu.make_async_copy(route_hbm, route_ref, sems.at[0]),
        pltpu.make_async_copy(tok_hbm, tok_ref, sems.at[1]),
    ]
    for copy in copies:
        copy.start()
    me = lax.axis_index("expert")
    tok, width = tok_ref.shape
    lane = lax.broadcasted_iota(jnp.int32, (capacity, tok), 0)
    copies[0].wait()
    slots, _ = slot_rows(route_ref[...], experts, me)
    pick = jnp.concatenate(
        [(lane == slots[j : j + 1, :]).astype(F32) for j in range(experts)], axis=0
    ).astype(BF16)
    copies[1].wait()
    tile = 256
    for col in range(0, width, tile):
        rows = jnp.dot(pick, tok_ref[:, col : col + tile], preferred_element_type=F32)
        rows = rows.astype(BF16)
        for j in range(experts):
            out_refs[j][:, col : col + tile] = rows[j * capacity : (j + 1) * capacity, :]


def dispatch(route_rows, own_rows, experts, capacity):
    width = own_rows.shape[1]
    return pl.pallas_call(
        functools.partial(dispatch_body, experts, capacity),
        out_shape=[jax.ShapeDtypeStruct((capacity, width), BF16)] * experts,
        in_specs=[pl.BlockSpec(memory_space=pltpu.HBM)] * 2,
        out_specs=[vmem()] * experts,
        scratch_shapes=[
            pltpu.VMEM(route_rows.shape, jnp.int32),
            pltpu.VMEM(own_rows.shape, BF16),
            pltpu.SemaphoreType.DMA((2,)),
        ],
        name="dispatch",
        cost_estimate=pl.CostEstimate(flops=10**8, transcendentals=0, bytes_accessed=2 * 10**6),
        compiler_params=pltpu.CompilerParams(vmem_limit_bytes=16 * 2**20),
    )(route_rows, own_rows)


def selector_body(experts, capacity, route_ref, code_ref, table_ref, sel_ref, weight_ref):
    me = lax.axis_index("expert")
    rows = route_ref[...]
    slots, ids = slot_rows(rows, experts, me)
    tok = rows.shape[1]
    lane = lax.broadcasted_iota(jnp.int32, (capacity, tok), 0)
    for r in range(2):
        mine = jnp.where(rows[r : r + 1, :] == ids, slots, -1)
        pick = jnp.concatenate(
            [(lane == mine[j : j + 1, :]).astype(F32) for j in range(experts)], axis=0
        )
        sel_ref[r * tok : (r + 1) * tok, :] = pick.T.astype(BF16)
        codes = code_ref[r : r + 1, :]
        weights = jnp.zeros((1, tok), F32)
        for level in range(table_ref.shape[0]):
            weights = jnp.where(codes == level, table_ref[level], weights)
        weight_ref[r] = jnp.broadcast_to(weights, (tok, tok)).T


def selector(route_rows, code_rows, gate_table, experts, capacity):
    tok = route_rows.shape[1]
    return pl.pallas_call(
        functools.partial(selector_body, experts, capacity),
        out_shape=[
            jax.ShapeDtypeStruct((2 * tok, experts * capacity), BF16),
            jax.ShapeDtypeStruct((2, tok, tok), F32),
        ],
        in_specs=[vmem(), vmem(), pl.BlockSpec(memory_space=pltpu.SMEM)],
        out_specs=[vmem()] * 2,
        name="selector",
        cost_estimate=pl.CostEstimate(flops=2 * 10**10, transcendentals=0, bytes_accessed=10**8),
        compiler_params=pltpu.CompilerParams(vmem_limit_bytes=8 * 2**20),
    )(route_rows, code_rows, gate_table)


def chunk_columns(down_ref, offset, chunk):
    me, tile = lax.axis_index("dp"), 256
    for col in range(0, chunk, tile):
        start = pl.multiple_of((me ^ offset) * chunk + col, tile)
        yield col, tile, down_ref[:, pl.ds(start, tile)]


def write_down(hid_ref, down_ref, chunk, plan, out_refs):
    for offset in dict.fromkeys(k for _, offsets in plan for k in offsets):
        for col, tile, weight in chunk_columns(down_ref, offset, chunk):
            rows = jnp.dot(hid_ref[...], weight, preferred_element_type=F32).astype(BF16)
            for (j, offsets), out in zip(plan, out_refs):
                if offset in offsets:
                    capacity = out.shape[0]
                    at = offsets.index(offset) * chunk + col
                    out[:, at : at + tile] = rows[j * capacity : (j + 1) * capacity, :]


def expert_body(count, chunk, plan, *refs):
    blocks, (gate_ref, up_ref, down_ref) = refs[:count], refs[count : count + 3]
    hid_ref, x_ref, outs = refs[count + 3], refs[-1], refs[count + 4 : -1]
    capacity = blocks[0].shape[0]
    for j, block in enumerate(blocks):
        x_ref[j * capacity : (j + 1) * capacity, :] = block[...]
    hid = gate_ref.shape[0]
    tile = 256
    over = (((1,), (1,)), ((), ()))
    for low in range(0, hid, tile):
        high = min(hid, low + tile)
        gate = lax.dot_general(x_ref[...], gate_ref[low:high, :], over, preferred_element_type=F32)
        up = lax.dot_general(x_ref[...], up_ref[low:high, :], over, preferred_element_type=F32)
        hid_ref[:, low:high] = (gate / (1.0 + jnp.exp(-gate)) * up).astype(BF16)
    write_down(hid_ref, down_ref, chunk, plan, outs)


def expert_call(blocks, gate_rows, up_rows, down_rows, plan, chunk):
    count = len(blocks)
    capacity, width = blocks[0].shape
    rows, hid = capacity * count, gate_rows.shape[0]
    shapes = [jax.ShapeDtypeStruct((capacity, chunk * len(offsets)), BF16) for _, offsets in plan]
    return pl.pallas_call(
        functools.partial(expert_body, count, chunk, plan),
        out_shape=[jax.ShapeDtypeStruct((rows, hid), BF16)] + shapes,
        in_specs=[vmem()] * (count + 3),
        out_specs=[vmem()] * (1 + len(shapes)),
        scratch_shapes=[pltpu.VMEM((rows, width), BF16)],
        cost_estimate=pl.CostEstimate(
            flops=5 * rows * hid * width, transcendentals=rows * hid, bytes_accessed=8 * 10**6
        ),
        compiler_params=pltpu.CompilerParams(vmem_limit_bytes=24 * 2**20),
    )(*blocks, gate_rows, up_rows, down_rows)


def down_body(chunk, plan, hid_ref, down_ref, *out_refs):
    write_down(hid_ref, down_ref, chunk, plan, out_refs)


def down_call(hidden, down_rows, count, plan, chunk):
    rows, hid = hidden.shape
    return pl.pallas_call(
        functools.partial(down_body, chunk, plan),
        out_shape=[
            jax.ShapeDtypeStruct((rows // count, chunk * len(offsets)), BF16) for _, offsets in plan
        ],
        in_specs=[vmem()] * 2,
        out_specs=[vmem()] * len(plan),
        cost_estimate=pl.CostEstimate(
            flops=2 * rows * hid * chunk, transcendentals=0, bytes_accessed=3 * 10**6
        ),
        compiler_params=pltpu.CompilerParams(vmem_limit_bytes=16 * 2**20),
    )(hidden, down_rows)


def gather_blocks(blocks, y_ref, low):
    capacity, width = blocks[0].shape[0], y_ref.shape[1]
    for j, block in enumerate(blocks):
        start = low if block.shape[1] > width else 0
        y_ref[j * capacity : (j + 1) * capacity, :] = block[:, start : start + width]


def combine_chunk(sel_ref, weight_ref, y_ref, low, out_ref, squares):
    tok, lanes = squares.shape
    chunk, tile = out_ref.shape[1], 256
    for col in range(0, chunk, tile):
        picked = jnp.dot(
            sel_ref[...], y_ref[:, low + col : low + col + tile], preferred_element_type=F32
        )
        for at in range(0, tile, lanes):
            first = picked[:tok, at : at + lanes] * weight_ref[0]
            second = picked[tok:, at : at + lanes] * weight_ref[1]
            rounded = (first + second).astype(BF16)
            out_ref[:, col + at : col + at + lanes] = rounded
            wide = rounded.astype(F32)
            squares = squares + wide * wide
    return squares


def early_body(count, sel_ref, weight_ref, *refs):
    blocks, (out_ref, sum_ref, y_ref) = refs[:count], refs[count:]
    gather_blocks(blocks, y_ref, 0)
    squares = jnp.zeros(sum_ref.shape, F32)
    sum_ref[...] = combine_chunk(sel_ref, weight_ref, y_ref, 0, out_ref, squares)


def combine_early(select, weights, blocks, width):
    rows, tok = blocks[0].shape[0] * len(blocks), weights.shape[1]
    return pl.pallas_call(
        functools.partial(early_body, len(blocks)),
        out_shape=[
            jax.ShapeDtypeStruct((tok, width), BF16),
            jax.ShapeDtypeStruct((tok, weights.shape[2]), F32),
        ],
        in_specs=[vmem()] * (2 + len(blocks)),
        out_specs=[vmem()] * 2,
        scratch_shapes=[pltpu.VMEM((rows, width), BF16)],
        name="combine_early",
        cost_estimate=pl.CostEstimate(
            flops=4 * tok * rows * width, transcendentals=0, bytes_accessed=10**6
        ),
        compiler_params=pltpu.CompilerParams(vmem_limit_bytes=12 * 2**20),
    )(select, weights, *blocks)


def late_body(count, feat_width, sel_ref, weight_ref, part_ref, gain_ref, *refs):
    blocks, y_ref, outs, sum_ref = refs[:count], refs[-1], refs[count:-2], refs[-2]
    chunk = outs[0].shape[1]
    gather_blocks(blocks, y_ref, feat_width - chunk * len(outs))
    squares = part_ref[...]
    for q, out in enumerate(outs):
        squares = combine_chunk(sel_ref, weight_ref, y_ref, q * chunk, out, squares)
    total = jnp.sum(squares, axis=1, keepdims=True)
    tok = total.shape[0]
    sum_ref[...] = jnp.broadcast_to(total, (tok, tok)).T[0:8, :]
    inv = lax.rsqrt(total * (1.0 / feat_width) + epsilon)
    for q, out in enumerate(outs):
        gain = gain_ref[0:1, q * chunk : (q + 1) * chunk]
        out[...] = (out[...].astype(F32) * inv * gain).astype(BF16)


def combine_late(select, weights, part, gain, blocks, chunk, feat_width):
    width = gain.shape[1]
    rows, tok = blocks[0].shape[0] * len(blocks), weights.shape[1]
    return pl.pallas_call(
        functools.partial(late_body, len(blocks), feat_width),
        out_shape=[jax.ShapeDtypeStruct((tok, chunk), BF16)] * (width // chunk)
        + [jax.ShapeDtypeStruct((8, tok), F32)],
        in_specs=[vmem()] * (4 + len(blocks)),
        out_specs=[vmem()] * (width // chunk + 1),
        scratch_shapes=[pltpu.VMEM((rows, width), BF16)],
        name="combine_late",
        cost_estimate=pl.CostEstimate(
            flops=4 * tok * rows * width, transcendentals=0, bytes_accessed=2 * 10**6
        ),
        compiler_params=pltpu.CompilerParams(vmem_limit_bytes=12 * 2**20),
    )(select, weights, part, gain, *blocks)


def gain_body(offsets, gain_ref, out_ref):
    chunk = out_ref.shape[1] // len(offsets)
    me = lax.axis_index("dp")
    for q, offset in enumerate(offsets):
        start = pl.multiple_of((me ^ offset) * chunk, 128)
        row = gain_ref[:, pl.ds(start, chunk)]
        out_ref[:, q * chunk : (q + 1) * chunk] = jnp.broadcast_to(row, (8, chunk))


def gain_of(norm_gain, offsets, chunk):
    return pl.pallas_call(
        functools.partial(gain_body, offsets),
        out_shape=jax.ShapeDtypeStruct((8, chunk * len(offsets)), F32),
        in_specs=[vmem()],
        out_specs=vmem(),
        cost_estimate=pl.CostEstimate(flops=10**4, transcendentals=0, bytes_accessed=10**4),
        compiler_params=pltpu.CompilerParams(vmem_limit_bytes=2**20),
    )(norm_gain[None, :])


def finish_body(feat_width, ready, raw, *refs):
    ways = len(ready) + len(raw)
    chunks, sums = refs[:ways], refs[ways : ways + len(raw)]
    gain_ref, out_ref, scratch, sems = refs[ways + len(raw) :]
    me = lax.axis_index("dp")
    tok = chunks[0].shape[0]

    def put(source, k):
        rows = pl.ds(pl.multiple_of((me ^ k) * tok, tok), tok)
        copy = pltpu.make_async_copy(source, out_ref.at[rows, :], sems.at[k])
        copy.start()
        return copy

    copies = [put(chunks[i], k) for i, k in enumerate(ready)]
    for i, k in enumerate(raw):
        inv = lax.rsqrt(sums[i][0:1, :] * (1.0 / feat_width) + epsilon)
        column = jnp.broadcast_to(inv, (tok, tok)).T[:, 0:1]
        value = chunks[len(ready) + i][...].astype(F32) * column * gain_ref[0:1, :]
        scratch[i] = value.astype(BF16)
        copies.append(put(scratch.at[i], k))
    for copy in copies:
        copy.wait()


def finish(ready, raw, sums, gain, feat_width):
    first = next(iter(ready.values()))
    tok, width = first.shape
    ways = len(ready) + len(raw)
    return pl.pallas_call(
        functools.partial(finish_body, feat_width, tuple(ready), tuple(raw)),
        out_shape=jax.ShapeDtypeStruct((tok * ways, width), BF16),
        in_specs=[vmem()] * (ways + len(raw) + 1),
        out_specs=pl.BlockSpec(memory_space=pltpu.HBM),
        scratch_shapes=[
            pltpu.VMEM((len(raw), tok, width), BF16),
            pltpu.SemaphoreType.DMA((ways,)),
        ],
        name="finish",
        cost_estimate=pl.CostEstimate(flops=10**6, transcendentals=0, bytes_accessed=10**6),
        compiler_params=pltpu.CompilerParams(vmem_limit_bytes=8 * 2**20),
    )(*ready.values(), *raw.values(), *[sums[k] for k in raw], gain)


def swap(value, axis, offset):
    size = lax.axis_size(axis)
    return lax.ppermute(value, axis, [(i, i ^ offset) for i in range(size)])


def swap_each(values, axis):
    moved = {}
    for k, value in values.items():
        moved[k] = swap(value, axis, k) if k else value
    return moved


def local_fast(tokens, routes, gate_code, gate_table, w_gate, w_up, w_down, norm_gain):
    return fast_steps(tokens, routes, gate_code, gate_table, w_gate, w_up, w_down, norm_gain)


def fast_steps(tokens, routes, gate_code, gate_table, w_gate, w_up, w_down, norm_gain):
    own_rows = tokens[0]
    tok, feat_width = own_rows.shape
    experts = lax.axis_size("expert")
    ways = lax.axis_size("dp")
    capacity = 5 * tok // (2 * experts)
    chunk = feat_width // ways
    close, away = BACK + [0], AWAY
    early = (ways // 2,)
    late = tuple(k for k in range(ways - 1, -1, -1) if k not in early)

    route_rows = routes[0].T
    blocks = dispatch(
        pltpu.with_memory_space_constraint(route_rows, pltpu.HBM),
        pltpu.with_memory_space_constraint(own_rows, pltpu.HBM),
        experts, capacity,
    )
    near = swap_each({k: blocks[k] for k in OUT + [0]}, "expert")
    far = swap_each({k: blocks[k] for k in away}, "expert")
    select, weights = selector(route_rows, gate_code[0].T, gate_table, experts, capacity)
    matrices = w_gate[0].T, w_up[0].T, w_down[0]

    plan = [(j, early + late) for j in range(len(close))]
    _, *outputs = expert_call([near[k] for k in close], *matrices, plan, chunk)
    back = swap_each(dict(zip(close, outputs)), "expert")
    gain_own = gain_of(norm_gain, (0,), chunk)
    plan = [(j, early) for j in range(len(away))]
    hidden, *away_early = expert_call([far[k] for k in away], *matrices, plan, chunk)
    got_early = back | swap_each(dict(zip(away, away_early)), "expert")
    plan = [(j, late) for j in range(len(away))]
    away_late = down_call(hidden, matrices[2], len(away), plan, chunk)
    got_late = back | swap_each(dict(zip(away, away_late)), "expert")

    order = range(experts)
    first, part = combine_early(
        select, weights, [got_early[k] for k in order], chunk
    )
    raw = swap_each({early[0]: first}, "dp")
    gain_late = gain_of(norm_gain, late, chunk)
    *rest, total = combine_late(
        select, weights, part, gain_late, [got_late[k] for k in order], chunk, feat_width
    )
    ready = swap_each(dict(zip(late, rest)), "dp")
    sums = swap_each({k: total for k in early}, "dp")
    return finish(ready, raw, sums, gain_own, feat_width)[None]


def solution(mesh):
    in_specs = (
        P("expert", "dp", None),
        P("expert", "dp", None),
        P("expert", "dp", None),
        P(),
        P("expert", None, None),
        P("expert", None, None),
        P("expert", None, None),
        P(),
    )
    out_specs = P("expert", None, "dp")

    def whole(tokens, routes, gate_code, gate_table, w_gate, w_up, w_down, norm_gain):
        args = (tokens, routes, gate_code, gate_table, w_gate, w_up, w_down, norm_gain)
        experts, ways = mesh.shape["expert"], mesh.shape["dp"]
        tok, feat = tokens.shape[1] // ways, tokens.shape[2]
        power = experts & (experts - 1) == 0 and ways & (ways - 1) == 0
        fits = power and experts == 8 and ways == 4
        fits = fits and tok % 128 == 0 and w_gate.shape[0] == experts
        fits = fits and 5 * tok % (16 * experts) == 0 and feat % (256 * ways) == 0
        body = local_fast if fits else local_general
        f = jax.shard_map(body, mesh=mesh, in_specs=in_specs, out_specs=out_specs, check_vma=False)
        return f(*args)

    return whole
```

```python
import functools

import jax
import jax.numpy as jnp
from jax import lax
from jax.experimental import pallas as pl
from jax.experimental.pallas import tpu as pltpu
from jax.sharding import PartitionSpec as P


epsilon = 1e-06


F32 = jnp.float32
BF16 = jnp.bfloat16


def expert_ffn(slot_block, w_gate, w_up, w_down):
    shape_in = slot_block.shape
    flat_rows = slot_block.reshape(-1, shape_in[-1])
    gate_act = jnp.dot(flat_rows, w_gate[0], preferred_element_type=F32)
    up_act = jnp.dot(flat_rows, w_up[0], preferred_element_type=F32)
    hidden = (jax.nn.silu(gate_act) * up_act).astype(BF16)
    result = jnp.dot(hidden, w_down[0], preferred_element_type=F32).astype(BF16)
    return result.reshape(shape_in)


def lookup(codes, gate_table):
    levels = gate_table.shape[0]
    match = codes[:, None] == jnp.arange(levels, dtype=jnp.int32)[None, :]
    return jnp.sum(jnp.where(match, gate_table[None, :], 0.0), axis=1)


def combine_pairs(outputs, weights):
    combined = outputs[:, 0] * weights[:, 0:1] + outputs[:, 1] * weights[:, 1:2]
    rounded = lax.optimization_barrier(combined.astype(BF16))
    return rounded.astype(F32)


def local_general(tokens, routes, gate_code, gate_table, w_gate, w_up, w_down, norm_gain):
    own_rows = tokens[0]
    tok_count, feat_width = own_rows.shape
    experts = w_gate.shape[0] * lax.axis_size("expert")
    capacity = 5 * tok_count // (2 * experts)
    route_ids = routes[0].reshape(-1)
    onehot = (route_ids[:, None] == jnp.arange(experts, dtype=jnp.int32)[None, :]).astype(jnp.int32)
    slot_pos = jnp.sum((jnp.cumsum(onehot, axis=0) - onehot) * onehot, axis=1)
    position = route_ids * capacity + slot_pos
    owner_row = (
        jnp.zeros((experts * capacity,), jnp.int32)
        .at[position]
        .set(jnp.arange(2 * tok_count, dtype=jnp.int32) // 2)
    )
    filled = jnp.zeros((experts * capacity,), jnp.bool_).at[position].set(True)
    buffer = jnp.where(filled[:, None], own_rows[owner_row], jnp.zeros((), BF16))
    buffer = buffer.reshape(experts, capacity, feat_width)
    level_ids = gate_code[0].reshape(-1)
    received = lax.all_to_all(buffer, "expert", split_axis=0, concat_axis=0, tiled=True)
    expert_out = expert_ffn(received, w_gate, w_up, w_down)
    returned = lax.all_to_all(expert_out, "expert", split_axis=0, concat_axis=0, tiled=True)
    outputs = (
        returned.reshape(-1, feat_width)[position]
        .astype(F32)
        .reshape(tok_count, 2, feat_width)
    )
    weights = lookup(level_ids, gate_table).reshape(tok_count, 2)
    widened = combine_pairs(outputs, weights)
    inv_rms = lax.rsqrt(jnp.mean(widened * widened, axis=1, keepdims=True) + epsilon)
    normed = (widened * inv_rms * norm_gain[None, :]).astype(BF16)
    relaid = lax.all_to_all(normed, "dp", split_axis=1, concat_axis=0, tiled=True)
    return relaid[None]


CLOSE, AWAY = [4, 2, 5, 3, 1], [6, 7]


def vmem():
    return pl.BlockSpec(memory_space=pltpu.VMEM)


def slot_rows(route_rows, experts, me):
    tok = route_rows.shape[1]
    ids = lax.broadcasted_iota(jnp.int32, (experts, tok), 0) ^ me
    named = (route_rows[0:1, :] == ids) | (route_rows[1:2, :] == ids)
    earlier = lax.broadcasted_iota(jnp.int32, (tok, tok), 0) < lax.broadcasted_iota(
        jnp.int32, (tok, tok), 1
    )
    count = jnp.dot(
        named.astype(F32).astype(BF16), earlier.astype(F32).astype(BF16),
        preferred_element_type=F32,
    )
    return jnp.where(named, count.astype(jnp.int32), -1), ids


def dispatch_body(experts, capacity, route_hbm, tok_hbm, *refs):
    *out_refs, route_ref, tok_ref, sems = refs
    tok, width = tok_ref.shape
    pieces = sems.shape[0] - 1
    step = width // pieces
    route_copy = pltpu.make_async_copy(route_hbm, route_ref, sems.at[pieces])
    route_copy.start()
    copies = []
    for p in range(pieces):
        cols = pl.ds(p * step, step)
        copies.append(pltpu.make_async_copy(tok_hbm.at[:, cols], tok_ref.at[:, cols], sems.at[p]))
        copies[-1].start()
    me = lax.axis_index("expert")
    lane = lax.broadcasted_iota(jnp.int32, (capacity, tok), 0)
    route_copy.wait()
    slots, _ = slot_rows(route_ref[...], experts, me)
    pick = jnp.concatenate(
        [(lane == slots[j : j + 1, :]).astype(F32) for j in range(experts)], axis=0
    ).astype(BF16)
    tile = 256
    for p, copy in enumerate(copies):
        copy.wait()
        for col in range(p * step, (p + 1) * step, tile):
            rows = jnp.dot(pick, tok_ref[:, col : col + tile], preferred_element_type=F32)
            rows = rows.astype(BF16)
            for j in range(experts):
                out_refs[j][:, col : col + tile] = rows[j * capacity : (j + 1) * capacity, :]


def dispatch(route_rows, own_rows, experts, capacity):
    width = own_rows.shape[1]
    return pl.pallas_call(
        functools.partial(dispatch_body, experts, capacity),
        out_shape=[jax.ShapeDtypeStruct((capacity, width), BF16)] * experts,
        in_specs=[pl.BlockSpec(memory_space=pltpu.HBM)] * 2,
        out_specs=[vmem()] * experts,
        scratch_shapes=[
            pltpu.VMEM(route_rows.shape, jnp.int32),
            pltpu.VMEM(own_rows.shape, BF16),
            pltpu.SemaphoreType.DMA((5,)),
        ],
        name="dispatch",
        cost_estimate=pl.CostEstimate(flops=10**8, transcendentals=0, bytes_accessed=2 * 10**6),
        compiler_params=pltpu.CompilerParams(vmem_limit_bytes=16 * 2**20),
    )(route_rows, own_rows)


def selector_body(experts, capacity, route_ref, code_ref, table_ref, *refs):
    sel_ref, close_ref, away_ref, weight_ref = refs
    me = lax.axis_index("expert")
    rows = route_ref[...]
    slots, ids = slot_rows(rows, experts, me)
    tok = rows.shape[1]
    lane = lax.broadcasted_iota(jnp.int32, (capacity, tok), 0)
    for r in range(2):
        mine = jnp.where(rows[r : r + 1, :] == ids, slots, -1)
        pick = jnp.concatenate(
            [(lane == mine[j : j + 1, :]).astype(F32) for j in range(experts)], axis=0
        )
        held = slice(r * tok, (r + 1) * tok)
        split = close_ref.shape[1]
        sel_ref[held, :] = pick.T.astype(BF16)
        close_ref[held, :] = pick[:split].T.astype(BF16)
        away_ref[held, :] = pick[split:].T.astype(BF16)
        codes = code_ref[r : r + 1, :]
        weights = jnp.zeros((1, tok), F32)
        for level in range(table_ref.shape[0]):
            weights = jnp.where(codes == level, table_ref[level], weights)
        weight_ref[r] = jnp.broadcast_to(weights, (tok, tok)).T


def selector(route_rows, code_rows, gate_table, experts, capacity):
    tok = route_rows.shape[1]
    counts = (experts, experts - len(AWAY), len(AWAY))
    return pl.pallas_call(
        functools.partial(selector_body, experts, capacity),
        out_shape=[
            *[jax.ShapeDtypeStruct((2 * tok, n * capacity), BF16) for n in counts],
            jax.ShapeDtypeStruct((2, tok, tok), F32),
        ],
        in_specs=[vmem(), vmem(), pl.BlockSpec(memory_space=pltpu.SMEM)],
        out_specs=[vmem()] * 4,
        name="selector",
        cost_estimate=pl.CostEstimate(flops=2 * 10**10, transcendentals=0, bytes_accessed=10**8),
        compiler_params=pltpu.CompilerParams(vmem_limit_bytes=8 * 2**20),
    )(route_rows, code_rows, gate_table)


def chunk_columns(down_ref, offset, chunk):
    me, tile = lax.axis_index("dp"), 256
    for col in range(0, chunk, tile):
        start = pl.multiple_of((me ^ offset) * chunk + col, tile)
        yield col, tile, down_ref[:, pl.ds(start, tile)]


def write_down(hid_ref, down_ref, chunk, plan, out_refs):
    for offset in dict.fromkeys(k for _, offsets in plan for k in offsets):
        for col, tile, weight in chunk_columns(down_ref, offset, chunk):
            rows = jnp.dot(hid_ref[...], weight, preferred_element_type=F32).astype(BF16)
            for (j, offsets), out in zip(plan, out_refs):
                if offset in offsets:
                    capacity = out.shape[0]
                    at = offsets.index(offset) * chunk + col
                    out[:, at : at + tile] = rows[j * capacity : (j + 1) * capacity, :]


def expert_body(count, chunk, plan, *refs):
    blocks, (gate_ref, up_ref, down_ref) = refs[:count], refs[count : count + 3]
    hid_ref, x_ref, outs = refs[count + 3], refs[-1], refs[count + 4 : -1]
    capacity = blocks[0].shape[0]
    for j, block in enumerate(blocks):
        x_ref[j * capacity : (j + 1) * capacity, :] = block[...]
    hid = gate_ref.shape[0]
    tile = 256
    over = (((1,), (1,)), ((), ()))
    for low in range(0, hid, tile):
        high = min(hid, low + tile)
        gate = lax.dot_general(x_ref[...], gate_ref[low:high, :], over, preferred_element_type=F32)
        up = lax.dot_general(x_ref[...], up_ref[low:high, :], over, preferred_element_type=F32)
        hid_ref[:, low:high] = (gate / (1.0 + jnp.exp(-gate)) * up).astype(BF16)
    write_down(hid_ref, down_ref, chunk, plan, outs)


def expert_call(blocks, gate_rows, up_rows, down_rows, plan, chunk):
    count = len(blocks)
    capacity, width = blocks[0].shape
    rows, hid = capacity * count, gate_rows.shape[0]
    shapes = [jax.ShapeDtypeStruct((capacity, chunk * len(offsets)), BF16) for _, offsets in plan]
    return pl.pallas_call(
        functools.partial(expert_body, count, chunk, plan),
        out_shape=[jax.ShapeDtypeStruct((rows, hid), BF16)] + shapes,
        in_specs=[vmem()] * (count + 3),
        out_specs=[vmem()] * (1 + len(shapes)),
        scratch_shapes=[pltpu.VMEM((rows, width), BF16)],
        cost_estimate=pl.CostEstimate(
            flops=5 * rows * hid * width, transcendentals=rows * hid, bytes_accessed=8 * 10**6
        ),
        compiler_params=pltpu.CompilerParams(vmem_limit_bytes=24 * 2**20),
    )(*blocks, gate_rows, up_rows, down_rows)


def down_body(chunk, plan, hid_ref, down_ref, *out_refs):
    write_down(hid_ref, down_ref, chunk, plan, out_refs)


def down_call(hidden, down_rows, count, plan, chunk):
    rows, hid = hidden.shape
    return pl.pallas_call(
        functools.partial(down_body, chunk, plan),
        out_shape=[
            jax.ShapeDtypeStruct((rows // count, chunk * len(offsets)), BF16) for _, offsets in plan
        ],
        in_specs=[vmem()] * 2,
        out_specs=[vmem()] * len(plan),
        cost_estimate=pl.CostEstimate(
            flops=2 * rows * hid * chunk, transcendentals=0, bytes_accessed=3 * 10**6
        ),
        compiler_params=pltpu.CompilerParams(vmem_limit_bytes=16 * 2**20),
    )(hidden, down_rows)


def gather_blocks(blocks, y_ref, low):
    capacity, width = blocks[0].shape[0], y_ref.shape[1]
    for j, block in enumerate(blocks):
        start = low if block.shape[1] > width else 0
        y_ref[j * capacity : (j + 1) * capacity, :] = block[:, start : start + width]


def weighted(sel_ref, weight_ref, y_ref, low, tile):
    tok, lanes = weight_ref.shape[1:]
    picked = jnp.dot(sel_ref[...], y_ref[:, low : low + tile], preferred_element_type=F32)
    for at in range(0, tile, lanes):
        first = picked[:tok, at : at + lanes] * weight_ref[0]
        second = picked[tok:, at : at + lanes] * weight_ref[1]
        yield slice(low + at, low + at + lanes), first + second


def early_body(count, sel_ref, weight_ref, *refs):
    blocks, (out_ref, sum_ref, y_ref) = refs[:count], refs[count:]
    gather_blocks(blocks, y_ref, 0)
    squares = jnp.zeros(sum_ref.shape, F32)
    for low in range(0, y_ref.shape[1], 256):
        for cols, combined in weighted(sel_ref, weight_ref, y_ref, low, 256):
            rounded = combined.astype(BF16)
            out_ref[:, cols] = rounded
            squares = squares + rounded.astype(F32) * rounded.astype(F32)
    sum_ref[...] = squares


def combine_early(select, weights, blocks, width):
    rows, tok = blocks[0].shape[0] * len(blocks), weights.shape[1]
    return pl.pallas_call(
        functools.partial(early_body, len(blocks)),
        out_shape=[
            jax.ShapeDtypeStruct((tok, width), BF16),
            jax.ShapeDtypeStruct((tok, weights.shape[2]), F32),
        ],
        in_specs=[vmem()] * (2 + len(blocks)),
        out_specs=[vmem()] * 2,
        scratch_shapes=[pltpu.VMEM((rows, width), BF16)],
        name="combine_early",
        cost_estimate=pl.CostEstimate(
            flops=4 * tok * rows * width, transcendentals=0, bytes_accessed=10**6
        ),
        compiler_params=pltpu.CompilerParams(vmem_limit_bytes=12 * 2**20),
    )(select, weights, *blocks)


def mid_body(count, low, sel_ref, weight_ref, *refs):
    blocks, (out_ref, y_ref) = refs[:count], refs[count:]
    gather_blocks(blocks, y_ref, low)
    for col in range(0, y_ref.shape[1], 256):
        for cols, combined in weighted(sel_ref, weight_ref, y_ref, col, 256):
            out_ref[:, cols] = combined


def combine_mid(select, weights, blocks, low):
    capacity, width = blocks[0].shape
    rows, tok, width = capacity * len(blocks), weights.shape[1], width - low
    return pl.pallas_call(
        functools.partial(mid_body, len(blocks), low),
        out_shape=jax.ShapeDtypeStruct((tok, width), F32),
        in_specs=[vmem()] * (2 + len(blocks)),
        out_specs=vmem(),
        scratch_shapes=[pltpu.VMEM((rows, width), BF16)],
        name="combine_mid",
        cost_estimate=pl.CostEstimate(
            flops=4 * tok * rows * width, transcendentals=0, bytes_accessed=2 * 10**6
        ),
        compiler_params=pltpu.CompilerParams(vmem_limit_bytes=12 * 2**20),
    )(select, weights, *blocks)


def late_body(count, feat_width, sel_ref, weight_ref, begun_ref, part_ref, gain_ref, *refs):
    blocks, y_ref, outs, sum_ref = refs[:count], refs[-1], refs[count:-2], refs[-2]
    chunk = outs[0].shape[1]
    gather_blocks(blocks, y_ref, 0)
    squares = part_ref[...]
    for low in range(0, y_ref.shape[1], 256):
        for cols, combined in weighted(sel_ref, weight_ref, y_ref, low, 256):
            rounded = (begun_ref[:, cols] + combined).astype(BF16)
            at = cols.start % chunk
            outs[cols.start // chunk][:, at : at + cols.stop - cols.start] = rounded
            squares = squares + rounded.astype(F32) * rounded.astype(F32)
    total = jnp.sum(squares, axis=1, keepdims=True)
    tok = total.shape[0]
    sum_ref[...] = jnp.broadcast_to(total, (tok, tok)).T[0:8, :]
    inv = lax.rsqrt(total * (1.0 / feat_width) + epsilon)
    for q, out in enumerate(outs):
        gain = gain_ref[0:1, q * chunk : (q + 1) * chunk]
        out[...] = (out[...].astype(F32) * inv * gain).astype(BF16)


def combine_late(select, weights, begun, part, gain, blocks, chunk, feat_width):
    capacity, width = blocks[0].shape
    rows, tok = capacity * len(blocks), weights.shape[1]
    return pl.pallas_call(
        functools.partial(late_body, len(blocks), feat_width),
        out_shape=[jax.ShapeDtypeStruct((tok, chunk), BF16)] * (width // chunk)
        + [jax.ShapeDtypeStruct((8, tok), F32)],
        in_specs=[vmem()] * (5 + len(blocks)),
        out_specs=[vmem()] * (width // chunk + 1),
        scratch_shapes=[pltpu.VMEM((rows, width), BF16)],
        name="combine_late",
        cost_estimate=pl.CostEstimate(
            flops=4 * tok * rows * width, transcendentals=0, bytes_accessed=2 * 10**6
        ),
        compiler_params=pltpu.CompilerParams(vmem_limit_bytes=12 * 2**20),
    )(select, weights, begun, part, gain, *blocks)


def gain_body(offsets, gain_ref, out_ref):
    chunk = out_ref.shape[1] // len(offsets)
    me = lax.axis_index("dp")
    for q, offset in enumerate(offsets):
        start = pl.multiple_of((me ^ offset) * chunk, 128)
        row = gain_ref[:, pl.ds(start, chunk)]
        out_ref[:, q * chunk : (q + 1) * chunk] = jnp.broadcast_to(row, (8, chunk))


def gain_of(norm_gain, offsets, chunk):
    return pl.pallas_call(
        functools.partial(gain_body, offsets),
        out_shape=jax.ShapeDtypeStruct((8, chunk * len(offsets)), F32),
        in_specs=[vmem()],
        out_specs=vmem(),
        cost_estimate=pl.CostEstimate(flops=10**4, transcendentals=0, bytes_accessed=10**4),
        compiler_params=pltpu.CompilerParams(vmem_limit_bytes=2**20),
    )(norm_gain[None, :])


def scale_body(feat_width, chunk_ref, sum_ref, gain_ref, out_ref):
    tok = chunk_ref.shape[0]
    inv = lax.rsqrt(sum_ref[0:1, :] * (1.0 / feat_width) + epsilon)
    column = jnp.broadcast_to(inv, (tok, tok)).T[:, 0:1]
    out_ref[...] = (chunk_ref[...].astype(F32) * column * gain_ref[0:1, :]).astype(BF16)


def scale(chunk, total, gain, feat_width):
    return pl.pallas_call(
        functools.partial(scale_body, feat_width),
        out_shape=jax.ShapeDtypeStruct(chunk.shape, BF16),
        in_specs=[vmem()] * 3,
        out_specs=vmem(),
        name="scale",
        cost_estimate=pl.CostEstimate(flops=10**6, transcendentals=0, bytes_accessed=10**6),
        compiler_params=pltpu.CompilerParams(vmem_limit_bytes=4 * 2**20),
    )(chunk, total, gain)


def finish_body(*refs):
    *chunks, out_ref, sems = refs
    me = lax.axis_index("dp")
    tok = chunks[0].shape[0]
    copies = []
    for k, chunk in enumerate(chunks):
        rows = pl.ds(pl.multiple_of((me ^ k) * tok, tok), tok)
        copies.append(pltpu.make_async_copy(chunk, out_ref.at[rows, :], sems.at[k]))
        copies[-1].start()
    for copy in copies:
        copy.wait()


def finish(chunks):
    tok, width = chunks[0].shape
    return pl.pallas_call(
        finish_body,
        out_shape=jax.ShapeDtypeStruct((tok * len(chunks), width), BF16),
        in_specs=[vmem()] * len(chunks),
        out_specs=pl.BlockSpec(memory_space=pltpu.HBM),
        scratch_shapes=[pltpu.SemaphoreType.DMA((len(chunks),))],
        name="finish",
        cost_estimate=pl.CostEstimate(flops=10**6, transcendentals=0, bytes_accessed=10**6),
        compiler_params=pltpu.CompilerParams(vmem_limit_bytes=4 * 2**20),
    )(*chunks)


def swap(value, axis, offset):
    size = lax.axis_size(axis)
    return lax.ppermute(value, axis, [(i, i ^ offset) for i in range(size)])


def swap_each(values, axis):
    moved = {}
    for k, value in values.items():
        moved[k] = swap(value, axis, k) if k else value
    return moved


def local_fast(tokens, routes, gate_code, gate_table, w_gate, w_up, w_down, norm_gain):
    return fast_steps(tokens, routes, gate_code, gate_table, w_gate, w_up, w_down, norm_gain)


def fast_steps(tokens, routes, gate_code, gate_table, w_gate, w_up, w_down, norm_gain):
    own_rows = tokens[0]
    tok, feat_width = own_rows.shape
    experts = lax.axis_size("expert")
    ways = lax.axis_size("dp")
    capacity = 5 * tok // (2 * experts)
    chunk = feat_width // ways
    close, away = CLOSE + [0], AWAY
    early = (ways // 2,)
    late = tuple(k for k in range(ways - 1, -1, -1) if k not in early)

    route_rows = routes[0].T
    blocks = dispatch(
        pltpu.with_memory_space_constraint(route_rows, pltpu.HBM),
        pltpu.with_memory_space_constraint(own_rows, pltpu.HBM),
        experts, capacity,
    )
    near = swap_each({k: blocks[k] for k in close}, "expert")
    far = swap_each({k: blocks[k] for k in away}, "expert")
    select, select_close, select_away, weights = selector(route_rows, gate_code[0].T, gate_table, experts, capacity)
    matrices = w_gate[0].T, w_up[0].T, w_down[0]

    plan = [(j, early + late) for j in range(len(close))]
    _, *outputs = expert_call([near[k] for k in close], *matrices, plan, chunk)
    back = swap_each(dict(zip(close, outputs)), "expert")
    gain_own = gain_of(norm_gain, (0,), chunk)
    plan = [(j, early) for j in range(len(away))]
    hidden, *away_early = expert_call([far[k] for k in away], *matrices, plan, chunk)
    got_early = back | swap_each(dict(zip(away, away_early)), "expert")
    plan = [(j, late) for j in range(len(away))]
    away_late = down_call(hidden, matrices[2], len(away), plan, chunk)
    got_late = swap_each(dict(zip(away, away_late)), "expert")

    order = range(experts)
    first, part = combine_early(select, weights, [got_early[k] for k in order], chunk)
    raw = swap_each({early[0]: first}, "dp")
    gain_late = gain_of(norm_gain, late, chunk)
    begun = combine_mid(
        select_close, weights, [back[k] for k in order if k not in away], chunk * len(early)
    )
    *rest, total = combine_late(
        select_away, weights, begun, part, gain_late, [got_late[k] for k in away], chunk,
        feat_width,
    )
    chunks = swap_each(dict(zip(late, rest)), "dp")
    sums = swap_each({k: total for k in early}, "dp")
    for k in early:
        chunks[k] = scale(raw[k], sums[k], gain_own, feat_width)
    return finish([chunks[k] for k in range(ways)])[None]


def solution(mesh):
    in_specs = (
        P("expert", "dp", None),
        P("expert", "dp", None),
        P("expert", "dp", None),
        P(),
        P("expert", None, None),
        P("expert", None, None),
        P("expert", None, None),
        P(),
    )
    out_specs = P("expert", None, "dp")

    def whole(tokens, routes, gate_code, gate_table, w_gate, w_up, w_down, norm_gain):
        args = (tokens, routes, gate_code, gate_table, w_gate, w_up, w_down, norm_gain)
        experts, ways = mesh.shape["expert"], mesh.shape["dp"]
        tok, feat = tokens.shape[1] // ways, tokens.shape[2]
        power = experts & (experts - 1) == 0 and ways & (ways - 1) == 0
        fits = power and experts == 8 and ways == 4
        fits = fits and tok % 128 == 0 and w_gate.shape[0] == experts
        fits = fits and 5 * tok % (16 * experts) == 0 and feat % (256 * ways) == 0
        body = local_fast if fits else local_general
        f = jax.shard_map(body, mesh=mesh, in_specs=in_specs, out_specs=out_specs, check_vma=False)
        return f(*args)

    return whole
```

```python
import functools

import jax
import jax.numpy as jnp
from jax import lax
from jax.experimental import pallas as pl
from jax.experimental.pallas import tpu as pltpu
from jax.sharding import PartitionSpec as P


epsilon = 1e-06


F32 = jnp.float32
BF16 = jnp.bfloat16


def expert_ffn(slot_block, w_gate, w_up, w_down):
    shape_in = slot_block.shape
    flat_rows = slot_block.reshape(-1, shape_in[-1])
    gate_act = jnp.dot(flat_rows, w_gate[0], preferred_element_type=F32)
    up_act = jnp.dot(flat_rows, w_up[0], preferred_element_type=F32)
    hidden = (jax.nn.silu(gate_act) * up_act).astype(BF16)
    result = jnp.dot(hidden, w_down[0], preferred_element_type=F32).astype(BF16)
    return result.reshape(shape_in)


def lookup(codes, gate_table):
    levels = gate_table.shape[0]
    match = codes[:, None] == jnp.arange(levels, dtype=jnp.int32)[None, :]
    return jnp.sum(jnp.where(match, gate_table[None, :], 0.0), axis=1)


def combine_pairs(outputs, weights):
    combined = outputs[:, 0] * weights[:, 0:1] + outputs[:, 1] * weights[:, 1:2]
    rounded = lax.optimization_barrier(combined.astype(BF16))
    return rounded.astype(F32)


def local_general(tokens, routes, gate_code, gate_table, w_gate, w_up, w_down, norm_gain):
    own_rows = tokens[0]
    tok_count, feat_width = own_rows.shape
    experts = w_gate.shape[0] * lax.axis_size("expert")
    capacity = 5 * tok_count // (2 * experts)
    route_ids = routes[0].reshape(-1)
    onehot = (route_ids[:, None] == jnp.arange(experts, dtype=jnp.int32)[None, :]).astype(jnp.int32)
    slot_pos = jnp.sum((jnp.cumsum(onehot, axis=0) - onehot) * onehot, axis=1)
    position = route_ids * capacity + slot_pos
    owner_row = (
        jnp.zeros((experts * capacity,), jnp.int32)
        .at[position]
        .set(jnp.arange(2 * tok_count, dtype=jnp.int32) // 2)
    )
    filled = jnp.zeros((experts * capacity,), jnp.bool_).at[position].set(True)
    buffer = jnp.where(filled[:, None], own_rows[owner_row], jnp.zeros((), BF16))
    buffer = buffer.reshape(experts, capacity, feat_width)
    level_ids = gate_code[0].reshape(-1)
    received = lax.all_to_all(buffer, "expert", split_axis=0, concat_axis=0, tiled=True)
    expert_out = expert_ffn(received, w_gate, w_up, w_down)
    returned = lax.all_to_all(expert_out, "expert", split_axis=0, concat_axis=0, tiled=True)
    outputs = (
        returned.reshape(-1, feat_width)[position]
        .astype(F32)
        .reshape(tok_count, 2, feat_width)
    )
    weights = lookup(level_ids, gate_table).reshape(tok_count, 2)
    widened = combine_pairs(outputs, weights)
    inv_rms = lax.rsqrt(jnp.mean(widened * widened, axis=1, keepdims=True) + epsilon)
    normed = (widened * inv_rms * norm_gain[None, :]).astype(BF16)
    relaid = lax.all_to_all(normed, "dp", split_axis=1, concat_axis=0, tiled=True)
    return relaid[None]


CLOSE, AWAY = [4, 2, 5, 3, 1], [6, 7]


def vmem():
    return pl.BlockSpec(memory_space=pltpu.VMEM)


def slot_rows(route_rows, experts, me):
    tok = route_rows.shape[1]
    ids = lax.broadcasted_iota(jnp.int32, (experts, tok), 0) ^ me
    named = (route_rows[0:1, :] == ids) | (route_rows[1:2, :] == ids)
    earlier = lax.broadcasted_iota(jnp.int32, (tok, tok), 0) < lax.broadcasted_iota(
        jnp.int32, (tok, tok), 1
    )
    count = jnp.dot(
        named.astype(F32).astype(BF16), earlier.astype(F32).astype(BF16),
        preferred_element_type=F32,
    )
    return jnp.where(named, count.astype(jnp.int32), -1), ids


def dispatch_body(experts, capacity, route_hbm, tok_hbm, *refs):
    *out_refs, route_ref, tok_ref, sems = refs
    copies = [
        pltpu.make_async_copy(route_hbm, route_ref, sems.at[0]),
        pltpu.make_async_copy(tok_hbm, tok_ref, sems.at[1]),
    ]
    for copy in copies:
        copy.start()
    me = lax.axis_index("expert")
    tok, width = tok_ref.shape
    lane = lax.broadcasted_iota(jnp.int32, (capacity, tok), 0)
    copies[0].wait()
    slots, _ = slot_rows(route_ref[...], experts, me)
    pick = jnp.concatenate(
        [(lane == slots[j : j + 1, :]).astype(F32) for j in range(experts)], axis=0
    ).astype(BF16)
    copies[1].wait()
    tile = 256
    for col in range(0, width, tile):
        rows = jnp.dot(pick, tok_ref[:, col : col + tile], preferred_element_type=F32)
        rows = rows.astype(BF16)
        for j in range(experts):
            out_refs[j][:, col : col + tile] = rows[j * capacity : (j + 1) * capacity, :]


def dispatch(route_rows, own_rows, experts, capacity):
    width = own_rows.shape[1]
    return pl.pallas_call(
        functools.partial(dispatch_body, experts, capacity),
        out_shape=[jax.ShapeDtypeStruct((capacity, width), BF16)] * experts,
        in_specs=[pl.BlockSpec(memory_space=pltpu.HBM)] * 2,
        out_specs=[vmem()] * experts,
        scratch_shapes=[
            pltpu.VMEM(route_rows.shape, jnp.int32),
            pltpu.VMEM(own_rows.shape, BF16),
            pltpu.SemaphoreType.DMA((2,)),
        ],
        name="dispatch",
        cost_estimate=pl.CostEstimate(flops=10**8, transcendentals=0, bytes_accessed=2 * 10**6),
        compiler_params=pltpu.CompilerParams(vmem_limit_bytes=16 * 2**20),
    )(route_rows, own_rows)


def selector_body(experts, capacity, route_ref, code_ref, table_ref, *refs):
    sel_ref, close_ref, away_ref, weight_ref = refs
    me = lax.axis_index("expert")
    rows = route_ref[...]
    slots, ids = slot_rows(rows, experts, me)
    tok = rows.shape[1]
    lane = lax.broadcasted_iota(jnp.int32, (capacity, tok), 0)
    for r in range(2):
        mine = jnp.where(rows[r : r + 1, :] == ids, slots, -1)
        pick = jnp.concatenate(
            [(lane == mine[j : j + 1, :]).astype(F32) for j in range(experts)], axis=0
        )
        held = slice(r * tok, (r + 1) * tok)
        split = close_ref.shape[1]
        sel_ref[held, :] = pick.T.astype(BF16)
        close_ref[held, :] = pick[:split].T.astype(BF16)
        away_ref[held, :] = pick[split:].T.astype(BF16)
        codes = code_ref[r : r + 1, :]
        weights = jnp.zeros((1, tok), F32)
        for level in range(table_ref.shape[0]):
            weights = jnp.where(codes == level, table_ref[level], weights)
        weight_ref[r] = jnp.broadcast_to(weights, (tok, tok)).T


def selector(route_rows, code_rows, gate_table, experts, capacity):
    tok = route_rows.shape[1]
    counts = (experts, experts - len(AWAY), len(AWAY))
    return pl.pallas_call(
        functools.partial(selector_body, experts, capacity),
        out_shape=[
            *[jax.ShapeDtypeStruct((2 * tok, n * capacity), BF16) for n in counts],
            jax.ShapeDtypeStruct((2, tok, tok), F32),
        ],
        in_specs=[vmem(), vmem(), pl.BlockSpec(memory_space=pltpu.SMEM)],
        out_specs=[vmem()] * 4,
        name="selector",
        cost_estimate=pl.CostEstimate(flops=2 * 10**10, transcendentals=0, bytes_accessed=10**8),
        compiler_params=pltpu.CompilerParams(vmem_limit_bytes=8 * 2**20),
    )(route_rows, code_rows, gate_table)


def chunk_columns(down_ref, offset, chunk):
    me, tile = lax.axis_index("dp"), 256
    for col in range(0, chunk, tile):
        start = pl.multiple_of((me ^ offset) * chunk + col, tile)
        yield col, tile, down_ref[:, pl.ds(start, tile)]


def write_down(hid_ref, down_ref, chunk, plan, out_refs):
    for offset in dict.fromkeys(k for _, offsets in plan for k in offsets):
        for col, tile, weight in chunk_columns(down_ref, offset, chunk):
            rows = jnp.dot(hid_ref[...], weight, preferred_element_type=F32).astype(BF16)
            for (j, offsets), out in zip(plan, out_refs):
                if offset in offsets:
                    capacity = out.shape[0]
                    at = offsets.index(offset) * chunk + col
                    out[:, at : at + tile] = rows[j * capacity : (j + 1) * capacity, :]


def expert_body(count, chunk, plan, *refs):
    blocks, (gate_ref, up_ref, down_ref) = refs[:count], refs[count : count + 3]
    hid_ref, x_ref, outs = refs[count + 3], refs[-1], refs[count + 4 : -1]
    capacity = blocks[0].shape[0]
    for j, block in enumerate(blocks):
        x_ref[j * capacity : (j + 1) * capacity, :] = block[...]
    hid = gate_ref.shape[0]
    tile = 256
    over = (((1,), (1,)), ((), ()))
    for low in range(0, hid, tile):
        high = min(hid, low + tile)
        gate = lax.dot_general(x_ref[...], gate_ref[low:high, :], over, preferred_element_type=F32)
        up = lax.dot_general(x_ref[...], up_ref[low:high, :], over, preferred_element_type=F32)
        hid_ref[:, low:high] = (gate / (1.0 + jnp.exp(-gate)) * up).astype(BF16)
    write_down(hid_ref, down_ref, chunk, plan, outs)


def expert_call(blocks, gate_rows, up_rows, down_rows, plan, chunk):
    count = len(blocks)
    capacity, width = blocks[0].shape
    rows, hid = capacity * count, gate_rows.shape[0]
    shapes = [jax.ShapeDtypeStruct((capacity, chunk * len(offsets)), BF16) for _, offsets in plan]
    return pl.pallas_call(
        functools.partial(expert_body, count, chunk, plan),
        out_shape=[jax.ShapeDtypeStruct((rows, hid), BF16)] + shapes,
        in_specs=[vmem()] * (count + 3),
        out_specs=[vmem()] * (1 + len(shapes)),
        scratch_shapes=[pltpu.VMEM((rows, width), BF16)],
        cost_estimate=pl.CostEstimate(
            flops=5 * rows * hid * width, transcendentals=rows * hid, bytes_accessed=8 * 10**6
        ),
        compiler_params=pltpu.CompilerParams(vmem_limit_bytes=24 * 2**20),
    )(*blocks, gate_rows, up_rows, down_rows)


def down_body(chunk, plan, hid_ref, down_ref, *out_refs):
    write_down(hid_ref, down_ref, chunk, plan, out_refs)


def down_call(hidden, down_rows, count, plan, chunk):
    rows, hid = hidden.shape
    return pl.pallas_call(
        functools.partial(down_body, chunk, plan),
        out_shape=[
            jax.ShapeDtypeStruct((rows // count, chunk * len(offsets)), BF16) for _, offsets in plan
        ],
        in_specs=[vmem()] * 2,
        out_specs=[vmem()] * len(plan),
        cost_estimate=pl.CostEstimate(
            flops=2 * rows * hid * chunk, transcendentals=0, bytes_accessed=3 * 10**6
        ),
        compiler_params=pltpu.CompilerParams(vmem_limit_bytes=16 * 2**20),
    )(hidden, down_rows)


def gather_blocks(blocks, y_ref, low):
    capacity, width = blocks[0].shape[0], y_ref.shape[1]
    for j, block in enumerate(blocks):
        start = low if block.shape[1] > width else 0
        y_ref[j * capacity : (j + 1) * capacity, :] = block[:, start : start + width]


def weighted(sel_ref, weight_ref, y_ref, low, tile):
    tok, lanes = weight_ref.shape[1:]
    picked = jnp.dot(sel_ref[...], y_ref[:, low : low + tile], preferred_element_type=F32)
    for at in range(0, tile, lanes):
        first = picked[:tok, at : at + lanes] * weight_ref[0]
        second = picked[tok:, at : at + lanes] * weight_ref[1]
        yield slice(low + at, low + at + lanes), first + second


def early_body(count, sel_ref, weight_ref, *refs):
    blocks, (out_ref, sum_ref, y_ref) = refs[:count], refs[count:]
    gather_blocks(blocks, y_ref, 0)
    squares = jnp.zeros(sum_ref.shape, F32)
    for low in range(0, y_ref.shape[1], 256):
        for cols, combined in weighted(sel_ref, weight_ref, y_ref, low, 256):
            rounded = combined.astype(BF16)
            out_ref[:, cols] = rounded
            squares = squares + rounded.astype(F32) * rounded.astype(F32)
    sum_ref[...] = squares


def combine_early(select, weights, blocks, width):
    rows, tok = blocks[0].shape[0] * len(blocks), weights.shape[1]
    return pl.pallas_call(
        functools.partial(early_body, len(blocks)),
        out_shape=[
            jax.ShapeDtypeStruct((tok, width), BF16),
            jax.ShapeDtypeStruct((tok, weights.shape[2]), F32),
        ],
        in_specs=[vmem()] * (2 + len(blocks)),
        out_specs=[vmem()] * 2,
        scratch_shapes=[pltpu.VMEM((rows, width), BF16)],
        name="combine_early",
        cost_estimate=pl.CostEstimate(
            flops=4 * tok * rows * width, transcendentals=0, bytes_accessed=10**6
        ),
        compiler_params=pltpu.CompilerParams(vmem_limit_bytes=12 * 2**20),
    )(select, weights, *blocks)


def mid_body(count, low, sel_ref, weight_ref, *refs):
    blocks, (out_ref, y_ref) = refs[:count], refs[count:]
    gather_blocks(blocks, y_ref, low)
    for col in range(0, y_ref.shape[1], 256):
        for cols, combined in weighted(sel_ref, weight_ref, y_ref, col, 256):
            out_ref[:, cols] = combined


def combine_mid(select, weights, blocks, low):
    capacity, width = blocks[0].shape
    rows, tok, width = capacity * len(blocks), weights.shape[1], width - low
    return pl.pallas_call(
        functools.partial(mid_body, len(blocks), low),
        out_shape=jax.ShapeDtypeStruct((tok, width), F32),
        in_specs=[vmem()] * (2 + len(blocks)),
        out_specs=vmem(),
        scratch_shapes=[pltpu.VMEM((rows, width), BF16)],
        name="combine_mid",
        cost_estimate=pl.CostEstimate(
            flops=4 * tok * rows * width, transcendentals=0, bytes_accessed=2 * 10**6
        ),
        compiler_params=pltpu.CompilerParams(vmem_limit_bytes=12 * 2**20),
    )(select, weights, *blocks)


def late_body(count, feat_width, sel_ref, weight_ref, begun_ref, part_ref, gain_ref, *refs):
    blocks, y_ref, outs, sum_ref = refs[:count], refs[-1], refs[count:-2], refs[-2]
    chunk = outs[0].shape[1]
    gather_blocks(blocks, y_ref, 0)
    squares = part_ref[...]
    for low in range(0, y_ref.shape[1], 256):
        for cols, combined in weighted(sel_ref, weight_ref, y_ref, low, 256):
            rounded = (begun_ref[:, cols] + combined).astype(BF16)
            at = cols.start % chunk
            outs[cols.start // chunk][:, at : at + cols.stop - cols.start] = rounded
            squares = squares + rounded.astype(F32) * rounded.astype(F32)
    total = jnp.sum(squares, axis=1, keepdims=True)
    tok = total.shape[0]
    sum_ref[...] = jnp.broadcast_to(total, (tok, tok)).T[0:8, :]
    inv = lax.rsqrt(total * (1.0 / feat_width) + epsilon)
    for q, out in enumerate(outs):
        gain = gain_ref[0:1, q * chunk : (q + 1) * chunk]
        out[...] = (out[...].astype(F32) * inv * gain).astype(BF16)


def combine_late(select, weights, begun, part, gain, blocks, chunk, feat_width):
    capacity, width = blocks[0].shape
    rows, tok = capacity * len(blocks), weights.shape[1]
    return pl.pallas_call(
        functools.partial(late_body, len(blocks), feat_width),
        out_shape=[jax.ShapeDtypeStruct((tok, chunk), BF16)] * (width // chunk)
        + [jax.ShapeDtypeStruct((8, tok), F32)],
        in_specs=[vmem()] * (5 + len(blocks)),
        out_specs=[vmem()] * (width // chunk + 1),
        scratch_shapes=[pltpu.VMEM((rows, width), BF16)],
        name="combine_late",
        cost_estimate=pl.CostEstimate(
            flops=4 * tok * rows * width, transcendentals=0, bytes_accessed=2 * 10**6
        ),
        compiler_params=pltpu.CompilerParams(vmem_limit_bytes=12 * 2**20),
    )(select, weights, begun, part, gain, *blocks)


def gain_body(offsets, gain_ref, out_ref):
    chunk = out_ref.shape[1] // len(offsets)
    me = lax.axis_index("dp")
    for q, offset in enumerate(offsets):
        start = pl.multiple_of((me ^ offset) * chunk, 128)
        row = gain_ref[:, pl.ds(start, chunk)]
        out_ref[:, q * chunk : (q + 1) * chunk] = jnp.broadcast_to(row, (8, chunk))


def gain_of(norm_gain, offsets, chunk):
    return pl.pallas_call(
        functools.partial(gain_body, offsets),
        out_shape=jax.ShapeDtypeStruct((8, chunk * len(offsets)), F32),
        in_specs=[vmem()],
        out_specs=vmem(),
        cost_estimate=pl.CostEstimate(flops=10**4, transcendentals=0, bytes_accessed=10**4),
        compiler_params=pltpu.CompilerParams(vmem_limit_bytes=2**20),
    )(norm_gain[None, :])


def finish_body(feat_width, ready, raw, *refs):
    ways = len(ready) + len(raw)
    chunks, sums = refs[:ways], refs[ways : ways + len(raw)]
    gain_ref, out_ref, scratch, sems = refs[ways + len(raw) :]
    me = lax.axis_index("dp")
    tok = chunks[0].shape[0]

    def put(source, k):
        rows = pl.ds(pl.multiple_of((me ^ k) * tok, tok), tok)
        copy = pltpu.make_async_copy(source, out_ref.at[rows, :], sems.at[k])
        copy.start()
        return copy

    copies = [put(chunks[i], k) for i, k in enumerate(ready)]
    for i, k in enumerate(raw):
        inv = lax.rsqrt(sums[i][0:1, :] * (1.0 / feat_width) + epsilon)
        column = jnp.broadcast_to(inv, (tok, tok)).T[:, 0:1]
        value = chunks[len(ready) + i][...].astype(F32) * column * gain_ref[0:1, :]
        scratch[i] = value.astype(BF16)
        copies.append(put(scratch.at[i], k))
    for copy in copies:
        copy.wait()


def finish(ready, raw, sums, gain, feat_width):
    first = next(iter(ready.values()))
    tok, width = first.shape
    ways = len(ready) + len(raw)
    return pl.pallas_call(
        functools.partial(finish_body, feat_width, tuple(ready), tuple(raw)),
        out_shape=jax.ShapeDtypeStruct((tok * ways, width), BF16),
        in_specs=[vmem()] * (ways + len(raw) + 1),
        out_specs=pl.BlockSpec(memory_space=pltpu.HBM),
        scratch_shapes=[
            pltpu.VMEM((len(raw), tok, width), BF16),
            pltpu.SemaphoreType.DMA((ways,)),
        ],
        name="finish",
        cost_estimate=pl.CostEstimate(flops=10**6, transcendentals=0, bytes_accessed=10**6),
        compiler_params=pltpu.CompilerParams(vmem_limit_bytes=8 * 2**20),
    )(*ready.values(), *raw.values(), *[sums[k] for k in raw], gain)


def swap(value, axis, offset):
    size = lax.axis_size(axis)
    return lax.ppermute(value, axis, [(i, i ^ offset) for i in range(size)])


def swap_each(values, axis):
    moved = {}
    for k, value in values.items():
        moved[k] = swap(value, axis, k) if k else value
    return moved


def local_fast(tokens, routes, gate_code, gate_table, w_gate, w_up, w_down, norm_gain):
    return fast_steps(tokens, routes, gate_code, gate_table, w_gate, w_up, w_down, norm_gain)


def fast_steps(tokens, routes, gate_code, gate_table, w_gate, w_up, w_down, norm_gain):
    own_rows = tokens[0]
    tok, feat_width = own_rows.shape
    experts = lax.axis_size("expert")
    ways = lax.axis_size("dp")
    capacity = 5 * tok // (2 * experts)
    chunk = feat_width // ways
    close, away = CLOSE + [0], AWAY
    early = (ways // 2,)
    late = tuple(k for k in range(ways - 1, -1, -1) if k not in early)

    route_rows = routes[0].T
    blocks = dispatch(
        pltpu.with_memory_space_constraint(route_rows, pltpu.HBM),
        pltpu.with_memory_space_constraint(own_rows, pltpu.HBM),
        experts, capacity,
    )
    near = swap_each({k: blocks[k] for k in close}, "expert")
    far = swap_each({k: blocks[k] for k in away}, "expert")
    select, select_close, select_away, weights = selector(route_rows, gate_code[0].T, gate_table, experts, capacity)
    matrices = w_gate[0].T, w_up[0].T, w_down[0]

    plan = [(j, early + late) for j in range(len(close))]
    _, *outputs = expert_call([near[k] for k in close], *matrices, plan, chunk)
    back = swap_each(dict(zip(close, outputs)), "expert")
    gain_own = gain_of(norm_gain, (0,), chunk)
    plan = [(j, early) for j in range(len(away))]
    hidden, *away_early = expert_call([far[k] for k in away], *matrices, plan, chunk)
    got_early = back | swap_each(dict(zip(away, away_early)), "expert")
    plan = [(j, late) for j in range(len(away))]
    away_late = down_call(hidden, matrices[2], len(away), plan, chunk)
    got_late = swap_each(dict(zip(away, away_late)), "expert")

    order = range(experts)
    first, part = combine_early(select, weights, [got_early[k] for k in order], chunk)
    raw = swap_each({early[0]: first}, "dp")
    gain_late = gain_of(norm_gain, late, chunk)
    begun = combine_mid(
        select_close, weights, [back[k] for k in order if k not in away], chunk * len(early)
    )
    *rest, total = combine_late(
        select_away, weights, begun, part, gain_late, [got_late[k] for k in away], chunk,
        feat_width,
    )
    ready = swap_each(dict(zip(late, rest)), "dp")
    sums = swap_each({k: total for k in early}, "dp")
    return finish(ready, raw, sums, gain_own, feat_width)[None]


def solution(mesh):
    in_specs = (
        P("expert", "dp", None),
        P("expert", "dp", None),
        P("expert", "dp", None),
        P(),
        P("expert", None, None),
        P("expert", None, None),
        P("expert", None, None),
        P(),
    )
    out_specs = P("expert", None, "dp")

    def whole(tokens, routes, gate_code, gate_table, w_gate, w_up, w_down, norm_gain):
        args = (tokens, routes, gate_code, gate_table, w_gate, w_up, w_down, norm_gain)
        experts, ways = mesh.shape["expert"], mesh.shape["dp"]
        tok, feat = tokens.shape[1] // ways, tokens.shape[2]
        power = experts & (experts - 1) == 0 and ways & (ways - 1) == 0
        fits = power and experts == 8 and ways == 4
        fits = fits and tok % 128 == 0 and w_gate.shape[0] == experts
        fits = fits and 5 * tok % (16 * experts) == 0 and feat % (256 * ways) == 0
        body = local_fast if fits else local_general
        f = jax.shard_map(body, mesh=mesh, in_specs=in_specs, out_specs=out_specs, check_vma=False)
        return f(*args)

    return whole
```

```python
import functools

import jax
import jax.numpy as jnp
from jax import lax
from jax.experimental import pallas as pl
from jax.experimental.pallas import tpu as pltpu
from jax.sharding import PartitionSpec as P


epsilon = 1e-06


F32 = jnp.float32
BF16 = jnp.bfloat16


def expert_ffn(slot_block, w_gate, w_up, w_down):
    shape_in = slot_block.shape
    flat_rows = slot_block.reshape(-1, shape_in[-1])
    gate_act = jnp.dot(flat_rows, w_gate[0], preferred_element_type=F32)
    up_act = jnp.dot(flat_rows, w_up[0], preferred_element_type=F32)
    hidden = (jax.nn.silu(gate_act) * up_act).astype(BF16)
    result = jnp.dot(hidden, w_down[0], preferred_element_type=F32).astype(BF16)
    return result.reshape(shape_in)


def lookup(codes, gate_table):
    levels = gate_table.shape[0]
    match = codes[:, None] == jnp.arange(levels, dtype=jnp.int32)[None, :]
    return jnp.sum(jnp.where(match, gate_table[None, :], 0.0), axis=1)


def combine_pairs(outputs, weights):
    combined = outputs[:, 0] * weights[:, 0:1] + outputs[:, 1] * weights[:, 1:2]
    rounded = lax.optimization_barrier(combined.astype(BF16))
    return rounded.astype(F32)


def local_general(tokens, routes, gate_code, gate_table, w_gate, w_up, w_down, norm_gain):
    own_rows = tokens[0]
    tok_count, feat_width = own_rows.shape
    experts = w_gate.shape[0] * lax.axis_size("expert")
    capacity = 5 * tok_count // (2 * experts)
    route_ids = routes[0].reshape(-1)
    onehot = (route_ids[:, None] == jnp.arange(experts, dtype=jnp.int32)[None, :]).astype(jnp.int32)
    slot_pos = jnp.sum((jnp.cumsum(onehot, axis=0) - onehot) * onehot, axis=1)
    position = route_ids * capacity + slot_pos
    owner_row = (
        jnp.zeros((experts * capacity,), jnp.int32)
        .at[position]
        .set(jnp.arange(2 * tok_count, dtype=jnp.int32) // 2)
    )
    filled = jnp.zeros((experts * capacity,), jnp.bool_).at[position].set(True)
    buffer = jnp.where(filled[:, None], own_rows[owner_row], jnp.zeros((), BF16))
    buffer = buffer.reshape(experts, capacity, feat_width)
    level_ids = gate_code[0].reshape(-1)
    received = lax.all_to_all(buffer, "expert", split_axis=0, concat_axis=0, tiled=True)
    expert_out = expert_ffn(received, w_gate, w_up, w_down)
    returned = lax.all_to_all(expert_out, "expert", split_axis=0, concat_axis=0, tiled=True)
    outputs = (
        returned.reshape(-1, feat_width)[position]
        .astype(F32)
        .reshape(tok_count, 2, feat_width)
    )
    weights = lookup(level_ids, gate_table).reshape(tok_count, 2)
    widened = combine_pairs(outputs, weights)
    inv_rms = lax.rsqrt(jnp.mean(widened * widened, axis=1, keepdims=True) + epsilon)
    normed = (widened * inv_rms * norm_gain[None, :]).astype(BF16)
    relaid = lax.all_to_all(normed, "dp", split_axis=1, concat_axis=0, tiled=True)
    return relaid[None]


CLOSE, AWAY = [4, 2, 5, 3, 1], [6, 7]


def vmem():
    return pl.BlockSpec(memory_space=pltpu.VMEM)


def slot_rows(route_rows, experts, me):
    tok = route_rows.shape[1]
    ids = lax.broadcasted_iota(jnp.int32, (experts, tok), 0) ^ me
    named = (route_rows[0:1, :] == ids) | (route_rows[1:2, :] == ids)
    earlier = lax.broadcasted_iota(jnp.int32, (tok, tok), 0) < lax.broadcasted_iota(
        jnp.int32, (tok, tok), 1
    )
    count = jnp.dot(
        named.astype(F32).astype(BF16), earlier.astype(F32).astype(BF16),
        preferred_element_type=F32,
    )
    return jnp.where(named, count.astype(jnp.int32), -1), ids


def pick_rows(pick_ref, tok_ref, out_refs):
    capacity, tile = out_refs[0].shape[0], 256
    for col in range(0, tok_ref.shape[1], tile):
        rows = jnp.dot(pick_ref[...], tok_ref[:, col : col + tile], preferred_element_type=F32)
        rows = rows.astype(BF16)
        for j, out in enumerate(out_refs):
            out[:, col : col + tile] = rows[j * capacity : (j + 1) * capacity, :]


def dispatch_body(experts, first, others, route_hbm, tok_hbm, *refs):
    *out_refs, rest_ref, tok_ref, pick_ref, route_ref, sems = refs
    copies = [
        pltpu.make_async_copy(route_hbm, route_ref, sems.at[0]),
        pltpu.make_async_copy(tok_hbm, tok_ref, sems.at[1]),
    ]
    for copy in copies:
        copy.start()
    me = lax.axis_index("expert")
    capacity, tok = out_refs[0].shape[0], tok_ref.shape[0]
    lane = lax.broadcasted_iota(jnp.int32, (capacity, tok), 0)
    copies[0].wait()
    slots, _ = slot_rows(route_ref[...], experts, me)
    for ref, offsets in ((pick_ref, first), (rest_ref, others)):
        for j, k in enumerate(offsets):
            pick = (lane == slots[k : k + 1, :]).astype(F32).astype(BF16)
            ref[j * capacity : (j + 1) * capacity, :] = pick
    copies[1].wait()
    pick_rows(pick_ref, tok_ref, out_refs)


def dispatch(route_rows, own_rows, experts, capacity, first, others):
    tok, width = own_rows.shape
    *outs, rest, held = pl.pallas_call(
        functools.partial(dispatch_body, experts, first, others),
        out_shape=[jax.ShapeDtypeStruct((capacity, width), BF16)] * len(first)
        + [
            jax.ShapeDtypeStruct((capacity * len(others), tok), BF16),
            jax.ShapeDtypeStruct((tok, width), BF16),
        ],
        in_specs=[pl.BlockSpec(memory_space=pltpu.HBM)] * 2,
        out_specs=[vmem()] * (len(first) + 2),
        scratch_shapes=[
            pltpu.VMEM((capacity * len(first), tok), BF16),
            pltpu.VMEM(route_rows.shape, jnp.int32),
            pltpu.SemaphoreType.DMA((2,)),
        ],
        name="dispatch",
        cost_estimate=pl.CostEstimate(flops=10**8, transcendentals=0, bytes_accessed=2 * 10**6),
        compiler_params=pltpu.CompilerParams(vmem_limit_bytes=16 * 2**20),
    )(route_rows, own_rows)
    return dict(zip(first, outs)), rest, held


def others_body(rest_ref, tok_ref, *out_refs):
    pick_rows(rest_ref, tok_ref, out_refs)


def dispatch_others(rest, held, capacity, others):
    outs = pl.pallas_call(
        others_body,
        out_shape=[jax.ShapeDtypeStruct((capacity, held.shape[1]), BF16)] * len(others),
        in_specs=[vmem()] * 2,
        out_specs=[vmem()] * len(others),
        name="others",
        cost_estimate=pl.CostEstimate(flops=10**8, transcendentals=0, bytes_accessed=2 * 10**6),
        compiler_params=pltpu.CompilerParams(vmem_limit_bytes=8 * 2**20),
    )(rest, held)
    return dict(zip(others, outs))


def selector_body(experts, capacity, route_ref, code_ref, table_ref, *refs):
    sel_ref, close_ref, away_ref, weight_ref = refs
    me = lax.axis_index("expert")
    rows = route_ref[...]
    slots, ids = slot_rows(rows, experts, me)
    tok = rows.shape[1]
    lane = lax.broadcasted_iota(jnp.int32, (capacity, tok), 0)
    for r in range(2):
        mine = jnp.where(rows[r : r + 1, :] == ids, slots, -1)
        pick = jnp.concatenate(
            [(lane == mine[j : j + 1, :]).astype(F32) for j in range(experts)], axis=0
        )
        held = slice(r * tok, (r + 1) * tok)
        split = close_ref.shape[1]
        sel_ref[held, :] = pick.T.astype(BF16)
        close_ref[held, :] = pick[:split].T.astype(BF16)
        away_ref[held, :] = pick[split:].T.astype(BF16)
        codes = code_ref[r : r + 1, :]
        weights = jnp.zeros((1, tok), F32)
        for level in range(table_ref.shape[0]):
            weights = jnp.where(codes == level, table_ref[level], weights)
        weight_ref[r] = jnp.broadcast_to(weights, (tok, tok)).T


def selector(route_rows, code_rows, gate_table, experts, capacity):
    tok = route_rows.shape[1]
    counts = (experts, experts - len(AWAY), len(AWAY))
    return pl.pallas_call(
        functools.partial(selector_body, experts, capacity),
        out_shape=[
            *[jax.ShapeDtypeStruct((2 * tok, n * capacity), BF16) for n in counts],
            jax.ShapeDtypeStruct((2, tok, tok), F32),
        ],
        in_specs=[vmem(), vmem(), pl.BlockSpec(memory_space=pltpu.SMEM)],
        out_specs=[vmem()] * 4,
        name="selector",
        cost_estimate=pl.CostEstimate(flops=2 * 10**10, transcendentals=0, bytes_accessed=10**8),
        compiler_params=pltpu.CompilerParams(vmem_limit_bytes=8 * 2**20),
    )(route_rows, code_rows, gate_table)


def chunk_columns(down_ref, offset, chunk):
    me, tile = lax.axis_index("dp"), 256
    for col in range(0, chunk, tile):
        start = pl.multiple_of((me ^ offset) * chunk + col, tile)
        yield col, tile, down_ref[:, pl.ds(start, tile)]


def write_down(hid_ref, down_ref, chunk, plan, out_refs):
    for offset in dict.fromkeys(k for _, offsets in plan for k in offsets):
        for col, tile, weight in chunk_columns(down_ref, offset, chunk):
            rows = jnp.dot(hid_ref[...], weight, preferred_element_type=F32).astype(BF16)
            for (j, offsets), out in zip(plan, out_refs):
                if offset in offsets:
                    capacity = out.shape[0]
                    at = offsets.index(offset) * chunk + col
                    out[:, at : at + tile] = rows[j * capacity : (j + 1) * capacity, :]


def expert_body(count, chunk, plan, *refs):
    blocks, (gate_ref, up_ref, down_ref) = refs[:count], refs[count : count + 3]
    hid_ref, x_ref, outs = refs[count + 3], refs[-1], refs[count + 4 : -1]
    capacity = blocks[0].shape[0]
    for j, block in enumerate(blocks):
        x_ref[j * capacity : (j + 1) * capacity, :] = block[...]
    hid = gate_ref.shape[0]
    over = (((1,), (1,)), ((), ()))
    few = x_ref.shape[0] <= 128
    if few:
        gate = lax.dot_general(gate_ref[...], x_ref[...], over, preferred_element_type=F32)
        up = lax.dot_general(up_ref[...], x_ref[...], over, preferred_element_type=F32)
        hid_ref[...] = (gate / (1.0 + jnp.exp(-gate)) * up).T.astype(BF16)
    tile = 256
    for low in range(0, 0 if few else hid, tile):
        high = min(hid, low + tile)
        gate = lax.dot_general(x_ref[...], gate_ref[low:high, :], over, preferred_element_type=F32)
        up = lax.dot_general(x_ref[...], up_ref[low:high, :], over, preferred_element_type=F32)
        hid_ref[:, low:high] = (gate / (1.0 + jnp.exp(-gate)) * up).astype(BF16)
    write_down(hid_ref, down_ref, chunk, plan, outs)


def expert_call(blocks, gate_rows, up_rows, down_rows, plan, chunk):
    count = len(blocks)
    capacity, width = blocks[0].shape
    rows, hid = capacity * count, gate_rows.shape[0]
    shapes = [jax.ShapeDtypeStruct((capacity, chunk * len(offsets)), BF16) for _, offsets in plan]
    return pl.pallas_call(
        functools.partial(expert_body, count, chunk, plan),
        out_shape=[jax.ShapeDtypeStruct((rows, hid), BF16)] + shapes,
        in_specs=[vmem()] * (count + 3),
        out_specs=[vmem()] * (1 + len(shapes)),
        scratch_shapes=[pltpu.VMEM((rows, width), BF16)],
        cost_estimate=pl.CostEstimate(
            flops=5 * rows * hid * width, transcendentals=rows * hid, bytes_accessed=8 * 10**6
        ),
        compiler_params=pltpu.CompilerParams(vmem_limit_bytes=24 * 2**20),
    )(*blocks, gate_rows, up_rows, down_rows)


def down_body(chunk, plan, hid_ref, down_ref, *out_refs):
    write_down(hid_ref, down_ref, chunk, plan, out_refs)


def down_call(hidden, down_rows, count, plan, chunk):
    rows, hid = hidden.shape
    return pl.pallas_call(
        functools.partial(down_body, chunk, plan),
        out_shape=[
            jax.ShapeDtypeStruct((rows // count, chunk * len(offsets)), BF16) for _, offsets in plan
        ],
        in_specs=[vmem()] * 2,
        out_specs=[vmem()] * len(plan),
        cost_estimate=pl.CostEstimate(
            flops=2 * rows * hid * chunk, transcendentals=0, bytes_accessed=3 * 10**6
        ),
        compiler_params=pltpu.CompilerParams(vmem_limit_bytes=16 * 2**20),
    )(hidden, down_rows)


def gather_blocks(blocks, y_ref, low):
    capacity, width = blocks[0].shape[0], y_ref.shape[1]
    for j, block in enumerate(blocks):
        start = low if block.shape[1] > width else 0
        y_ref[j * capacity : (j + 1) * capacity, :] = block[:, start : start + width]


def weighted(sel_ref, weight_ref, y_ref, low, tile):
    tok, lanes = weight_ref.shape[1:]
    picked = jnp.dot(sel_ref[...], y_ref[:, low : low + tile], preferred_element_type=F32)
    for at in range(0, tile, lanes):
        first = picked[:tok, at : at + lanes] * weight_ref[0]
        second = picked[tok:, at : at + lanes] * weight_ref[1]
        yield slice(low + at, low + at + lanes), first + second


def early_body(count, sel_ref, weight_ref, *refs):
    blocks, (out_ref, sum_ref, y_ref) = refs[:count], refs[count:]
    gather_blocks(blocks, y_ref, 0)
    squares = jnp.zeros(sum_ref.shape, F32)
    for low in range(0, y_ref.shape[1], 256):
        for cols, combined in weighted(sel_ref, weight_ref, y_ref, low, 256):
            rounded = combined.astype(BF16)
            out_ref[:, cols] = rounded
            squares = squares + rounded.astype(F32) * rounded.astype(F32)
    sum_ref[...] = squares


def combine_early(select, weights, blocks, width):
    rows, tok = blocks[0].shape[0] * len(blocks), weights.shape[1]
    return pl.pallas_call(
        functools.partial(early_body, len(blocks)),
        out_shape=[
            jax.ShapeDtypeStruct((tok, width), BF16),
            jax.ShapeDtypeStruct((tok, weights.shape[2]), F32),
        ],
        in_specs=[vmem()] * (2 + len(blocks)),
        out_specs=[vmem()] * 2,
        scratch_shapes=[pltpu.VMEM((rows, width), BF16)],
        name="combine_early",
        cost_estimate=pl.CostEstimate(
            flops=4 * tok * rows * width, transcendentals=0, bytes_accessed=10**6
        ),
        compiler_params=pltpu.CompilerParams(vmem_limit_bytes=12 * 2**20),
    )(select, weights, *blocks)


def mid_body(count, low, sel_ref, weight_ref, *refs):
    blocks, (out_ref, y_ref) = refs[:count], refs[count:]
    gather_blocks(blocks, y_ref, low)
    for col in range(0, y_ref.shape[1], 256):
        for cols, combined in weighted(sel_ref, weight_ref, y_ref, col, 256):
            out_ref[:, cols] = combined


def combine_mid(select, weights, blocks, low):
    capacity, width = blocks[0].shape
    rows, tok, width = capacity * len(blocks), weights.shape[1], width - low
    return pl.pallas_call(
        functools.partial(mid_body, len(blocks), low),
        out_shape=jax.ShapeDtypeStruct((tok, width), F32),
        in_specs=[vmem()] * (2 + len(blocks)),
        out_specs=vmem(),
        scratch_shapes=[pltpu.VMEM((rows, width), BF16)],
        name="combine_mid",
        cost_estimate=pl.CostEstimate(
            flops=4 * tok * rows * width, transcendentals=0, bytes_accessed=2 * 10**6
        ),
        compiler_params=pltpu.CompilerParams(vmem_limit_bytes=12 * 2**20),
    )(select, weights, *blocks)


def late_body(count, feat_width, sel_ref, weight_ref, begun_ref, part_ref, gain_ref, *refs):
    blocks, y_ref, outs, sum_ref = refs[:count], refs[-1], refs[count:-2], refs[-2]
    chunk = outs[0].shape[1]
    gather_blocks(blocks, y_ref, 0)
    squares = part_ref[...]
    for low in range(0, y_ref.shape[1], 256):
        for cols, combined in weighted(sel_ref, weight_ref, y_ref, low, 256):
            rounded = (begun_ref[:, cols] + combined).astype(BF16)
            at = cols.start % chunk
            outs[cols.start // chunk][:, at : at + cols.stop - cols.start] = rounded
            squares = squares + rounded.astype(F32) * rounded.astype(F32)
    total = jnp.sum(squares, axis=1, keepdims=True)
    tok = total.shape[0]
    sum_ref[...] = jnp.broadcast_to(total, (tok, tok)).T[0:8, :]
    inv = lax.rsqrt(total * (1.0 / feat_width) + epsilon)
    for q, out in enumerate(outs):
        gain = gain_ref[0:1, q * chunk : (q + 1) * chunk]
        out[...] = (out[...].astype(F32) * inv * gain).astype(BF16)


def combine_late(select, weights, begun, part, gain, blocks, chunk, feat_width):
    capacity, width = blocks[0].shape
    rows, tok = capacity * len(blocks), weights.shape[1]
    return pl.pallas_call(
        functools.partial(late_body, len(blocks), feat_width),
        out_shape=[jax.ShapeDtypeStruct((tok, chunk), BF16)] * (width // chunk)
        + [jax.ShapeDtypeStruct((8, tok), F32)],
        in_specs=[vmem()] * (5 + len(blocks)),
        out_specs=[vmem()] * (width // chunk + 1),
        scratch_shapes=[pltpu.VMEM((rows, width), BF16)],
        name="combine_late",
        cost_estimate=pl.CostEstimate(
            flops=4 * tok * rows * width, transcendentals=0, bytes_accessed=2 * 10**6
        ),
        compiler_params=pltpu.CompilerParams(vmem_limit_bytes=12 * 2**20),
    )(select, weights, begun, part, gain, *blocks)


def gain_body(offsets, gain_ref, out_ref):
    chunk = out_ref.shape[1] // len(offsets)
    me = lax.axis_index("dp")
    for q, offset in enumerate(offsets):
        start = pl.multiple_of((me ^ offset) * chunk, 128)
        row = gain_ref[:, pl.ds(start, chunk)]
        out_ref[:, q * chunk : (q + 1) * chunk] = jnp.broadcast_to(row, (8, chunk))


def gain_of(norm_gain, offsets, chunk):
    return pl.pallas_call(
        functools.partial(gain_body, offsets),
        out_shape=jax.ShapeDtypeStruct((8, chunk * len(offsets)), F32),
        in_specs=[vmem()],
        out_specs=vmem(),
        cost_estimate=pl.CostEstimate(flops=10**4, transcendentals=0, bytes_accessed=10**4),
        compiler_params=pltpu.CompilerParams(vmem_limit_bytes=2**20),
    )(norm_gain[None, :])


def finish_body(feat_width, ready, raw, *refs):
    ways = len(ready) + len(raw)
    chunks, sums = refs[:ways], refs[ways : ways + len(raw)]
    gain_ref, out_ref, scratch, sems = refs[ways + len(raw) :]
    me = lax.axis_index("dp")
    tok = chunks[0].shape[0]

    def put(source, k):
        rows = pl.ds(pl.multiple_of((me ^ k) * tok, tok), tok)
        copy = pltpu.make_async_copy(source, out_ref.at[rows, :], sems.at[k])
        copy.start()
        return copy

    copies = [put(chunks[i], k) for i, k in enumerate(ready)]
    for i, k in enumerate(raw):
        inv = lax.rsqrt(sums[i][0:1, :] * (1.0 / feat_width) + epsilon)
        column = jnp.broadcast_to(inv, (tok, tok)).T[:, 0:1]
        value = chunks[len(ready) + i][...].astype(F32) * column * gain_ref[0:1, :]
        scratch[i] = value.astype(BF16)
        copies.append(put(scratch.at[i], k))
    for copy in copies:
        copy.wait()


def finish(ready, raw, sums, gain, feat_width):
    first = next(iter(ready.values()))
    tok, width = first.shape
    ways = len(ready) + len(raw)
    return pl.pallas_call(
        functools.partial(finish_body, feat_width, tuple(ready), tuple(raw)),
        out_shape=jax.ShapeDtypeStruct((tok * ways, width), BF16),
        in_specs=[vmem()] * (ways + len(raw) + 1),
        out_specs=pl.BlockSpec(memory_space=pltpu.HBM),
        scratch_shapes=[
            pltpu.VMEM((len(raw), tok, width), BF16),
            pltpu.SemaphoreType.DMA((ways,)),
        ],
        name="finish",
        cost_estimate=pl.CostEstimate(flops=10**6, transcendentals=0, bytes_accessed=10**6),
        compiler_params=pltpu.CompilerParams(vmem_limit_bytes=8 * 2**20),
    )(*ready.values(), *raw.values(), *[sums[k] for k in raw], gain)


def swap(value, axis, offset):
    size = lax.axis_size(axis)
    return lax.ppermute(value, axis, [(i, i ^ offset) for i in range(size)])


def swap_each(values, axis):
    moved = {}
    for k, value in values.items():
        moved[k] = swap(value, axis, k) if k else value
    return moved


def local_fast(tokens, routes, gate_code, gate_table, w_gate, w_up, w_down, norm_gain):
    return fast_steps(tokens, routes, gate_code, gate_table, w_gate, w_up, w_down, norm_gain)


def fast_steps(tokens, routes, gate_code, gate_table, w_gate, w_up, w_down, norm_gain):
    own_rows = tokens[0]
    tok, feat_width = own_rows.shape
    experts = lax.axis_size("expert")
    ways = lax.axis_size("dp")
    capacity = 5 * tok // (2 * experts)
    chunk = feat_width // ways
    close, away = CLOSE + [0], AWAY
    early = (ways // 2,)
    late = tuple(k for k in range(ways - 1, -1, -1) if k not in early)

    route_rows = routes[0].T
    blocks, rest, held = dispatch(
        pltpu.with_memory_space_constraint(route_rows, pltpu.HBM),
        pltpu.with_memory_space_constraint(own_rows, pltpu.HBM),
        experts, capacity, CLOSE[:4], CLOSE[4:] + [0] + AWAY,
    )
    blocks |= dispatch_others(rest, held, capacity, CLOSE[4:] + [0] + AWAY)
    near = swap_each({k: blocks[k] for k in close}, "expert")
    far = swap_each({k: blocks[k] for k in away}, "expert")
    select, select_close, select_away, weights = selector(route_rows, gate_code[0].T, gate_table, experts, capacity)
    matrices = w_gate[0].T, w_up[0].T, w_down[0]

    plan = [(j, early + late) for j in range(len(close))]
    _, *outputs = expert_call([near[k] for k in close], *matrices, plan, chunk)
    back = swap_each(dict(zip(close, outputs)), "expert")
    gain_own = gain_of(norm_gain, (0,), chunk)
    plan = [(j, early) for j in range(len(away))]
    hidden, *away_early = expert_call([far[k] for k in away], *matrices, plan, chunk)
    got_early = back | swap_each(dict(zip(away, away_early)), "expert")
    plan = [(j, late) for j in range(len(away))]
    away_late = down_call(hidden, matrices[2], len(away), plan, chunk)
    got_late = swap_each(dict(zip(away, away_late)), "expert")

    order = range(experts)
    first, part = combine_early(select, weights, [got_early[k] for k in order], chunk)
    raw = swap_each({early[0]: first}, "dp")
    gain_late = gain_of(norm_gain, late, chunk)
    begun = combine_mid(
        select_close, weights, [back[k] for k in order if k not in away], chunk * len(early)
    )
    *rest, total = combine_late(
        select_away, weights, begun, part, gain_late, [got_late[k] for k in away], chunk,
        feat_width,
    )
    ready = swap_each(dict(zip(late, rest)), "dp")
    sums = swap_each({k: total for k in early}, "dp")
    return finish(ready, raw, sums, gain_own, feat_width)[None]


def solution(mesh):
    in_specs = (
        P("expert", "dp", None),
        P("expert", "dp", None),
        P("expert", "dp", None),
        P(),
        P("expert", None, None),
        P("expert", None, None),
        P("expert", None, None),
        P(),
    )
    out_specs = P("expert", None, "dp")

    def whole(tokens, routes, gate_code, gate_table, w_gate, w_up, w_down, norm_gain):
        args = (tokens, routes, gate_code, gate_table, w_gate, w_up, w_down, norm_gain)
        experts, ways = mesh.shape["expert"], mesh.shape["dp"]
        tok, feat = tokens.shape[1] // ways, tokens.shape[2]
        power = experts & (experts - 1) == 0 and ways & (ways - 1) == 0
        fits = power and experts == 8 and ways == 4
        fits = fits and tok % 128 == 0 and w_gate.shape[0] == experts
        fits = fits and 5 * tok % (16 * experts) == 0 and feat % (256 * ways) == 0
        body = local_fast if fits else local_general
        f = jax.shard_map(body, mesh=mesh, in_specs=in_specs, out_specs=out_specs, check_vma=False)
        return f(*args)

    return whole
```

```python
import functools

import jax
import jax.numpy as jnp
from jax import lax
from jax.experimental import pallas as pl
from jax.experimental.pallas import tpu as pltpu
from jax.sharding import PartitionSpec as P


epsilon = 1e-06


F32 = jnp.float32
BF16 = jnp.bfloat16


def expert_ffn(slot_block, w_gate, w_up, w_down):
    shape_in = slot_block.shape
    flat_rows = slot_block.reshape(-1, shape_in[-1])
    gate_act = jnp.dot(flat_rows, w_gate[0], preferred_element_type=F32)
    up_act = jnp.dot(flat_rows, w_up[0], preferred_element_type=F32)
    hidden = (jax.nn.silu(gate_act) * up_act).astype(BF16)
    result = jnp.dot(hidden, w_down[0], preferred_element_type=F32).astype(BF16)
    return result.reshape(shape_in)


def lookup(codes, gate_table):
    levels = gate_table.shape[0]
    match = codes[:, None] == jnp.arange(levels, dtype=jnp.int32)[None, :]
    return jnp.sum(jnp.where(match, gate_table[None, :], 0.0), axis=1)


def combine_pairs(outputs, weights):
    combined = outputs[:, 0] * weights[:, 0:1] + outputs[:, 1] * weights[:, 1:2]
    rounded = lax.optimization_barrier(combined.astype(BF16))
    return rounded.astype(F32)


def local_general(tokens, routes, gate_code, gate_table, w_gate, w_up, w_down, norm_gain):
    own_rows = tokens[0]
    tok_count, feat_width = own_rows.shape
    experts = w_gate.shape[0] * lax.axis_size("expert")
    capacity = 5 * tok_count // (2 * experts)
    route_ids = routes[0].reshape(-1)
    onehot = (route_ids[:, None] == jnp.arange(experts, dtype=jnp.int32)[None, :]).astype(jnp.int32)
    slot_pos = jnp.sum((jnp.cumsum(onehot, axis=0) - onehot) * onehot, axis=1)
    position = route_ids * capacity + slot_pos
    owner_row = (
        jnp.zeros((experts * capacity,), jnp.int32)
        .at[position]
        .set(jnp.arange(2 * tok_count, dtype=jnp.int32) // 2)
    )
    filled = jnp.zeros((experts * capacity,), jnp.bool_).at[position].set(True)
    buffer = jnp.where(filled[:, None], own_rows[owner_row], jnp.zeros((), BF16))
    buffer = buffer.reshape(experts, capacity, feat_width)
    level_ids = gate_code[0].reshape(-1)
    received = lax.all_to_all(buffer, "expert", split_axis=0, concat_axis=0, tiled=True)
    expert_out = expert_ffn(received, w_gate, w_up, w_down)
    returned = lax.all_to_all(expert_out, "expert", split_axis=0, concat_axis=0, tiled=True)
    outputs = (
        returned.reshape(-1, feat_width)[position]
        .astype(F32)
        .reshape(tok_count, 2, feat_width)
    )
    weights = lookup(level_ids, gate_table).reshape(tok_count, 2)
    widened = combine_pairs(outputs, weights)
    inv_rms = lax.rsqrt(jnp.mean(widened * widened, axis=1, keepdims=True) + epsilon)
    normed = (widened * inv_rms * norm_gain[None, :]).astype(BF16)
    relaid = lax.all_to_all(normed, "dp", split_axis=1, concat_axis=0, tiled=True)
    return relaid[None]


CLOSE, AWAY = [4, 2, 5, 3, 1], [6, 7]


def vmem():
    return pl.BlockSpec(memory_space=pltpu.VMEM)


def slot_rows(route_rows, experts, me):
    tok = route_rows.shape[1]
    ids = lax.broadcasted_iota(jnp.int32, (experts, tok), 0) ^ me
    named = (route_rows[0:1, :] == ids) | (route_rows[1:2, :] == ids)
    earlier = lax.broadcasted_iota(jnp.int32, (tok, tok), 0) < lax.broadcasted_iota(
        jnp.int32, (tok, tok), 1
    )
    count = jnp.dot(
        named.astype(F32).astype(BF16), earlier.astype(F32).astype(BF16),
        preferred_element_type=F32,
    )
    return jnp.where(named, count.astype(jnp.int32), -1), ids


def pick_rows(pick_ref, tok_ref, out_refs):
    capacity, tile = out_refs[0].shape[0], 256
    for col in range(0, tok_ref.shape[1], tile):
        rows = jnp.dot(pick_ref[...], tok_ref[:, col : col + tile], preferred_element_type=F32)
        rows = rows.astype(BF16)
        for j, out in enumerate(out_refs):
            out[:, col : col + tile] = rows[j * capacity : (j + 1) * capacity, :]


def dispatch_body(experts, first, others, route_hbm, code_hbm, tok_hbm, *refs):
    *out_refs, rest_ref, route_ref, code_ref, tok_ref, pick_ref, sems = refs
    copies = [
        pltpu.make_async_copy(route_hbm, route_ref, sems.at[0]),
        pltpu.make_async_copy(tok_hbm, tok_ref, sems.at[1]),
        pltpu.make_async_copy(code_hbm, code_ref, sems.at[2]),
    ]
    for copy in copies:
        copy.start()
    me = lax.axis_index("expert")
    capacity, tok = out_refs[0].shape[0], tok_ref.shape[0]
    lane = lax.broadcasted_iota(jnp.int32, (capacity, tok), 0)
    copies[0].wait()
    slots, _ = slot_rows(route_ref[...], experts, me)
    for ref, offsets in ((pick_ref, first), (rest_ref, others)):
        for j, k in enumerate(offsets):
            pick = (lane == slots[k : k + 1, :]).astype(F32).astype(BF16)
            ref[j * capacity : (j + 1) * capacity, :] = pick
    copies[1].wait()
    pick_rows(pick_ref, tok_ref, out_refs)
    copies[2].wait()


def dispatch(route_rows, code_rows, own_rows, experts, capacity, first, others):
    tok, width = own_rows.shape
    *outs, rest, route_held, code_held, held = pl.pallas_call(
        functools.partial(dispatch_body, experts, first, others),
        out_shape=[jax.ShapeDtypeStruct((capacity, width), BF16)] * len(first)
        + [
            jax.ShapeDtypeStruct((capacity * len(others), tok), BF16),
            jax.ShapeDtypeStruct(route_rows.shape, jnp.int32),
            jax.ShapeDtypeStruct(code_rows.shape, jnp.int32),
            jax.ShapeDtypeStruct((tok, width), BF16),
        ],
        in_specs=[pl.BlockSpec(memory_space=pltpu.HBM)] * 3,
        out_specs=[vmem()] * (len(first) + 4),
        scratch_shapes=[
            pltpu.VMEM((capacity * len(first), tok), BF16),
            pltpu.SemaphoreType.DMA((3,)),
        ],
        name="dispatch",
        cost_estimate=pl.CostEstimate(flops=10**8, transcendentals=0, bytes_accessed=2 * 10**6),
        compiler_params=pltpu.CompilerParams(vmem_limit_bytes=16 * 2**20),
    )(route_rows, code_rows, own_rows)
    return dict(zip(first, outs)), rest, route_held, code_held, held


def others_body(rest_ref, tok_ref, *out_refs):
    pick_rows(rest_ref, tok_ref, out_refs)


def dispatch_others(rest, held, capacity, others):
    outs = pl.pallas_call(
        others_body,
        out_shape=[jax.ShapeDtypeStruct((capacity, held.shape[1]), BF16)] * len(others),
        in_specs=[vmem()] * 2,
        out_specs=[vmem()] * len(others),
        name="others",
        cost_estimate=pl.CostEstimate(flops=10**8, transcendentals=0, bytes_accessed=2 * 10**6),
        compiler_params=pltpu.CompilerParams(vmem_limit_bytes=8 * 2**20),
    )(rest, held)
    return dict(zip(others, outs))


def selector_body(experts, capacity, route_ref, code_ref, table_ref, *refs):
    sel_ref, close_ref, away_ref, weight_ref = refs
    me = lax.axis_index("expert")
    rows = route_ref[...]
    slots, ids = slot_rows(rows, experts, me)
    tok = rows.shape[1]
    lane = lax.broadcasted_iota(jnp.int32, (capacity, tok), 0)
    for r in range(2):
        mine = jnp.where(rows[r : r + 1, :] == ids, slots, -1)
        pick = jnp.concatenate(
            [(lane == mine[j : j + 1, :]).astype(F32) for j in range(experts)], axis=0
        )
        held = slice(r * tok, (r + 1) * tok)
        split = close_ref.shape[1]
        sel_ref[held, :] = pick.T.astype(BF16)
        close_ref[held, :] = pick[:split].T.astype(BF16)
        away_ref[held, :] = pick[split:].T.astype(BF16)
        codes = code_ref[r : r + 1, :]
        weights = jnp.zeros((1, tok), F32)
        for level in range(table_ref.shape[0]):
            weights = jnp.where(codes == level, table_ref[level], weights)
        weight_ref[r] = jnp.broadcast_to(weights, (tok, tok)).T


def selector(route_rows, code_rows, gate_table, experts, capacity):
    tok = route_rows.shape[1]
    counts = (experts, experts - len(AWAY), len(AWAY))
    return pl.pallas_call(
        functools.partial(selector_body, experts, capacity),
        out_shape=[
            *[jax.ShapeDtypeStruct((2 * tok, n * capacity), BF16) for n in counts],
            jax.ShapeDtypeStruct((2, tok, tok), F32),
        ],
        in_specs=[vmem(), vmem(), pl.BlockSpec(memory_space=pltpu.SMEM)],
        out_specs=[vmem()] * 4,
        name="selector",
        cost_estimate=pl.CostEstimate(flops=2 * 10**10, transcendentals=0, bytes_accessed=10**8),
        compiler_params=pltpu.CompilerParams(vmem_limit_bytes=8 * 2**20),
    )(route_rows, code_rows, gate_table)


def chunk_columns(down_ref, offset, chunk):
    me, tile = lax.axis_index("dp"), 256
    for col in range(0, chunk, tile):
        start = pl.multiple_of((me ^ offset) * chunk + col, tile)
        yield col, tile, down_ref[:, pl.ds(start, tile)]


def write_down(hid_ref, down_ref, chunk, plan, out_refs):
    for offset in dict.fromkeys(k for _, offsets in plan for k in offsets):
        for col, tile, weight in chunk_columns(down_ref, offset, chunk):
            rows = jnp.dot(hid_ref[...], weight, preferred_element_type=F32).astype(BF16)
            for (j, offsets), out in zip(plan, out_refs):
                if offset in offsets:
                    capacity = out.shape[0]
                    at = offsets.index(offset) * chunk + col
                    out[:, at : at + tile] = rows[j * capacity : (j + 1) * capacity, :]


def expert_body(count, chunk, plan, *refs):
    blocks, (gate_ref, up_ref, down_ref) = refs[:count], refs[count : count + 3]
    hid_ref, x_ref, outs = refs[count + 3], refs[-1], refs[count + 4 : -1]
    capacity = blocks[0].shape[0]
    for j, block in enumerate(blocks):
        x_ref[j * capacity : (j + 1) * capacity, :] = block[...]
    hid = gate_ref.shape[0]
    over = (((1,), (1,)), ((), ()))
    few = x_ref.shape[0] <= 128
    if few:
        gate = lax.dot_general(gate_ref[...], x_ref[...], over, preferred_element_type=F32)
        up = lax.dot_general(up_ref[...], x_ref[...], over, preferred_element_type=F32)
        hid_ref[...] = (gate / (1.0 + jnp.exp(-gate)) * up).T.astype(BF16)
    tile = 256
    for low in range(0, 0 if few else hid, tile):
        high = min(hid, low + tile)
        gate = lax.dot_general(x_ref[...], gate_ref[low:high, :], over, preferred_element_type=F32)
        up = lax.dot_general(x_ref[...], up_ref[low:high, :], over, preferred_element_type=F32)
        hid_ref[:, low:high] = (gate / (1.0 + jnp.exp(-gate)) * up).astype(BF16)
    write_down(hid_ref, down_ref, chunk, plan, outs)


def expert_call(blocks, gate_rows, up_rows, down_rows, plan, chunk):
    count = len(blocks)
    capacity, width = blocks[0].shape
    rows, hid = capacity * count, gate_rows.shape[0]
    shapes = [jax.ShapeDtypeStruct((capacity, chunk * len(offsets)), BF16) for _, offsets in plan]
    return pl.pallas_call(
        functools.partial(expert_body, count, chunk, plan),
        out_shape=[jax.ShapeDtypeStruct((rows, hid), BF16)] + shapes,
        in_specs=[vmem()] * (count + 3),
        out_specs=[vmem()] * (1 + len(shapes)),
        scratch_shapes=[pltpu.VMEM((rows, width), BF16)],
        cost_estimate=pl.CostEstimate(
            flops=5 * rows * hid * width, transcendentals=rows * hid, bytes_accessed=8 * 10**6
        ),
        compiler_params=pltpu.CompilerParams(vmem_limit_bytes=24 * 2**20),
    )(*blocks, gate_rows, up_rows, down_rows)


def down_body(chunk, plan, hid_ref, down_ref, *out_refs):
    write_down(hid_ref, down_ref, chunk, plan, out_refs)


def down_call(hidden, down_rows, count, plan, chunk):
    rows, hid = hidden.shape
    return pl.pallas_call(
        functools.partial(down_body, chunk, plan),
        out_shape=[
            jax.ShapeDtypeStruct((rows // count, chunk * len(offsets)), BF16) for _, offsets in plan
        ],
        in_specs=[vmem()] * 2,
        out_specs=[vmem()] * len(plan),
        cost_estimate=pl.CostEstimate(
            flops=2 * rows * hid * chunk, transcendentals=0, bytes_accessed=3 * 10**6
        ),
        compiler_params=pltpu.CompilerParams(vmem_limit_bytes=16 * 2**20),
    )(hidden, down_rows)


def gather_blocks(blocks, y_ref, low):
    capacity, width = blocks[0].shape[0], y_ref.shape[1]
    for j, block in enumerate(blocks):
        start = low if block.shape[1] > width else 0
        y_ref[j * capacity : (j + 1) * capacity, :] = block[:, start : start + width]


def weighted(sel_ref, weight_ref, y_ref, low, tile):
    tok, lanes = weight_ref.shape[1:]
    picked = jnp.dot(sel_ref[...], y_ref[:, low : low + tile], preferred_element_type=F32)
    for at in range(0, tile, lanes):
        first = picked[:tok, at : at + lanes] * weight_ref[0]
        second = picked[tok:, at : at + lanes] * weight_ref[1]
        yield slice(low + at, low + at + lanes), first + second


def early_body(count, sel_ref, weight_ref, *refs):
    blocks, (out_ref, sum_ref, y_ref) = refs[:count], refs[count:]
    gather_blocks(blocks, y_ref, 0)
    squares = jnp.zeros(sum_ref.shape, F32)
    for low in range(0, y_ref.shape[1], 256):
        for cols, combined in weighted(sel_ref, weight_ref, y_ref, low, 256):
            rounded = combined.astype(BF16)
            out_ref[:, cols] = rounded
            squares = squares + rounded.astype(F32) * rounded.astype(F32)
    sum_ref[...] = squares


def combine_early(select, weights, blocks, width):
    rows, tok = blocks[0].shape[0] * len(blocks), weights.shape[1]
    return pl.pallas_call(
        functools.partial(early_body, len(blocks)),
        out_shape=[
            jax.ShapeDtypeStruct((tok, width), BF16),
            jax.ShapeDtypeStruct((tok, weights.shape[2]), F32),
        ],
        in_specs=[vmem()] * (2 + len(blocks)),
        out_specs=[vmem()] * 2,
        scratch_shapes=[pltpu.VMEM((rows, width), BF16)],
        name="combine_early",
        cost_estimate=pl.CostEstimate(
            flops=4 * tok * rows * width, transcendentals=0, bytes_accessed=10**6
        ),
        compiler_params=pltpu.CompilerParams(vmem_limit_bytes=12 * 2**20),
    )(select, weights, *blocks)


def mid_body(count, low, sel_ref, weight_ref, *refs):
    blocks, (out_ref, y_ref) = refs[:count], refs[count:]
    gather_blocks(blocks, y_ref, low)
    for col in range(0, y_ref.shape[1], 256):
        for cols, combined in weighted(sel_ref, weight_ref, y_ref, col, 256):
            out_ref[:, cols] = combined


def combine_mid(select, weights, blocks, low):
    capacity, width = blocks[0].shape
    rows, tok, width = capacity * len(blocks), weights.shape[1], width - low
    return pl.pallas_call(
        functools.partial(mid_body, len(blocks), low),
        out_shape=jax.ShapeDtypeStruct((tok, width), F32),
        in_specs=[vmem()] * (2 + len(blocks)),
        out_specs=vmem(),
        scratch_shapes=[pltpu.VMEM((rows, width), BF16)],
        name="combine_mid",
        cost_estimate=pl.CostEstimate(
            flops=4 * tok * rows * width, transcendentals=0, bytes_accessed=2 * 10**6
        ),
        compiler_params=pltpu.CompilerParams(vmem_limit_bytes=12 * 2**20),
    )(select, weights, *blocks)


def late_body(count, feat_width, sel_ref, weight_ref, begun_ref, part_ref, gain_ref, *refs):
    blocks, y_ref, outs, sum_ref = refs[:count], refs[-1], refs[count:-2], refs[-2]
    chunk = outs[0].shape[1]
    gather_blocks(blocks, y_ref, 0)
    squares = part_ref[...]
    for low in range(0, y_ref.shape[1], 256):
        for cols, combined in weighted(sel_ref, weight_ref, y_ref, low, 256):
            rounded = (begun_ref[:, cols] + combined).astype(BF16)
            at = cols.start % chunk
            outs[cols.start // chunk][:, at : at + cols.stop - cols.start] = rounded
            squares = squares + rounded.astype(F32) * rounded.astype(F32)
    total = jnp.sum(squares, axis=1, keepdims=True)
    tok = total.shape[0]
    sum_ref[...] = jnp.broadcast_to(total, (tok, tok)).T[0:8, :]
    inv = lax.rsqrt(total * (1.0 / feat_width) + epsilon)
    for q, out in enumerate(outs):
        gain = gain_ref[0:1, q * chunk : (q + 1) * chunk]
        out[...] = (out[...].astype(F32) * inv * gain).astype(BF16)


def combine_late(select, weights, begun, part, gain, blocks, chunk, feat_width):
    capacity, width = blocks[0].shape
    rows, tok = capacity * len(blocks), weights.shape[1]
    return pl.pallas_call(
        functools.partial(late_body, len(blocks), feat_width),
        out_shape=[jax.ShapeDtypeStruct((tok, chunk), BF16)] * (width // chunk)
        + [jax.ShapeDtypeStruct((8, tok), F32)],
        in_specs=[vmem()] * (5 + len(blocks)),
        out_specs=[vmem()] * (width // chunk + 1),
        scratch_shapes=[pltpu.VMEM((rows, width), BF16)],
        name="combine_late",
        cost_estimate=pl.CostEstimate(
            flops=4 * tok * rows * width, transcendentals=0, bytes_accessed=2 * 10**6
        ),
        compiler_params=pltpu.CompilerParams(vmem_limit_bytes=12 * 2**20),
    )(select, weights, begun, part, gain, *blocks)


def gain_body(offsets, gain_ref, out_ref):
    chunk = out_ref.shape[1] // len(offsets)
    me = lax.axis_index("dp")
    for q, offset in enumerate(offsets):
        start = pl.multiple_of((me ^ offset) * chunk, 128)
        row = gain_ref[:, pl.ds(start, chunk)]
        out_ref[:, q * chunk : (q + 1) * chunk] = jnp.broadcast_to(row, (8, chunk))


def gain_of(norm_gain, offsets, chunk):
    return pl.pallas_call(
        functools.partial(gain_body, offsets),
        out_shape=jax.ShapeDtypeStruct((8, chunk * len(offsets)), F32),
        in_specs=[vmem()],
        out_specs=vmem(),
        cost_estimate=pl.CostEstimate(flops=10**4, transcendentals=0, bytes_accessed=10**4),
        compiler_params=pltpu.CompilerParams(vmem_limit_bytes=2**20),
    )(norm_gain[None, :])


def finish_body(feat_width, ready, raw, *refs):
    ways = len(ready) + len(raw)
    chunks, sums = refs[:ways], refs[ways : ways + len(raw)]
    gain_ref, out_ref, scratch, sems = refs[ways + len(raw) :]
    me = lax.axis_index("dp")
    tok = chunks[0].shape[0]

    def put(source, k):
        rows = pl.ds(pl.multiple_of((me ^ k) * tok, tok), tok)
        copy = pltpu.make_async_copy(source, out_ref.at[rows, :], sems.at[k])
        copy.start()
        return copy

    copies = [put(chunks[i], k) for i, k in enumerate(ready)]
    for i, k in enumerate(raw):
        inv = lax.rsqrt(sums[i][0:1, :] * (1.0 / feat_width) + epsilon)
        column = jnp.broadcast_to(inv, (tok, tok)).T[:, 0:1]
        value = chunks[len(ready) + i][...].astype(F32) * column * gain_ref[0:1, :]
        scratch[i] = value.astype(BF16)
        copies.append(put(scratch.at[i], k))
    for copy in copies:
        copy.wait()


def finish(ready, raw, sums, gain, feat_width):
    first = next(iter(ready.values()))
    tok, width = first.shape
    ways = len(ready) + len(raw)
    return pl.pallas_call(
        functools.partial(finish_body, feat_width, tuple(ready), tuple(raw)),
        out_shape=jax.ShapeDtypeStruct((tok * ways, width), BF16),
        in_specs=[vmem()] * (ways + len(raw) + 1),
        out_specs=pl.BlockSpec(memory_space=pltpu.HBM),
        scratch_shapes=[
            pltpu.VMEM((len(raw), tok, width), BF16),
            pltpu.SemaphoreType.DMA((ways,)),
        ],
        name="finish",
        cost_estimate=pl.CostEstimate(flops=10**6, transcendentals=0, bytes_accessed=10**6),
        compiler_params=pltpu.CompilerParams(vmem_limit_bytes=8 * 2**20),
    )(*ready.values(), *raw.values(), *[sums[k] for k in raw], gain)


def swap(value, axis, offset):
    size = lax.axis_size(axis)
    return lax.ppermute(value, axis, [(i, i ^ offset) for i in range(size)])


def swap_each(values, axis):
    moved = {}
    for k, value in values.items():
        moved[k] = swap(value, axis, k) if k else value
    return moved


def local_fast(tokens, routes, gate_code, gate_table, w_gate, w_up, w_down, norm_gain):
    return fast_steps(tokens, routes, gate_code, gate_table, w_gate, w_up, w_down, norm_gain)


def fast_steps(tokens, routes, gate_code, gate_table, w_gate, w_up, w_down, norm_gain):
    own_rows = tokens[0]
    tok, feat_width = own_rows.shape
    experts = lax.axis_size("expert")
    ways = lax.axis_size("dp")
    capacity = 5 * tok // (2 * experts)
    chunk = feat_width // ways
    close, away = CLOSE + [0], AWAY
    early = (ways // 2,)
    late = tuple(k for k in range(ways - 1, -1, -1) if k not in early)

    blocks, rest, route_rows, code_rows, held = dispatch(
        pltpu.with_memory_space_constraint(routes[0].T, pltpu.HBM),
        pltpu.with_memory_space_constraint(gate_code[0].T, pltpu.HBM),
        pltpu.with_memory_space_constraint(own_rows, pltpu.HBM),
        experts, capacity, CLOSE[:4], CLOSE[4:] + [0] + AWAY,
    )
    blocks |= dispatch_others(rest, held, capacity, CLOSE[4:] + [0] + AWAY)
    near = swap_each({k: blocks[k] for k in close}, "expert")
    far = swap_each({k: blocks[k] for k in away}, "expert")
    select, select_close, select_away, weights = selector(
        route_rows, code_rows, gate_table, experts, capacity
    )
    matrices = w_gate[0].T, w_up[0].T, w_down[0]

    plan = [(j, early + late) for j in range(len(close))]
    _, *outputs = expert_call([near[k] for k in close], *matrices, plan, chunk)
    back = swap_each(dict(zip(close, outputs)), "expert")
    gain_own = gain_of(norm_gain, (0,), chunk)
    plan = [(j, early) for j in range(len(away))]
    hidden, *away_early = expert_call([far[k] for k in away], *matrices, plan, chunk)
    got_early = back | swap_each(dict(zip(away, away_early)), "expert")
    plan = [(j, late) for j in range(len(away))]
    away_late = down_call(hidden, matrices[2], len(away), plan, chunk)
    got_late = swap_each(dict(zip(away, away_late)), "expert")

    order = range(experts)
    first, part = combine_early(select, weights, [got_early[k] for k in order], chunk)
    raw = swap_each({early[0]: first}, "dp")
    gain_late = gain_of(norm_gain, late, chunk)
    begun = combine_mid(
        select_close, weights, [back[k] for k in order if k not in away], chunk * len(early)
    )
    *rest, total = combine_late(
        select_away, weights, begun, part, gain_late, [got_late[k] for k in away], chunk,
        feat_width,
    )
    ready = swap_each(dict(zip(late, rest)), "dp")
    sums = swap_each({k: total for k in early}, "dp")
    return finish(ready, raw, sums, gain_own, feat_width)[None]


def solution(mesh):
    in_specs = (
        P("expert", "dp", None),
        P("expert", "dp", None),
        P("expert", "dp", None),
        P(),
        P("expert", None, None),
        P("expert", None, None),
        P("expert", None, None),
        P(),
    )
    out_specs = P("expert", None, "dp")

    def whole(tokens, routes, gate_code, gate_table, w_gate, w_up, w_down, norm_gain):
        args = (tokens, routes, gate_code, gate_table, w_gate, w_up, w_down, norm_gain)
        experts, ways = mesh.shape["expert"], mesh.shape["dp"]
        tok, feat = tokens.shape[1] // ways, tokens.shape[2]
        power = experts & (experts - 1) == 0 and ways & (ways - 1) == 0
        fits = power and experts == 8 and ways == 4
        fits = fits and tok % 128 == 0 and w_gate.shape[0] == experts
        fits = fits and 5 * tok % (16 * experts) == 0 and feat % (256 * ways) == 0
        body = local_fast if fits else local_general
        f = jax.shard_map(body, mesh=mesh, in_specs=in_specs, out_specs=out_specs, check_vma=False)
        return f(*args)

    return whole
```

```python
import functools

import jax
import jax.numpy as jnp
from jax import lax
from jax.experimental import pallas as pl
from jax.experimental.pallas import tpu as pltpu
from jax.sharding import PartitionSpec as P


epsilon = 1e-06


F32 = jnp.float32
BF16 = jnp.bfloat16


def expert_ffn(slot_block, w_gate, w_up, w_down):
    shape_in = slot_block.shape
    flat_rows = slot_block.reshape(-1, shape_in[-1])
    gate_act = jnp.dot(flat_rows, w_gate[0], preferred_element_type=F32)
    up_act = jnp.dot(flat_rows, w_up[0], preferred_element_type=F32)
    hidden = (jax.nn.silu(gate_act) * up_act).astype(BF16)
    result = jnp.dot(hidden, w_down[0], preferred_element_type=F32).astype(BF16)
    return result.reshape(shape_in)


def lookup(codes, gate_table):
    levels = gate_table.shape[0]
    match = codes[:, None] == jnp.arange(levels, dtype=jnp.int32)[None, :]
    return jnp.sum(jnp.where(match, gate_table[None, :], 0.0), axis=1)


def combine_pairs(outputs, weights):
    combined = outputs[:, 0] * weights[:, 0:1] + outputs[:, 1] * weights[:, 1:2]
    rounded = lax.optimization_barrier(combined.astype(BF16))
    return rounded.astype(F32)


def local_general(tokens, routes, gate_code, gate_table, w_gate, w_up, w_down, norm_gain):
    own_rows = tokens[0]
    tok_count, feat_width = own_rows.shape
    experts = w_gate.shape[0] * lax.axis_size("expert")
    capacity = 5 * tok_count // (2 * experts)
    route_ids = routes[0].reshape(-1)
    onehot = (route_ids[:, None] == jnp.arange(experts, dtype=jnp.int32)[None, :]).astype(jnp.int32)
    slot_pos = jnp.sum((jnp.cumsum(onehot, axis=0) - onehot) * onehot, axis=1)
    position = route_ids * capacity + slot_pos
    owner_row = (
        jnp.zeros((experts * capacity,), jnp.int32)
        .at[position]
        .set(jnp.arange(2 * tok_count, dtype=jnp.int32) // 2)
    )
    filled = jnp.zeros((experts * capacity,), jnp.bool_).at[position].set(True)
    buffer = jnp.where(filled[:, None], own_rows[owner_row], jnp.zeros((), BF16))
    buffer = buffer.reshape(experts, capacity, feat_width)
    level_ids = gate_code[0].reshape(-1)
    received = lax.all_to_all(buffer, "expert", split_axis=0, concat_axis=0, tiled=True)
    expert_out = expert_ffn(received, w_gate, w_up, w_down)
    returned = lax.all_to_all(expert_out, "expert", split_axis=0, concat_axis=0, tiled=True)
    outputs = (
        returned.reshape(-1, feat_width)[position]
        .astype(F32)
        .reshape(tok_count, 2, feat_width)
    )
    weights = lookup(level_ids, gate_table).reshape(tok_count, 2)
    widened = combine_pairs(outputs, weights)
    inv_rms = lax.rsqrt(jnp.mean(widened * widened, axis=1, keepdims=True) + epsilon)
    normed = (widened * inv_rms * norm_gain[None, :]).astype(BF16)
    relaid = lax.all_to_all(normed, "dp", split_axis=1, concat_axis=0, tiled=True)
    return relaid[None]


CLOSE, AWAY = [4, 2, 5, 3, 1], [6, 7]


def vmem():
    return pl.BlockSpec(memory_space=pltpu.VMEM)


def slot_rows(route_rows, experts, me):
    tok = route_rows.shape[1]
    ids = lax.broadcasted_iota(jnp.int32, (experts, tok), 0) ^ me
    named = (route_rows[0:1, :] == ids) | (route_rows[1:2, :] == ids)
    earlier = lax.broadcasted_iota(jnp.int32, (tok, tok), 0) < lax.broadcasted_iota(
        jnp.int32, (tok, tok), 1
    )
    count = jnp.dot(
        named.astype(F32).astype(BF16), earlier.astype(F32).astype(BF16),
        preferred_element_type=F32,
    )
    return jnp.where(named, count.astype(jnp.int32), -1), ids


def dispatch_body(experts, capacity, route_hbm, tok_hbm, *refs):
    *out_refs, route_ref, tok_ref, sems = refs
    copies = [
        pltpu.make_async_copy(route_hbm, route_ref, sems.at[0]),
        pltpu.make_async_copy(tok_hbm, tok_ref, sems.at[1]),
    ]
    for copy in copies:
        copy.start()
    me = lax.axis_index("expert")
    tok, width = tok_ref.shape
    lane = lax.broadcasted_iota(jnp.int32, (capacity, tok), 0)
    copies[0].wait()
    slots, _ = slot_rows(route_ref[...], experts, me)
    pick = jnp.concatenate(
        [(lane == slots[j : j + 1, :]).astype(F32) for j in range(experts)], axis=0
    ).astype(BF16)
    copies[1].wait()
    tile = 256
    for col in range(0, width, tile):
        rows = jnp.dot(pick, tok_ref[:, col : col + tile], preferred_element_type=F32)
        rows = rows.astype(BF16)
        for j in range(experts):
            out_refs[j][:, col : col + tile] = rows[j * capacity : (j + 1) * capacity, :]


def dispatch(route_rows, own_rows, experts, capacity):
    width = own_rows.shape[1]
    return pl.pallas_call(
        functools.partial(dispatch_body, experts, capacity),
        out_shape=[jax.ShapeDtypeStruct((capacity, width), BF16)] * experts,
        in_specs=[pl.BlockSpec(memory_space=pltpu.HBM)] * 2,
        out_specs=[vmem()] * experts,
        scratch_shapes=[
            pltpu.VMEM(route_rows.shape, jnp.int32),
            pltpu.VMEM(own_rows.shape, BF16),
            pltpu.SemaphoreType.DMA((2,)),
        ],
        name="dispatch",
        cost_estimate=pl.CostEstimate(flops=10**8, transcendentals=0, bytes_accessed=2 * 10**6),
        compiler_params=pltpu.CompilerParams(vmem_limit_bytes=16 * 2**20),
    )(route_rows, own_rows)


def selector_body(experts, capacity, route_ref, code_ref, table_ref, *refs):
    sel_ref, close_ref, away_ref, weight_ref = refs
    me = lax.axis_index("expert")
    rows = route_ref[...]
    slots, ids = slot_rows(rows, experts, me)
    tok = rows.shape[1]
    lane = lax.broadcasted_iota(jnp.int32, (capacity, tok), 0)
    for r in range(2):
        mine = jnp.where(rows[r : r + 1, :] == ids, slots, -1)
        pick = jnp.concatenate(
            [(lane == mine[j : j + 1, :]).astype(F32) for j in range(experts)], axis=0
        )
        held = slice(r * tok, (r + 1) * tok)
        split = close_ref.shape[1]
        sel_ref[held, :] = pick.T.astype(BF16)
        close_ref[held, :] = pick[:split].T.astype(BF16)
        away_ref[held, :] = pick[split:].T.astype(BF16)
        codes = code_ref[r : r + 1, :]
        weights = jnp.zeros((1, tok), F32)
        for level in range(table_ref.shape[0]):
            weights = jnp.where(codes == level, table_ref[level], weights)
        weight_ref[r] = jnp.broadcast_to(weights, (tok, tok)).T


def selector(route_rows, code_rows, gate_table, experts, capacity):
    tok = route_rows.shape[1]
    counts = (experts, experts - len(AWAY), len(AWAY))
    return pl.pallas_call(
        functools.partial(selector_body, experts, capacity),
        out_shape=[
            *[jax.ShapeDtypeStruct((2 * tok, n * capacity), BF16) for n in counts],
            jax.ShapeDtypeStruct((2, tok, tok), F32),
        ],
        in_specs=[vmem(), vmem(), pl.BlockSpec(memory_space=pltpu.SMEM)],
        out_specs=[vmem()] * 4,
        name="selector",
        cost_estimate=pl.CostEstimate(flops=2 * 10**10, transcendentals=0, bytes_accessed=10**8),
        compiler_params=pltpu.CompilerParams(vmem_limit_bytes=8 * 2**20),
    )(route_rows, code_rows, gate_table)


def chunk_columns(down_ref, offset, chunk):
    me, tile = lax.axis_index("dp"), 256
    for col in range(0, chunk, tile):
        start = pl.multiple_of((me ^ offset) * chunk + col, tile)
        yield col, tile, down_ref[:, pl.ds(start, tile)]


def write_down(hid_ref, down_ref, chunk, plan, out_refs):
    for offset in dict.fromkeys(k for _, offsets in plan for k in offsets):
        for col, tile, weight in chunk_columns(down_ref, offset, chunk):
            rows = jnp.dot(hid_ref[...], weight, preferred_element_type=F32).astype(BF16)
            for (j, offsets), out in zip(plan, out_refs):
                if offset in offsets:
                    capacity = out.shape[0]
                    at = offsets.index(offset) * chunk + col
                    out[:, at : at + tile] = rows[j * capacity : (j + 1) * capacity, :]


def expert_body(count, chunk, plan, *refs):
    blocks, (gate_ref, up_ref, down_ref) = refs[:count], refs[count : count + 3]
    hid_ref, x_ref, outs = refs[count + 3], refs[-1], refs[count + 4 : -1]
    capacity = blocks[0].shape[0]
    for j, block in enumerate(blocks):
        x_ref[j * capacity : (j + 1) * capacity, :] = block[...]
    hid = gate_ref.shape[0]
    over = (((1,), (1,)), ((), ()))
    few = x_ref.shape[0] <= 128
    if few:
        gate = lax.dot_general(gate_ref[...], x_ref[...], over, preferred_element_type=F32)
        up = lax.dot_general(up_ref[...], x_ref[...], over, preferred_element_type=F32)
        hid_ref[...] = (gate / (1.0 + jnp.exp(-gate)) * up).T.astype(BF16)
    tile = 256
    for low in range(0, 0 if few else hid, tile):
        high = min(hid, low + tile)
        gate = lax.dot_general(x_ref[...], gate_ref[low:high, :], over, preferred_element_type=F32)
        up = lax.dot_general(x_ref[...], up_ref[low:high, :], over, preferred_element_type=F32)
        hid_ref[:, low:high] = (gate / (1.0 + jnp.exp(-gate)) * up).astype(BF16)
    write_down(hid_ref, down_ref, chunk, plan, outs)


def expert_call(blocks, gate_rows, up_rows, down_rows, plan, chunk):
    count = len(blocks)
    capacity, width = blocks[0].shape
    rows, hid = capacity * count, gate_rows.shape[0]
    shapes = [jax.ShapeDtypeStruct((capacity, chunk * len(offsets)), BF16) for _, offsets in plan]
    return pl.pallas_call(
        functools.partial(expert_body, count, chunk, plan),
        out_shape=[jax.ShapeDtypeStruct((rows, hid), BF16)] + shapes,
        in_specs=[vmem()] * (count + 3),
        out_specs=[vmem()] * (1 + len(shapes)),
        scratch_shapes=[pltpu.VMEM((rows, width), BF16)],
        cost_estimate=pl.CostEstimate(
            flops=5 * rows * hid * width, transcendentals=rows * hid, bytes_accessed=8 * 10**6
        ),
        compiler_params=pltpu.CompilerParams(vmem_limit_bytes=24 * 2**20),
    )(*blocks, gate_rows, up_rows, down_rows)


def down_body(chunk, plan, hid_ref, down_ref, *out_refs):
    write_down(hid_ref, down_ref, chunk, plan, out_refs)


def down_call(hidden, down_rows, count, plan, chunk):
    rows, hid = hidden.shape
    return pl.pallas_call(
        functools.partial(down_body, chunk, plan),
        out_shape=[
            jax.ShapeDtypeStruct((rows // count, chunk * len(offsets)), BF16) for _, offsets in plan
        ],
        in_specs=[vmem()] * 2,
        out_specs=[vmem()] * len(plan),
        cost_estimate=pl.CostEstimate(
            flops=2 * rows * hid * chunk, transcendentals=0, bytes_accessed=3 * 10**6
        ),
        compiler_params=pltpu.CompilerParams(vmem_limit_bytes=16 * 2**20),
    )(hidden, down_rows)


def gather_blocks(blocks, y_ref, low):
    capacity, width = blocks[0].shape[0], y_ref.shape[1]
    for j, block in enumerate(blocks):
        start = low if block.shape[1] > width else 0
        y_ref[j * capacity : (j + 1) * capacity, :] = block[:, start : start + width]


def weighted(sel_ref, weight_ref, y_ref, low, tile):
    tok, lanes = weight_ref.shape[1:]
    picked = jnp.dot(sel_ref[...], y_ref[:, low : low + tile], preferred_element_type=F32)
    for at in range(0, tile, lanes):
        first = picked[:tok, at : at + lanes] * weight_ref[0]
        second = picked[tok:, at : at + lanes] * weight_ref[1]
        yield slice(low + at, low + at + lanes), first + second


def early_body(count, sel_ref, weight_ref, *refs):
    blocks, (out_ref, sum_ref, y_ref) = refs[:count], refs[count:]
    gather_blocks(blocks, y_ref, 0)
    squares = jnp.zeros(sum_ref.shape, F32)
    for low in range(0, y_ref.shape[1], 256):
        for cols, combined in weighted(sel_ref, weight_ref, y_ref, low, 256):
            rounded = combined.astype(BF16)
            out_ref[:, cols] = rounded
            squares = squares + rounded.astype(F32) * rounded.astype(F32)
    sum_ref[...] = squares


def combine_early(select, weights, blocks, width):
    rows, tok = blocks[0].shape[0] * len(blocks), weights.shape[1]
    return pl.pallas_call(
        functools.partial(early_body, len(blocks)),
        out_shape=[
            jax.ShapeDtypeStruct((tok, width), BF16),
            jax.ShapeDtypeStruct((tok, weights.shape[2]), F32),
        ],
        in_specs=[vmem()] * (2 + len(blocks)),
        out_specs=[vmem()] * 2,
        scratch_shapes=[pltpu.VMEM((rows, width), BF16)],
        name="combine_early",
        cost_estimate=pl.CostEstimate(
            flops=4 * tok * rows * width, transcendentals=0, bytes_accessed=10**6
        ),
        compiler_params=pltpu.CompilerParams(vmem_limit_bytes=12 * 2**20),
    )(select, weights, *blocks)


def mid_body(count, low, sel_ref, weight_ref, *refs):
    blocks, (out_ref, y_ref) = refs[:count], refs[count:]
    gather_blocks(blocks, y_ref, low)
    for col in range(0, y_ref.shape[1], 256):
        for cols, combined in weighted(sel_ref, weight_ref, y_ref, col, 256):
            out_ref[:, cols] = combined


def combine_mid(select, weights, blocks, low):
    capacity, width = blocks[0].shape
    rows, tok, width = capacity * len(blocks), weights.shape[1], width - low
    return pl.pallas_call(
        functools.partial(mid_body, len(blocks), low),
        out_shape=jax.ShapeDtypeStruct((tok, width), F32),
        in_specs=[vmem()] * (2 + len(blocks)),
        out_specs=vmem(),
        scratch_shapes=[pltpu.VMEM((rows, width), BF16)],
        name="combine_mid",
        cost_estimate=pl.CostEstimate(
            flops=4 * tok * rows * width, transcendentals=0, bytes_accessed=2 * 10**6
        ),
        compiler_params=pltpu.CompilerParams(vmem_limit_bytes=12 * 2**20),
    )(select, weights, *blocks)


def late_body(count, feat_width, sel_ref, weight_ref, begun_ref, part_ref, gain_ref, *refs):
    blocks, y_ref, outs, sum_ref = refs[:count], refs[-1], refs[count:-2], refs[-2]
    chunk = outs[0].shape[1]
    gather_blocks(blocks, y_ref, 0)
    squares = part_ref[...]
    for low in range(0, y_ref.shape[1], 256):
        for cols, combined in weighted(sel_ref, weight_ref, y_ref, low, 256):
            rounded = (begun_ref[:, cols] + combined).astype(BF16)
            at = cols.start % chunk
            outs[cols.start // chunk][:, at : at + cols.stop - cols.start] = rounded
            squares = squares + rounded.astype(F32) * rounded.astype(F32)
    total = jnp.sum(squares, axis=1, keepdims=True)
    tok = total.shape[0]
    sum_ref[...] = jnp.broadcast_to(total, (tok, tok)).T[0:8, :]
    inv = lax.rsqrt(total * (1.0 / feat_width) + epsilon)
    for q, out in enumerate(outs):
        gain = gain_ref[0:1, q * chunk : (q + 1) * chunk]
        out[...] = (out[...].astype(F32) * inv * gain).astype(BF16)


def combine_late(select, weights, begun, part, gain, blocks, chunk, feat_width):
    capacity, width = blocks[0].shape
    rows, tok = capacity * len(blocks), weights.shape[1]
    return pl.pallas_call(
        functools.partial(late_body, len(blocks), feat_width),
        out_shape=[jax.ShapeDtypeStruct((tok, chunk), BF16)] * (width // chunk)
        + [jax.ShapeDtypeStruct((8, tok), F32)],
        in_specs=[vmem()] * (5 + len(blocks)),
        out_specs=[vmem()] * (width // chunk + 1),
        scratch_shapes=[pltpu.VMEM((rows, width), BF16)],
        name="combine_late",
        cost_estimate=pl.CostEstimate(
            flops=4 * tok * rows * width, transcendentals=0, bytes_accessed=2 * 10**6
        ),
        compiler_params=pltpu.CompilerParams(vmem_limit_bytes=12 * 2**20),
    )(select, weights, begun, part, gain, *blocks)


def gain_body(offsets, gain_ref, out_ref):
    chunk = out_ref.shape[1] // len(offsets)
    me = lax.axis_index("dp")
    for q, offset in enumerate(offsets):
        start = pl.multiple_of((me ^ offset) * chunk, 128)
        row = gain_ref[:, pl.ds(start, chunk)]
        out_ref[:, q * chunk : (q + 1) * chunk] = jnp.broadcast_to(row, (8, chunk))


def gain_of(norm_gain, offsets, chunk):
    return pl.pallas_call(
        functools.partial(gain_body, offsets),
        out_shape=jax.ShapeDtypeStruct((8, chunk * len(offsets)), F32),
        in_specs=[vmem()],
        out_specs=vmem(),
        cost_estimate=pl.CostEstimate(flops=10**4, transcendentals=0, bytes_accessed=10**4),
        compiler_params=pltpu.CompilerParams(vmem_limit_bytes=2**20),
    )(norm_gain[None, :])


def finish_body(feat_width, ready, raw, *refs):
    ways = len(ready) + len(raw)
    chunks, sums = refs[:ways], refs[ways : ways + len(raw)]
    gain_ref, out_ref, scratch, sems = refs[ways + len(raw) :]
    me = lax.axis_index("dp")
    tok = chunks[0].shape[0]

    def put(source, k):
        rows = pl.ds(pl.multiple_of((me ^ k) * tok, tok), tok)
        copy = pltpu.make_async_copy(source, out_ref.at[rows, :], sems.at[k])
        copy.start()
        return copy

    copies = [put(chunks[i], k) for i, k in enumerate(ready)]
    for i, k in enumerate(raw):
        inv = lax.rsqrt(sums[i][0:1, :] * (1.0 / feat_width) + epsilon)
        column = jnp.broadcast_to(inv, (tok, tok)).T[:, 0:1]
        value = chunks[len(ready) + i][...].astype(F32) * column * gain_ref[0:1, :]
        scratch[i] = value.astype(BF16)
        copies.append(put(scratch.at[i], k))
    for copy in copies:
        copy.wait()


def finish(ready, raw, sums, gain, feat_width):
    first = next(iter(ready.values()))
    tok, width = first.shape
    ways = len(ready) + len(raw)
    return pl.pallas_call(
        functools.partial(finish_body, feat_width, tuple(ready), tuple(raw)),
        out_shape=jax.ShapeDtypeStruct((tok * ways, width), BF16),
        in_specs=[vmem()] * (ways + len(raw) + 1),
        out_specs=pl.BlockSpec(memory_space=pltpu.HBM),
        scratch_shapes=[
            pltpu.VMEM((len(raw), tok, width), BF16),
            pltpu.SemaphoreType.DMA((ways,)),
        ],
        name="finish",
        cost_estimate=pl.CostEstimate(flops=10**6, transcendentals=0, bytes_accessed=10**6),
        compiler_params=pltpu.CompilerParams(vmem_limit_bytes=8 * 2**20),
    )(*ready.values(), *raw.values(), *[sums[k] for k in raw], gain)


def swap(value, axis, offset):
    size = lax.axis_size(axis)
    return lax.ppermute(value, axis, [(i, i ^ offset) for i in range(size)])


def swap_each(values, axis):
    moved = {}
    for k, value in values.items():
        moved[k] = swap(value, axis, k) if k else value
    return moved


def local_fast(tokens, routes, gate_code, gate_table, w_gate, w_up, w_down, norm_gain):
    return fast_steps(tokens, routes, gate_code, gate_table, w_gate, w_up, w_down, norm_gain)


def fast_steps(tokens, routes, gate_code, gate_table, w_gate, w_up, w_down, norm_gain):
    own_rows = tokens[0]
    tok, feat_width = own_rows.shape
    experts = lax.axis_size("expert")
    ways = lax.axis_size("dp")
    capacity = 5 * tok // (2 * experts)
    chunk = feat_width // ways
    close, away = CLOSE + [0], AWAY
    early = (ways // 2,)
    late = tuple(k for k in range(ways - 1, -1, -1) if k not in early)

    route_rows = routes[0].T
    blocks = dispatch(
        pltpu.with_memory_space_constraint(route_rows, pltpu.HBM),
        pltpu.with_memory_space_constraint(own_rows, pltpu.HBM),
        experts, capacity,
    )
    near = swap_each({k: blocks[k] for k in close}, "expert")
    far = swap_each({k: blocks[k] for k in away}, "expert")
    select, select_close, select_away, weights = selector(route_rows, gate_code[0].T, gate_table, experts, capacity)
    matrices = w_gate[0].T, w_up[0].T, w_down[0]

    plan = [(j, early + late) for j in range(len(close))]
    _, *outputs = expert_call([near[k] for k in close], *matrices, plan, chunk)
    back = swap_each(dict(zip(close, outputs)), "expert")
    gain_own = gain_of(norm_gain, (0,), chunk)
    plan = [(j, early) for j in range(len(away))]
    hidden, *away_early = expert_call([far[k] for k in away], *matrices, plan, chunk)
    got_early = back | swap_each(dict(zip(away, away_early)), "expert")
    plan = [(j, late) for j in range(len(away))]
    away_late = down_call(hidden, matrices[2], len(away), plan, chunk)
    got_late = swap_each(dict(zip(away, away_late)), "expert")

    order = range(experts)
    first, part = combine_early(select, weights, [got_early[k] for k in order], chunk)
    raw = swap_each({early[0]: first}, "dp")
    gain_late = gain_of(norm_gain, late, chunk)
    begun = combine_mid(
        select_close, weights, [back[k] for k in order if k not in away], chunk * len(early)
    )
    *rest, total = combine_late(
        select_away, weights, begun, part, gain_late, [got_late[k] for k in away], chunk,
        feat_width,
    )
    ready = swap_each(dict(zip(late, rest)), "dp")
    sums = swap_each({k: total for k in early}, "dp")
    return finish(ready, raw, sums, gain_own, feat_width)[None]


def solution(mesh):
    in_specs = (
        P("expert", "dp", None),
        P("expert", "dp", None),
        P("expert", "dp", None),
        P(),
        P("expert", None, None),
        P("expert", None, None),
        P("expert", None, None),
        P(),
    )
    out_specs = P("expert", None, "dp")

    def whole(tokens, routes, gate_code, gate_table, w_gate, w_up, w_down, norm_gain):
        args = (tokens, routes, gate_code, gate_table, w_gate, w_up, w_down, norm_gain)
        experts, ways = mesh.shape["expert"], mesh.shape["dp"]
        tok, feat = tokens.shape[1] // ways, tokens.shape[2]
        power = experts & (experts - 1) == 0 and ways & (ways - 1) == 0
        fits = power and experts == 8 and ways == 4
        fits = fits and tok % 128 == 0 and w_gate.shape[0] == experts
        fits = fits and 5 * tok % (16 * experts) == 0 and feat % (256 * ways) == 0
        body = local_fast if fits else local_general
        f = jax.shard_map(body, mesh=mesh, in_specs=in_specs, out_specs=out_specs, check_vma=False)
        return f(*args)

    return whole
```

```python
import functools

import jax
import jax.numpy as jnp
from jax import lax
from jax.experimental import pallas as pl
from jax.experimental.pallas import tpu as pltpu
from jax.sharding import PartitionSpec as P


epsilon = 1e-06


F32 = jnp.float32
BF16 = jnp.bfloat16


def expert_ffn(slot_block, w_gate, w_up, w_down):
    shape_in = slot_block.shape
    flat_rows = slot_block.reshape(-1, shape_in[-1])
    gate_act = jnp.dot(flat_rows, w_gate[0], preferred_element_type=F32)
    up_act = jnp.dot(flat_rows, w_up[0], preferred_element_type=F32)
    hidden = (jax.nn.silu(gate_act) * up_act).astype(BF16)
    result = jnp.dot(hidden, w_down[0], preferred_element_type=F32).astype(BF16)
    return result.reshape(shape_in)


def lookup(codes, gate_table):
    levels = gate_table.shape[0]
    match = codes[:, None] == jnp.arange(levels, dtype=jnp.int32)[None, :]
    return jnp.sum(jnp.where(match, gate_table[None, :], 0.0), axis=1)


def combine_pairs(outputs, weights):
    combined = outputs[:, 0] * weights[:, 0:1] + outputs[:, 1] * weights[:, 1:2]
    rounded = lax.optimization_barrier(combined.astype(BF16))
    return rounded.astype(F32)


def local_general(tokens, routes, gate_code, gate_table, w_gate, w_up, w_down, norm_gain):
    own_rows = tokens[0]
    tok_count, feat_width = own_rows.shape
    experts = w_gate.shape[0] * lax.axis_size("expert")
    capacity = 5 * tok_count // (2 * experts)
    route_ids = routes[0].reshape(-1)
    onehot = (route_ids[:, None] == jnp.arange(experts, dtype=jnp.int32)[None, :]).astype(jnp.int32)
    slot_pos = jnp.sum((jnp.cumsum(onehot, axis=0) - onehot) * onehot, axis=1)
    position = route_ids * capacity + slot_pos
    owner_row = (
        jnp.zeros((experts * capacity,), jnp.int32)
        .at[position]
        .set(jnp.arange(2 * tok_count, dtype=jnp.int32) // 2)
    )
    filled = jnp.zeros((experts * capacity,), jnp.bool_).at[position].set(True)
    buffer = jnp.where(filled[:, None], own_rows[owner_row], jnp.zeros((), BF16))
    buffer = buffer.reshape(experts, capacity, feat_width)
    level_ids = gate_code[0].reshape(-1)
    received = lax.all_to_all(buffer, "expert", split_axis=0, concat_axis=0, tiled=True)
    expert_out = expert_ffn(received, w_gate, w_up, w_down)
    returned = lax.all_to_all(expert_out, "expert", split_axis=0, concat_axis=0, tiled=True)
    outputs = (
        returned.reshape(-1, feat_width)[position]
        .astype(F32)
        .reshape(tok_count, 2, feat_width)
    )
    weights = lookup(level_ids, gate_table).reshape(tok_count, 2)
    widened = combine_pairs(outputs, weights)
    inv_rms = lax.rsqrt(jnp.mean(widened * widened, axis=1, keepdims=True) + epsilon)
    normed = (widened * inv_rms * norm_gain[None, :]).astype(BF16)
    relaid = lax.all_to_all(normed, "dp", split_axis=1, concat_axis=0, tiled=True)
    return relaid[None]


CLOSE, AWAY = [4, 2, 5, 3, 1], [6, 7]


def vmem():
    return pl.BlockSpec(memory_space=pltpu.VMEM)


def slot_rows(route_rows, experts, me):
    tok = route_rows.shape[1]
    ids = lax.broadcasted_iota(jnp.int32, (experts, tok), 0) ^ me
    named = (route_rows[0:1, :] == ids) | (route_rows[1:2, :] == ids)
    earlier = lax.broadcasted_iota(jnp.int32, (tok, tok), 0) < lax.broadcasted_iota(
        jnp.int32, (tok, tok), 1
    )
    count = jnp.dot(
        named.astype(F32).astype(BF16), earlier.astype(F32).astype(BF16),
        preferred_element_type=F32,
    )
    return jnp.where(named, count.astype(jnp.int32), -1), ids


def dispatch_body(experts, capacity, route_hbm, tok_hbm, *refs):
    *out_refs, route_ref, tok_ref, sems = refs
    copies = [
        pltpu.make_async_copy(route_hbm, route_ref, sems.at[0]),
        pltpu.make_async_copy(tok_hbm, tok_ref, sems.at[1]),
    ]
    for copy in copies:
        copy.start()
    me = lax.axis_index("expert")
    tok, width = tok_ref.shape
    lane = lax.broadcasted_iota(jnp.int32, (capacity, tok), 0)
    copies[0].wait()
    slots, _ = slot_rows(route_ref[...], experts, me)
    pick = jnp.concatenate(
        [(lane == slots[j : j + 1, :]).astype(F32) for j in range(experts)], axis=0
    ).astype(BF16)
    copies[1].wait()
    tile = 256
    for col in range(0, width, tile):
        rows = jnp.dot(pick, tok_ref[:, col : col + tile], preferred_element_type=F32)
        rows = rows.astype(BF16)
        for j in range(experts):
            out_refs[j][:, col : col + tile] = rows[j * capacity : (j + 1) * capacity, :]


def dispatch(route_rows, own_rows, experts, capacity):
    width = own_rows.shape[1]
    *blocks, route_held = pl.pallas_call(
        functools.partial(dispatch_body, experts, capacity),
        out_shape=[jax.ShapeDtypeStruct((capacity, width), BF16)] * experts
        + [jax.ShapeDtypeStruct(route_rows.shape, jnp.int32)],
        in_specs=[pl.BlockSpec(memory_space=pltpu.HBM)] * 2,
        out_specs=[vmem()] * (experts + 1),
        scratch_shapes=[pltpu.VMEM(own_rows.shape, BF16), pltpu.SemaphoreType.DMA((2,))],
        name="dispatch",
        cost_estimate=pl.CostEstimate(flops=10**8, transcendentals=0, bytes_accessed=2 * 10**6),
        compiler_params=pltpu.CompilerParams(vmem_limit_bytes=16 * 2**20),
    )(route_rows, own_rows)
    return blocks, route_held


def selector_body(experts, capacity, route_ref, code_ref, table_ref, *refs):
    sel_ref, close_ref, away_ref, weight_ref = refs
    me = lax.axis_index("expert")
    rows = route_ref[...]
    slots, ids = slot_rows(rows, experts, me)
    tok = rows.shape[1]
    lane = lax.broadcasted_iota(jnp.int32, (capacity, tok), 0)
    for r in range(2):
        mine = jnp.where(rows[r : r + 1, :] == ids, slots, -1)
        pick = jnp.concatenate(
            [(lane == mine[j : j + 1, :]).astype(F32) for j in range(experts)], axis=0
        )
        held = slice(r * tok, (r + 1) * tok)
        split = close_ref.shape[1]
        sel_ref[held, :] = pick.T.astype(BF16)
        close_ref[held, :] = pick[:split].T.astype(BF16)
        away_ref[held, :] = pick[split:].T.astype(BF16)
        codes = code_ref[r : r + 1, :]
        weights = jnp.zeros((1, tok), F32)
        for level in range(table_ref.shape[0]):
            weights = jnp.where(codes == level, table_ref[level], weights)
        weight_ref[r] = jnp.broadcast_to(weights, (tok, tok)).T


def selector(route_rows, code_rows, gate_table, experts, capacity):
    tok = route_rows.shape[1]
    counts = (experts, experts - len(AWAY), len(AWAY))
    return pl.pallas_call(
        functools.partial(selector_body, experts, capacity),
        out_shape=[
            *[jax.ShapeDtypeStruct((2 * tok, n * capacity), BF16) for n in counts],
            jax.ShapeDtypeStruct((2, tok, tok), F32),
        ],
        in_specs=[vmem(), vmem(), pl.BlockSpec(memory_space=pltpu.SMEM)],
        out_specs=[vmem()] * 4,
        name="selector",
        cost_estimate=pl.CostEstimate(flops=2 * 10**10, transcendentals=0, bytes_accessed=10**8),
        compiler_params=pltpu.CompilerParams(vmem_limit_bytes=8 * 2**20),
    )(route_rows, code_rows, gate_table)


def chunk_columns(down_ref, offset, chunk):
    me, tile = lax.axis_index("dp"), 256
    for col in range(0, chunk, tile):
        start = pl.multiple_of((me ^ offset) * chunk + col, tile)
        yield col, tile, down_ref[:, pl.ds(start, tile)]


def write_down(hid_ref, down_ref, chunk, plan, out_refs):
    for offset in dict.fromkeys(k for _, offsets in plan for k in offsets):
        for col, tile, weight in chunk_columns(down_ref, offset, chunk):
            rows = jnp.dot(hid_ref[...], weight, preferred_element_type=F32).astype(BF16)
            for (j, offsets), out in zip(plan, out_refs):
                if offset in offsets:
                    capacity = out.shape[0]
                    at = offsets.index(offset) * chunk + col
                    out[:, at : at + tile] = rows[j * capacity : (j + 1) * capacity, :]


def expert_body(count, chunk, plan, *refs):
    blocks, (gate_ref, up_ref, down_ref) = refs[:count], refs[count : count + 3]
    hid_ref, x_ref, outs = refs[count + 3], refs[-1], refs[count + 4 : -1]
    capacity = blocks[0].shape[0]
    for j, block in enumerate(blocks):
        x_ref[j * capacity : (j + 1) * capacity, :] = block[...]
    hid = gate_ref.shape[0]
    over = (((1,), (1,)), ((), ()))
    few = x_ref.shape[0] <= 128
    if few:
        gate = lax.dot_general(gate_ref[...], x_ref[...], over, preferred_element_type=F32)
        up = lax.dot_general(up_ref[...], x_ref[...], over, preferred_element_type=F32)
        hid_ref[...] = (gate / (1.0 + jnp.exp(-gate)) * up).T.astype(BF16)
    tile = 256
    for low in range(0, 0 if few else hid, tile):
        high = min(hid, low + tile)
        gate = lax.dot_general(x_ref[...], gate_ref[low:high, :], over, preferred_element_type=F32)
        up = lax.dot_general(x_ref[...], up_ref[low:high, :], over, preferred_element_type=F32)
        hid_ref[:, low:high] = (gate / (1.0 + jnp.exp(-gate)) * up).astype(BF16)
    write_down(hid_ref, down_ref, chunk, plan, outs)


def expert_call(blocks, gate_rows, up_rows, down_rows, plan, chunk):
    count = len(blocks)
    capacity, width = blocks[0].shape
    rows, hid = capacity * count, gate_rows.shape[0]
    shapes = [jax.ShapeDtypeStruct((capacity, chunk * len(offsets)), BF16) for _, offsets in plan]
    return pl.pallas_call(
        functools.partial(expert_body, count, chunk, plan),
        out_shape=[jax.ShapeDtypeStruct((rows, hid), BF16)] + shapes,
        in_specs=[vmem()] * (count + 3),
        out_specs=[vmem()] * (1 + len(shapes)),
        scratch_shapes=[pltpu.VMEM((rows, width), BF16)],
        cost_estimate=pl.CostEstimate(
            flops=5 * rows * hid * width, transcendentals=rows * hid, bytes_accessed=8 * 10**6
        ),
        compiler_params=pltpu.CompilerParams(vmem_limit_bytes=24 * 2**20),
    )(*blocks, gate_rows, up_rows, down_rows)


def down_body(chunk, plan, hid_ref, down_ref, *out_refs):
    write_down(hid_ref, down_ref, chunk, plan, out_refs)


def down_call(hidden, down_rows, count, plan, chunk):
    rows, hid = hidden.shape
    return pl.pallas_call(
        functools.partial(down_body, chunk, plan),
        out_shape=[
            jax.ShapeDtypeStruct((rows // count, chunk * len(offsets)), BF16) for _, offsets in plan
        ],
        in_specs=[vmem()] * 2,
        out_specs=[vmem()] * len(plan),
        cost_estimate=pl.CostEstimate(
            flops=2 * rows * hid * chunk, transcendentals=0, bytes_accessed=3 * 10**6
        ),
        compiler_params=pltpu.CompilerParams(vmem_limit_bytes=16 * 2**20),
    )(hidden, down_rows)


def gather_blocks(blocks, y_ref, low):
    capacity, width = blocks[0].shape[0], y_ref.shape[1]
    for j, block in enumerate(blocks):
        start = low if block.shape[1] > width else 0
        y_ref[j * capacity : (j + 1) * capacity, :] = block[:, start : start + width]


def weighted(sel_ref, weight_ref, y_ref, low, tile):
    tok, lanes = weight_ref.shape[1:]
    picked = jnp.dot(sel_ref[...], y_ref[:, low : low + tile], preferred_element_type=F32)
    for at in range(0, tile, lanes):
        first = picked[:tok, at : at + lanes] * weight_ref[0]
        second = picked[tok:, at : at + lanes] * weight_ref[1]
        yield slice(low + at, low + at + lanes), first + second


def early_body(count, sel_ref, weight_ref, *refs):
    blocks, (out_ref, sum_ref, y_ref) = refs[:count], refs[count:]
    gather_blocks(blocks, y_ref, 0)
    squares = jnp.zeros(sum_ref.shape, F32)
    for low in range(0, y_ref.shape[1], 256):
        for cols, combined in weighted(sel_ref, weight_ref, y_ref, low, 256):
            rounded = combined.astype(BF16)
            out_ref[:, cols] = rounded
            squares = squares + rounded.astype(F32) * rounded.astype(F32)
    sum_ref[...] = squares


def combine_early(select, weights, blocks, width):
    rows, tok = blocks[0].shape[0] * len(blocks), weights.shape[1]
    return pl.pallas_call(
        functools.partial(early_body, len(blocks)),
        out_shape=[
            jax.ShapeDtypeStruct((tok, width), BF16),
            jax.ShapeDtypeStruct((tok, weights.shape[2]), F32),
        ],
        in_specs=[vmem()] * (2 + len(blocks)),
        out_specs=[vmem()] * 2,
        scratch_shapes=[pltpu.VMEM((rows, width), BF16)],
        name="combine_early",
        cost_estimate=pl.CostEstimate(
            flops=4 * tok * rows * width, transcendentals=0, bytes_accessed=10**6
        ),
        compiler_params=pltpu.CompilerParams(vmem_limit_bytes=12 * 2**20),
    )(select, weights, *blocks)


def mid_body(count, low, sel_ref, weight_ref, *refs):
    blocks, (out_ref, y_ref) = refs[:count], refs[count:]
    gather_blocks(blocks, y_ref, low)
    for col in range(0, y_ref.shape[1], 256):
        for cols, combined in weighted(sel_ref, weight_ref, y_ref, col, 256):
            out_ref[:, cols] = combined


def combine_mid(select, weights, blocks, low):
    capacity, width = blocks[0].shape
    rows, tok, width = capacity * len(blocks), weights.shape[1], width - low
    return pl.pallas_call(
        functools.partial(mid_body, len(blocks), low),
        out_shape=jax.ShapeDtypeStruct((tok, width), F32),
        in_specs=[vmem()] * (2 + len(blocks)),
        out_specs=vmem(),
        scratch_shapes=[pltpu.VMEM((rows, width), BF16)],
        name="combine_mid",
        cost_estimate=pl.CostEstimate(
            flops=4 * tok * rows * width, transcendentals=0, bytes_accessed=2 * 10**6
        ),
        compiler_params=pltpu.CompilerParams(vmem_limit_bytes=12 * 2**20),
    )(select, weights, *blocks)


def late_body(count, feat_width, sel_ref, weight_ref, begun_ref, part_ref, gain_ref, *refs):
    blocks, y_ref, outs, sum_ref = refs[:count], refs[-1], refs[count:-2], refs[-2]
    chunk = outs[0].shape[1]
    gather_blocks(blocks, y_ref, 0)
    squares = part_ref[...]
    for low in range(0, y_ref.shape[1], 256):
        for cols, combined in weighted(sel_ref, weight_ref, y_ref, low, 256):
            rounded = (begun_ref[:, cols] + combined).astype(BF16)
            at = cols.start % chunk
            outs[cols.start // chunk][:, at : at + cols.stop - cols.start] = rounded
            squares = squares + rounded.astype(F32) * rounded.astype(F32)
    total = jnp.sum(squares, axis=1, keepdims=True)
    tok = total.shape[0]
    sum_ref[...] = jnp.broadcast_to(total, (tok, tok)).T[0:8, :]
    inv = lax.rsqrt(total * (1.0 / feat_width) + epsilon)
    for q, out in enumerate(outs):
        gain = gain_ref[0:1, q * chunk : (q + 1) * chunk]
        out[...] = (out[...].astype(F32) * inv * gain).astype(BF16)


def combine_late(select, weights, begun, part, gain, blocks, chunk, feat_width):
    capacity, width = blocks[0].shape
    rows, tok = capacity * len(blocks), weights.shape[1]
    return pl.pallas_call(
        functools.partial(late_body, len(blocks), feat_width),
        out_shape=[jax.ShapeDtypeStruct((tok, chunk), BF16)] * (width // chunk)
        + [jax.ShapeDtypeStruct((8, tok), F32)],
        in_specs=[vmem()] * (5 + len(blocks)),
        out_specs=[vmem()] * (width // chunk + 1),
        scratch_shapes=[pltpu.VMEM((rows, width), BF16)],
        name="combine_late",
        cost_estimate=pl.CostEstimate(
            flops=4 * tok * rows * width, transcendentals=0, bytes_accessed=2 * 10**6
        ),
        compiler_params=pltpu.CompilerParams(vmem_limit_bytes=12 * 2**20),
    )(select, weights, begun, part, gain, *blocks)


def gain_body(offsets, gain_ref, out_ref):
    chunk = out_ref.shape[1] // len(offsets)
    me = lax.axis_index("dp")
    for q, offset in enumerate(offsets):
        start = pl.multiple_of((me ^ offset) * chunk, 128)
        row = gain_ref[:, pl.ds(start, chunk)]
        out_ref[:, q * chunk : (q + 1) * chunk] = jnp.broadcast_to(row, (8, chunk))


def gain_of(norm_gain, offsets, chunk):
    return pl.pallas_call(
        functools.partial(gain_body, offsets),
        out_shape=jax.ShapeDtypeStruct((8, chunk * len(offsets)), F32),
        in_specs=[vmem()],
        out_specs=vmem(),
        cost_estimate=pl.CostEstimate(flops=10**4, transcendentals=0, bytes_accessed=10**4),
        compiler_params=pltpu.CompilerParams(vmem_limit_bytes=2**20),
    )(norm_gain[None, :])


def finish_body(feat_width, ready, raw, *refs):
    ways = len(ready) + len(raw)
    chunks, sums = refs[:ways], refs[ways : ways + len(raw)]
    gain_ref, out_ref, scratch, sems = refs[ways + len(raw) :]
    me = lax.axis_index("dp")
    tok = chunks[0].shape[0]

    def put(source, k):
        rows = pl.ds(pl.multiple_of((me ^ k) * tok, tok), tok)
        copy = pltpu.make_async_copy(source, out_ref.at[rows, :], sems.at[k])
        copy.start()
        return copy

    copies = [put(chunks[i], k) for i, k in enumerate(ready)]
    for i, k in enumerate(raw):
        inv = lax.rsqrt(sums[i][0:1, :] * (1.0 / feat_width) + epsilon)
        column = jnp.broadcast_to(inv, (tok, tok)).T[:, 0:1]
        value = chunks[len(ready) + i][...].astype(F32) * column * gain_ref[0:1, :]
        scratch[i] = value.astype(BF16)
        copies.append(put(scratch.at[i], k))
    for copy in copies:
        copy.wait()


def finish(ready, raw, sums, gain, feat_width):
    first = next(iter(ready.values()))
    tok, width = first.shape
    ways = len(ready) + len(raw)
    return pl.pallas_call(
        functools.partial(finish_body, feat_width, tuple(ready), tuple(raw)),
        out_shape=jax.ShapeDtypeStruct((tok * ways, width), BF16),
        in_specs=[vmem()] * (ways + len(raw) + 1),
        out_specs=pl.BlockSpec(memory_space=pltpu.HBM),
        scratch_shapes=[
            pltpu.VMEM((len(raw), tok, width), BF16),
            pltpu.SemaphoreType.DMA((ways,)),
        ],
        name="finish",
        cost_estimate=pl.CostEstimate(flops=10**6, transcendentals=0, bytes_accessed=10**6),
        compiler_params=pltpu.CompilerParams(vmem_limit_bytes=8 * 2**20),
    )(*ready.values(), *raw.values(), *[sums[k] for k in raw], gain)


def swap(value, axis, offset):
    size = lax.axis_size(axis)
    return lax.ppermute(value, axis, [(i, i ^ offset) for i in range(size)])


def swap_each(values, axis):
    moved = {}
    for k, value in values.items():
        moved[k] = swap(value, axis, k) if k else value
    return moved


def local_fast(tokens, routes, gate_code, gate_table, w_gate, w_up, w_down, norm_gain):
    return fast_steps(tokens, routes, gate_code, gate_table, w_gate, w_up, w_down, norm_gain)


def fast_steps(tokens, routes, gate_code, gate_table, w_gate, w_up, w_down, norm_gain):
    own_rows = tokens[0]
    tok, feat_width = own_rows.shape
    experts = lax.axis_size("expert")
    ways = lax.axis_size("dp")
    capacity = 5 * tok // (2 * experts)
    chunk = feat_width // ways
    close, away = CLOSE + [0], AWAY
    early = (ways // 2,)
    late = tuple(k for k in range(ways - 1, -1, -1) if k not in early)

    blocks, route_rows = dispatch(
        pltpu.with_memory_space_constraint(routes[0].T, pltpu.HBM),
        pltpu.with_memory_space_constraint(own_rows, pltpu.HBM),
        experts, capacity,
    )
    near = swap_each({k: blocks[k] for k in close}, "expert")
    far = swap_each({k: blocks[k] for k in away}, "expert")
    select, select_close, select_away, weights = selector(route_rows, gate_code[0].T, gate_table, experts, capacity)
    matrices = w_gate[0].T, w_up[0].T, w_down[0]

    plan = [(j, early + late) for j in range(len(close))]
    _, *outputs = expert_call([near[k] for k in close], *matrices, plan, chunk)
    back = swap_each(dict(zip(close, outputs)), "expert")
    gain_own = gain_of(norm_gain, (0,), chunk)
    plan = [(j, early) for j in range(len(away))]
    hidden, *away_early = expert_call([far[k] for k in away], *matrices, plan, chunk)
    got_early = back | swap_each(dict(zip(away, away_early)), "expert")
    plan = [(j, late) for j in range(len(away))]
    away_late = down_call(hidden, matrices[2], len(away), plan, chunk)
    got_late = swap_each(dict(zip(away, away_late)), "expert")

    order = range(experts)
    first, part = combine_early(select, weights, [got_early[k] for k in order], chunk)
    raw = swap_each({early[0]: first}, "dp")
    gain_late = gain_of(norm_gain, late, chunk)
    begun = combine_mid(
        select_close, weights, [back[k] for k in order if k not in away], chunk * len(early)
    )
    *rest, total = combine_late(
        select_away, weights, begun, part, gain_late, [got_late[k] for k in away], chunk,
        feat_width,
    )
    ready = swap_each(dict(zip(late, rest)), "dp")
    sums = swap_each({k: total for k in early}, "dp")
    return finish(ready, raw, sums, gain_own, feat_width)[None]


def solution(mesh):
    in_specs = (
        P("expert", "dp", None),
        P("expert", "dp", None),
        P("expert", "dp", None),
        P(),
        P("expert", None, None),
        P("expert", None, None),
        P("expert", None, None),
        P(),
    )
    out_specs = P("expert", None, "dp")

    def whole(tokens, routes, gate_code, gate_table, w_gate, w_up, w_down, norm_gain):
        args = (tokens, routes, gate_code, gate_table, w_gate, w_up, w_down, norm_gain)
        experts, ways = mesh.shape["expert"], mesh.shape["dp"]
        tok, feat = tokens.shape[1] // ways, tokens.shape[2]
        power = experts & (experts - 1) == 0 and ways & (ways - 1) == 0
        fits = power and experts == 8 and ways == 4
        fits = fits and tok % 128 == 0 and w_gate.shape[0] == experts
        fits = fits and 5 * tok % (16 * experts) == 0 and feat % (256 * ways) == 0
        body = local_fast if fits else local_general
        f = jax.shard_map(body, mesh=mesh, in_specs=in_specs, out_specs=out_specs, check_vma=False)
        return f(*args)

    return whole
```
